256 devices in a mesh: gx: 32 (over z, x_lo, core), gy: 8 (over y, x_hi).
Axes of the slice: x: 4 (x_hi: 2, x_lo: 2; x = x_hi * 2 + x_lo), y: 4, z: 8, core: 2. Of those that a mesh axis runs over, the one named last changes fastest.
Arguments:
- field: float32 [32, 128, 128, 256], P(None, 'gx', 'gy'), may hold values from -6 to 6
- spec_weight: float32 [2, 32, 32, 32, 32, 32], P(None, None, 'gx', 'gy'), may hold values from -6 to 6
- dw_kernel: float32 [32, 3, 3, 3], replicated, may hold values from -1.25 to 1.25
- point_weight: float32 [32, 32], replicated, may hold values from -1 to 1
- bias: float32 [32], replicated, may hold values from -3 to 3
Outputs:
- evolved: float32 [32, 128, 128, 256], P(None, 'gx', 'gy')
The draws below stay inside these ranges and needn't reach their ends.
All inputs are finite; a program needn't handle non-finite values.
Results may differ from the reference program's by a relative error of at most 0.00005.
Values sent between devices are 32-bit elements; how exact they have to be, the bound alone decides.
No kernel may reach another device: no remote copies, remote signals or barrier semaphores. Data moves between devices by JAX's collectives and lax.ppermute only.
A program may use at most 128 MiB of HBM per device.

```python
import jax
import jax.numpy as jnp
from jax import lax

C = 32
MODES = 32
NZ = 256
NX = 128
NY = 128


def steps_of(own_key, extent, pieces, smallest, top_value):
    gain, own = 1.0, jax.random.fold_in(own_key, 6)
    for axis_at, shards_of in pieces:
        steps = jnp.exp(jax.random.uniform(jax.random.fold_in(own, axis_at), (shards_of,), jnp.float32, smallest / len(pieces), top_value / len(pieces)))
        gain = gain * jnp.repeat(steps, extent[axis_at] // shards_of).reshape([-1 if axis == axis_at else 1 for axis in range(len(extent))])
    return gain


def noise(stream_key, dims, spread, bound, split=(), kind=jnp.bfloat16):
    drawn = spread * jax.random.normal(stream_key, dims, jnp.float32)
    if split:
        drawn = drawn * steps_of(stream_key, dims, split, -0.22, 0.18)
    return jnp.clip(drawn, -bound, bound).astype(kind)


def setup_inputs(seed: int = 0) -> dict:
    key_of = jax.random.split(jax.random.key(seed), 6)
    return {
        "field": noise(key_of[0], (C, NX, NY, NZ), 1.0, 6.0, ((1, 32), (2, 8)), jnp.float32),
        "spec_weight": noise(key_of[1], (2, MODES, MODES, MODES, C, C), (max(1, 2 * C * MODES**3 // (NX * NY * NZ))) ** -0.5, 6.0, ((2, 32), (3, 8)), jnp.float32),
        "dw_kernel": noise(key_of[2], (C, 3, 3, 3), 27 ** -0.5, 1.25, (), jnp.float32),
        "point_weight": noise(key_of[3], (C, C), C ** -0.5, 1.0, (), jnp.float32),
        "bias": noise(key_of[4], (C,), 0.5, 3.0, (), jnp.float32),
    }


def truncate(values, axis, length):
    half = MODES // 2
    low = lax.slice_in_dim(values, 0, half, axis=axis)
    high = lax.slice_in_dim(values, length - half, length, axis=axis)
    return jnp.concatenate([low, high], axis=axis)


def widen(values, axis, length):
    half = MODES // 2
    low = lax.slice_in_dim(values, 0, half, axis=axis)
    high = lax.slice_in_dim(values, half, MODES, axis=axis)
    shape = list(values.shape)
    shape[axis] = length - MODES
    return jnp.concatenate([low, jnp.zeros(shape, values.dtype), high], axis=axis)


def reference(field, spec_weight, dw_kernel, point_weight, bias):
    exact_mode = lax.Precision.HIGHEST
    zspec = jnp.fft.rfft(field, axis=3)[..., :MODES]
    yspec = truncate(jnp.fft.fft(zspec, axis=2), 2, NY)
    xspec = truncate(jnp.fft.fft(yspec, axis=1), 1, NX)
    real_in = jnp.real(xspec).astype(jnp.float32)
    imag_in = jnp.imag(xspec).astype(jnp.float32)
    weight_re = spec_weight[0].astype(jnp.float32)
    weight_im = spec_weight[1].astype(jnp.float32)
    pattern = "ixyz,xyzio->oxyz"
    out_re = jnp.einsum(pattern, real_in, weight_re, precision=exact_mode) - jnp.einsum(pattern, imag_in, weight_im, precision=exact_mode)
    out_im = jnp.einsum(pattern, real_in, weight_im, precision=exact_mode) + jnp.einsum(pattern, imag_in, weight_re, precision=exact_mode)
    mixed = out_re + 1j * out_im
    back_x = jnp.fft.ifft(widen(mixed, 1, NX), axis=1)
    back_y = jnp.fft.ifft(widen(back_x, 2, NY), axis=2)
    tail = jnp.zeros(back_y.shape[:3] + (NZ // 2 + 1 - MODES,), back_y.dtype)
    spectral = jnp.fft.irfft(jnp.concatenate([back_y, tail], axis=3), n=NZ, axis=3).astype(jnp.float32)
    padded = jnp.pad(field, ((0, 0), (1, 1), (1, 1), (1, 1)), mode="wrap")
    conv = jnp.zeros(field.shape, jnp.float32)
    for shift_x in range(3):
        for shift_y in range(3):
            for shift_z in range(3):
                tap = dw_kernel[:, shift_x, shift_y, shift_z][:, None, None, None]
                conv = conv + tap * padded[:, shift_x:shift_x + NX, shift_y:shift_y + NY, shift_z:shift_z + NZ]
    pointwise = jnp.einsum("ixyz,io->oxyz", field, point_weight, precision=exact_mode)
    total = spectral + conv + pointwise + bias[:, None, None, None]
    return jax.nn.gelu(total)
```

```python
import functools

import jax
import jax.numpy as jnp
import numpy as np
from jax import lax
from jax.experimental import pallas as pl
from jax.experimental.pallas import tpu as pltpu
from jax.sharding import PartitionSpec as P

F32 = jnp.float32
BF16 = jnp.bfloat16


def halves(table):
    high = np.asarray(table, np.float32).astype(BF16)
    low = (np.asarray(table, np.float64) - high.astype(np.float64)).astype(BF16)
    return high, low


def kept(modes, length):
    index = np.arange(modes)
    return np.where(index < modes // 2, index, index + length - modes)


def angles(freqs, length):
    product = np.outer(freqs, np.arange(length)) % length
    turn = 2.0 * np.pi * product / length
    return np.cos(turn), np.sin(turn)


def tables(modes, full_x, full_y, depth):
    zc, zs = angles(np.arange(modes), depth)
    fz = np.stack([zc, -zs], axis=1).reshape(2 * modes, depth)
    weight = np.where(np.arange(modes) == 0, 1.0, 2.0)[:, None] / depth
    iz = np.stack([weight * zc, -weight * zs], axis=1).reshape(2 * modes, depth)
    yc, ys = angles(kept(modes, full_y), full_y)
    fy = np.block([[yc, ys], [-ys, yc]])
    iy = np.block([[yc.T, -ys.T], [ys.T, yc.T]]) / full_y
    xc, xs = angles(kept(modes, full_x), full_x)
    fx = np.concatenate(
        [np.stack([xc, xs], axis=2), np.stack([-xs, xc], axis=2)], axis=0
    ).reshape(2 * modes, 2 * full_x)
    ix = np.stack(
        [np.concatenate([xc.T, -xs.T], axis=1), np.concatenate([xs.T, xc.T], axis=1)]
    ) / full_x
    ix = ix.reshape(2, full_x // 4, 4, 2 * modes).transpose(2, 0, 1, 3)
    ix = ix.reshape(2 * full_x, 2 * modes)
    return {"fz": fz, "iz": iz, "fy": fy, "iy": iy, "fx": fx, "ix": ix}


def split(value):
    high = value.astype(BF16)
    return high, (value - high.astype(F32)).astype(BF16)


def mm(a, b):
    return jnp.dot(a, b, preferred_element_type=F32)


def mm_nt(a, b):
    return lax.dot_general(a, b, (((1,), (1,)), ((), ())), preferred_element_type=F32)


def mm_tn(a, b):
    return lax.dot_general(a, b, (((0,), (0,)), ((), ())), preferred_element_type=F32)


def table_dot(high_ref, low_ref, data):
    high, low = split(data)
    return mm(high_ref[...], high) + mm(high_ref[...], low) + mm(low_ref[...], high)


def forward_z(left_ref, right_ref, th_ref, tl_ref, out_ref, first_ref, middle_ref, last_ref):
    sides = [left_ref.reshape(1024, 128), right_ref.reshape(1024, 128)]
    both = jnp.concatenate([th_ref[...], tl_ref[...]], axis=0)
    for y in range(8):
        parts = [
            jnp.concatenate([side[pl.ds(x * 8 + y, 32, stride=32), :] for side in sides], axis=1)
            for x in range(4)
        ]
        first_ref[y] = parts[0]
        middle_ref[0, y] = parts[1]
        middle_ref[1, y] = parts[2]
        last_ref[y] = parts[3]
        high, low = split(jnp.concatenate(parts, axis=0))
        wide = mm_nt(both, high)
        total = wide[:64] + wide[64:] + mm_nt(th_ref[...], low)
        out_ref[:, y] = total.reshape(8, 8, 128)


def forward_y(data_ref, th_ref, tl_ref, out_ref):
    rows = data_ref.reshape(1024, 128)
    results = []
    for k in range(4):
        parts = [rows[pl.ds(2 * k + part, 128, stride=8), :] for part in range(2)]
        results.append(table_dot(th_ref, tl_ref, jnp.concatenate(parts, axis=0)))
    out = out_ref.reshape(256, 128)
    for x in range(4):
        tile = jnp.concatenate([r[:, 32 * x : 32 * x + 32] for r in results], axis=1)
        for part in range(2):
            out[pl.ds(2 * x + part, 32, stride=8), :] = tile[32 * part : 32 * part + 32]


def middle(data_ref, weight_ref, fh_ref, fl_ref, ih_ref, il_ref, out_ref):
    spec = table_dot(fh_ref, fl_ref, data_ref[...].reshape(256, 128))
    spec_re, spec_im = spec[:32], spec[32:]
    lane = lax.broadcasted_iota(jnp.int32, (32, 128), 1)
    group = lane - lax.rem(lane, 32)
    mixed_re = jnp.zeros((32, 128), F32)
    mixed_im = jnp.zeros((32, 128), F32)
    for c in range(32):
        index = group + c
        in_re = jnp.take_along_axis(spec_re, index, axis=1)
        in_im = jnp.take_along_axis(spec_im, index, axis=1)
        w_re, w_im = weight_ref[0, c], weight_ref[1, c]
        mixed_re = mixed_re + (in_re * w_re - in_im * w_im)
        mixed_im = mixed_im + (in_re * w_im + in_im * w_re)
    back = table_dot(ih_ref, il_ref, jnp.concatenate([mixed_re, mixed_im], axis=0))
    out = out_ref.reshape(256, 128)
    for k in range(4):
        tile = jnp.concatenate(
            [back[64 * x : 64 * x + 64, 32 * k : 32 * k + 32] for x in range(4)], axis=1
        )
        for part in range(2):
            out[pl.ds(2 * k + part, 32, stride=8), :] = tile[32 * part : 32 * part + 32]


def inverse_y(data_ref, th_ref, tl_ref, out_ref):
    rows = data_ref.reshape(256, 128)
    out = out_ref.reshape(1024, 128)
    for k in range(4):
        parts = [rows[pl.ds(2 * k + part, 32, stride=8), :] for part in range(2)]
        result = table_dot(th_ref, tl_ref, jnp.concatenate(parts, axis=0))
        for part in range(2):
            out[pl.ds(2 * k + part, 128, stride=8), :] = result[128 * part : 128 * part + 128]


def final(data_ref, base_ref, th_ref, tl_ref, out_ref):
    rows = out_ref.reshape(1024, 128)
    table = jnp.concatenate([th_ref[...], th_ref[...], tl_ref[...]], axis=0)
    for y in range(8):
        high, low = split(data_ref[:, y].reshape(64, 128))
        stacked = jnp.concatenate([high, low, high], axis=0)
        spectral = mm_tn(stacked, table)
        for x in range(4):
            value = spectral[32 * x : 32 * x + 32] + base_ref[x, y]
            rows[pl.ds(x * 8 + y, 32, stride=32), :] = jax.nn.gelu(value)


def weights(data_ref, out_ref):
    def body(c, carry):
        for part in range(2):
            for k in range(4):
                start = (part * 128 + k) * 32 + c
                block = data_ref[pl.ds(start, 32, stride=128), :]
                out_ref[part, c, :, 32 * k : 32 * k + 32] = block
        return carry

    lax.fori_loop(0, 32, body, 0)


def local(
    first_ref, middle_ref, last_ref, before_ref, after_ref, left_ref, right_ref,
    tap_ref, ph_ref, pl_ref, bias_ref, out_ref, frame, sems
):
    moves = [
        (before_ref, frame.at[0, pl.ds(1, 16)]),
        (first_ref, frame.at[1, pl.ds(1, 16)]),
        (middle_ref, frame.at[pl.ds(2, 2), pl.ds(1, 16)]),
        (last_ref, frame.at[4, pl.ds(1, 16)]),
        (after_ref, frame.at[5, pl.ds(1, 16)]),
        (left_ref, frame.at[:, 0]),
        (right_ref, frame.at[:, 17]),
    ]
    copies = [
        pltpu.make_async_copy(src, dst, sems.at[i]) for i, (src, dst) in enumerate(moves)
    ]
    for copy in copies:
        copy.start()
    for copy in copies:
        copy.wait()
    point = jnp.concatenate([ph_ref[...], pl_ref[...], ph_ref[...]], axis=1)
    bias = jnp.concatenate([bias_ref[...]] * 4, axis=0)

    def pointwise(y, carry):
        data = frame[1:5, y + 1].reshape(128, 256)
        high, low = split(data)
        value = mm(point, jnp.concatenate([high, high, low], axis=0)) + bias
        out_ref[:, y] = value.reshape(4, 32, 256)
        return carry

    lax.fori_loop(0, 16, pointwise, 0)
    lane = lax.broadcasted_iota(jnp.int32, (8, 256), 1)
    for tile in range(4):
        chans = pl.ds(8 * tile, 8)
        taps = tap_ref[chans, :]
        taps = [
            jnp.broadcast_to(taps[:, i : i + 1], (8, 256)) for i in range(27)
        ]

        def row(y, carry):
            for x in range(4):
                sums = [None, None, None]
                for a in range(3):
                    for b in range(3):
                        cell = frame[x + a, y + b, chans, :]
                        for e in range(3):
                            term = taps[9 * a + 3 * b + e] * cell
                            sums[e] = term if sums[e] is None else sums[e] + term
                total = sums[1] + pltpu.roll(sums[0], 1, 1) + pltpu.roll(sums[2], 255, 1)
                out_ref[x, y, chans, :] = out_ref[x, y, chans, :] + total
            return carry

        lax.fori_loop(0, 16, row, 0)


VMEM = pl.BlockSpec(memory_space=pltpu.VMEM)
ANY = pl.BlockSpec(memory_space=pl.ANY)


def call(body, shapes, count, **kw):
    single = not isinstance(shapes, list)
    out_shape = [jax.ShapeDtypeStruct(s, F32) for s in ([shapes] if single else shapes)]
    kw.setdefault("in_specs", [VMEM] * count)
    kw.setdefault("out_specs", [VMEM] * len(out_shape))
    if single:
        out_shape = out_shape[0]
        if isinstance(kw["out_specs"], list):
            kw["out_specs"] = kw["out_specs"][0]
    return pl.pallas_call(body, out_shape=out_shape, name=body.__name__, **kw)


def shifted(axis, value, step):
    count = lax.axis_size(axis)
    return lax.ppermute(value, axis, [(i, (i + step) % count) for i in range(count)])


def exchange(value, axis):
    return lax.all_to_all(value, axis, split_axis=0, concat_axis=0, tiled=True)


def on_device(field, spec_weight, dw_kernel, point_weight, bias):
    tab = {
        name: tuple(jnp.asarray(half) for half in halves(value))
        for name, value in tables(32, 128, 128, 256).items()
    }
    whole = lambda *shape: pl.BlockSpec(shape, lambda i: (0,) * len(shape))
    zchunks, first, mid, last = call(
        forward_z,
        [(8, 16, 8, 128), (16, 32, 256), (2, 16, 32, 256), (16, 32, 256)],
        4,
        grid=(2,),
        in_specs=[
            pl.BlockSpec((128, 8, 128), lambda i: (0, i, 0)),
            pl.BlockSpec((128, 8, 128), lambda i: (0, i, 1)),
            whole(64, 256),
            whole(64, 256),
        ],
        out_specs=[
            pl.BlockSpec((8, 8, 8, 128), lambda i: (0, i, 0, 0)),
            pl.BlockSpec((8, 32, 256), lambda i: (i, 0, 0)),
            pl.BlockSpec((2, 8, 32, 256), lambda i: (0, i, 0, 0)),
            pl.BlockSpec((8, 32, 256), lambda i: (i, 0, 0)),
        ],
    )(field.reshape(128, 16, 256), field.reshape(128, 16, 256), *tab["fz"])
    zall = exchange(zchunks, "gy")
    before = shifted("gx", last, 1)
    after = shifted("gx", first, -1)
    packed = call(weights, (2, 32, 32, 128), 1)(spec_weight.reshape(8192, 32))
    ychunks = call(forward_y, (32, 8, 128), 3)(zall, *tab["fy"])
    yall = exchange(ychunks, "gx")
    rows = [before[None], first[None], mid, last[None], after[None]]
    top = jnp.concatenate([r[:, 15] for r in rows], axis=0)
    bottom = jnp.concatenate([r[:, 0] for r in rows], axis=0)
    left = shifted("gy", top, 1)
    right = shifted("gy", bottom, -1)
    xchunks = call(middle, (32, 8, 128), 6)(yall, packed, *tab["fx"], *tab["ix"])
    xall = exchange(xchunks, "gx")
    blocks = jnp.kron(jnp.eye(4, dtype=F32), point_weight.T)
    point_high = blocks.astype(BF16)
    point_low = (blocks - lax.reduce_precision(blocks, 8, 7)).astype(BF16)
    base = call(
        local,
        (4, 16, 32, 256),
        11,
        in_specs=[ANY] * 7 + [VMEM] * 4,
        scratch_shapes=[pltpu.VMEM((6, 18, 32, 256), F32), pltpu.SemaphoreType.DMA((7,))],
    )(
        first, mid, last, before, after, left, right,
        dw_kernel.reshape(32, 27), point_high, point_low, bias.reshape(32, 1),
    )
    back = call(inverse_y, (8, 16, 8, 128), 3)(xall, *tab["iy"])
    ball = exchange(back, "gy")
    out = call(
        final,
        (128, 16, 256),
        4,
        grid=(2, 2),
        in_specs=[
            pl.BlockSpec((8, 8, 8, 128), lambda i, j: (0, i, 0, 0)),
            pl.BlockSpec((4, 8, 32, 128), lambda i, j: (0, i, 0, j)),
            pl.BlockSpec((64, 128), lambda i, j: (0, j)),
            pl.BlockSpec((64, 128), lambda i, j: (0, j)),
        ],
        out_specs=pl.BlockSpec((128, 8, 128), lambda i, j: (0, i, j)),
    )(ball, base, *tab["iz"])
    return out.reshape(field.shape)


def solution(mesh):
    placed = (P(None, "gx", "gy", None), P(None, None, "gx", "gy", None, None), P(), P(), P())
    return jax.shard_map(
        on_device, mesh=mesh, in_specs=placed, out_specs=P(None, "gx", "gy", None), check_vma=False
    )
```

```python
import functools

import jax
import jax.numpy as jnp
import numpy as np
from jax import lax
from jax.experimental import pallas as pl
from jax.experimental.pallas import tpu as pltpu
from jax.sharding import PartitionSpec as P

F32 = jnp.float32
BF16 = jnp.bfloat16


def halves(table):
    high = np.asarray(table, np.float32).astype(BF16)
    low = (np.asarray(table, np.float64) - high.astype(np.float64)).astype(BF16)
    return high, low


def kept(modes, length):
    index = np.arange(modes)
    return np.where(index < modes // 2, index, index + length - modes)


def angles(freqs, length):
    product = np.outer(freqs, np.arange(length)) % length
    turn = 2.0 * np.pi * product / length
    return np.cos(turn), np.sin(turn)


def tables(modes, full_x, full_y, depth):
    zc, zs = angles(np.arange(modes), depth)
    fz = np.stack([zc, -zs], axis=1).reshape(2 * modes, depth)
    weight = np.where(np.arange(modes) == 0, 1.0, 2.0)[:, None] / depth
    iz = np.stack([weight * zc, -weight * zs], axis=1).reshape(2 * modes, depth)
    yc, ys = angles(kept(modes, full_y), full_y)
    fy = np.block([[yc, ys], [-ys, yc]])
    iy = np.block([[yc.T, -ys.T], [ys.T, yc.T]]) / full_y
    xc, xs = angles(kept(modes, full_x), full_x)
    fx = np.concatenate(
        [np.stack([xc, xs], axis=2), np.stack([-xs, xc], axis=2)], axis=0
    ).reshape(2 * modes, 2 * full_x)
    ix = np.stack(
        [np.concatenate([xc.T, -xs.T], axis=1), np.concatenate([xs.T, xc.T], axis=1)]
    ) / full_x
    ix = ix.reshape(2, full_x // 4, 4, 2 * modes).transpose(2, 0, 1, 3)
    ix = ix.reshape(2 * full_x, 2 * modes)
    return {"fz": fz, "iz": iz, "fy": fy, "iy": iy, "fx": fx, "ix": ix}


def split(value):
    high = value.astype(BF16)
    return high, (value - high.astype(F32)).astype(BF16)


def mm(a, b):
    return jnp.dot(a, b, preferred_element_type=F32)


def mm_nt(a, b):
    return lax.dot_general(a, b, (((1,), (1,)), ((), ())), preferred_element_type=F32)


def mm_tn(a, b):
    return lax.dot_general(a, b, (((0,), (0,)), ((), ())), preferred_element_type=F32)


def table_dot(high_ref, low_ref, data):
    high, low = split(data)
    return mm(high_ref[...], high) + mm(high_ref[...], low) + mm(low_ref[...], high)


def forward_z(left_ref, right_ref, th_ref, tl_ref, out_ref, first_ref, middle_ref, last_ref):
    sides = [left_ref.reshape(1024, 128), right_ref.reshape(1024, 128)]
    both = jnp.concatenate([th_ref[...], tl_ref[...]], axis=0)
    for y in range(8):
        parts = [
            jnp.concatenate([side[pl.ds(x * 8 + y, 32, stride=32), :] for side in sides], axis=1)
            for x in range(4)
        ]
        first_ref[y] = parts[0]
        middle_ref[0, y] = parts[1]
        middle_ref[1, y] = parts[2]
        last_ref[y] = parts[3]
        high, low = split(jnp.concatenate(parts, axis=0))
        wide = mm_nt(both, high)
        total = wide[:64] + wide[64:] + mm_nt(th_ref[...], low)
        out_ref[:, y] = total.reshape(8, 8, 128)


def forward_y(data_ref, th_ref, tl_ref, out_ref):
    rows = data_ref.reshape(1024, 128)
    results = []
    for k in range(4):
        parts = [rows[pl.ds(2 * k + part, 128, stride=8), :] for part in range(2)]
        results.append(table_dot(th_ref, tl_ref, jnp.concatenate(parts, axis=0)))
    out = out_ref.reshape(256, 128)
    for x in range(4):
        tile = jnp.concatenate([r[:, 32 * x : 32 * x + 32] for r in results], axis=1)
        for part in range(2):
            out[pl.ds(2 * x + part, 32, stride=8), :] = tile[32 * part : 32 * part + 32]


def middle(data_ref, weight_ref, fh_ref, fl_ref, ih_ref, il_ref, out_ref):
    spec = table_dot(fh_ref, fl_ref, data_ref[...].reshape(256, 128))
    spec_re, spec_im = spec[:32], spec[32:]
    lane = lax.broadcasted_iota(jnp.int32, (32, 128), 1)
    group = lane - lax.rem(lane, 32)
    mixed_re = jnp.zeros((32, 128), F32)
    mixed_im = jnp.zeros((32, 128), F32)
    for c in range(32):
        index = group + c
        in_re = jnp.take_along_axis(spec_re, index, axis=1)
        in_im = jnp.take_along_axis(spec_im, index, axis=1)
        w_re, w_im = weight_ref[0, c], weight_ref[1, c]
        mixed_re = mixed_re + (in_re * w_re - in_im * w_im)
        mixed_im = mixed_im + (in_re * w_im + in_im * w_re)
    back = table_dot(ih_ref, il_ref, jnp.concatenate([mixed_re, mixed_im], axis=0))
    out = out_ref.reshape(256, 128)
    for k in range(4):
        tile = jnp.concatenate(
            [back[64 * x : 64 * x + 64, 32 * k : 32 * k + 32] for x in range(4)], axis=1
        )
        for part in range(2):
            out[pl.ds(2 * k + part, 32, stride=8), :] = tile[32 * part : 32 * part + 32]


def inverse_y(data_ref, th_ref, tl_ref, out_ref):
    rows = data_ref.reshape(256, 128)
    out = out_ref.reshape(1024, 128)
    for k in range(4):
        parts = [rows[pl.ds(2 * k + part, 32, stride=8), :] for part in range(2)]
        result = table_dot(th_ref, tl_ref, jnp.concatenate(parts, axis=0))
        for part in range(2):
            out[pl.ds(2 * k + part, 128, stride=8), :] = result[128 * part : 128 * part + 128]


def final(data_ref, base_ref, th_ref, tl_ref, out_ref, held, sems):
    table = jnp.concatenate([th_ref[...], th_ref[...], tl_ref[...]], axis=0)
    copies = []
    for half in range(2):
        slots = [held.at[half, side] for side in range(2)]
        rows = [slot.reshape(1024, 128) for slot in slots]
        for y in range(8):
            high, low = split(data_ref[:, 8 * half + y].reshape(64, 128))
            stacked = jnp.concatenate([high, low, high], axis=0)
            spectral = mm_tn(stacked, table)
            for x in range(4):
                value = spectral[32 * x : 32 * x + 32] + base_ref[x, 8 * half + y]
                value = jax.nn.gelu(value)
                for side in range(2):
                    rows[side][pl.ds(x * 8 + y, 32, stride=32), :] = value[
                        :, 128 * side : 128 * side + 128
                    ]
        for side in range(2):
            copy = pltpu.make_async_copy(
                slots[side],
                out_ref.at[:, pl.ds(8 * half, 8), pl.ds(128 * side, 128)],
                sems.at[half, side],
            )
            copy.start()
            copies.append(copy)
    for copy in copies:
        copy.wait()


def weights(data_ref, out_ref, held, sem):
    copy = pltpu.make_async_copy(data_ref, held.at[:, pl.ds(0, 128), :], sem)
    copy.start()
    copy.wait()
    rows = held.reshape(64 * 136, 32)

    def body(c, carry):
        for part in range(2):
            for k in range(4):
                start = part * 32 * 136 + 32 * k + c
                block = rows[pl.ds(start, 32, stride=136), :]
                out_ref[part, c, :, 32 * k : 32 * k + 32] = block
        return carry

    lax.fori_loop(0, 32, body, 0)


def shift_sum(sums):
    whole = [jnp.concatenate(pair, axis=1) for pair in sums]
    return whole[1] + pltpu.roll(whole[0], 1, 1) + pltpu.roll(whole[2], 255, 1)


def tap_rows(tap_ref, chans, wanted):
    taps = tap_ref[chans, :]
    return {i: jnp.broadcast_to(taps[:, i : i + 1], (8, 128)) for i in wanted}


def add_taps(sums, taps, first, cells):
    for e in range(3):
        for side in range(2):
            term = taps[first + e] * cells[side]
            old = sums[e][side]
            sums[e][side] = term if old is None else old + term


def own_cells(
    first_ref, middle_ref, last_ref, tap_ref, ph_ref, pl_ref, bias_ref, out_ref, frame, sems
):
    moves = [
        (first_ref, frame.at[0, pl.ds(1, 16)]),
        (middle_ref, frame.at[pl.ds(1, 2), pl.ds(1, 16)]),
        (last_ref, frame.at[3, pl.ds(1, 16)]),
    ]
    copies = [
        pltpu.make_async_copy(src, dst, sems.at[i]) for i, (src, dst) in enumerate(moves)
    ]
    for copy in copies:
        copy.start()
    frame[:, 0] = jnp.zeros((4, 32, 256), F32)
    frame[:, 17] = jnp.zeros((4, 32, 256), F32)
    for copy in copies:
        copy.wait()
    point = jnp.concatenate([ph_ref[...], pl_ref[...], ph_ref[...]], axis=1)
    bias = jnp.concatenate([bias_ref[...]] * 4, axis=0)

    def pointwise(y, carry):
        data = frame[:, y + 1].reshape(128, 256)
        high, low = split(data)
        value = mm(point, jnp.concatenate([high, high, low], axis=0)) + bias
        out_ref[:, y] = value.reshape(4, 32, 256)
        return carry

    lax.fori_loop(0, 16, pointwise, 0)
    for tile in range(4):
        chans = pl.ds(8 * tile, 8)
        taps = tap_rows(tap_ref, chans, range(27))

        def row(y, carry):
            for x in range(4):
                sums = [[None, None] for _ in range(3)]
                for a in range(3):
                    if not 0 <= x + a - 1 < 4:
                        continue
                    for b in range(3):
                        cells = [
                            frame[x + a - 1, y + b, chans, 128 * side : 128 * side + 128]
                            for side in range(2)
                        ]
                        add_taps(sums, taps, 9 * a + 3 * b, cells)
                out_ref[x, y, chans, :] = out_ref[x, y, chans, :] + shift_sum(sums)
            return carry

        lax.fori_loop(0, 16, row, 0)


def edge_cells(
    base_ref, before_ref, after_ref, left_ref, right_ref, tap_ref, out_ref, frame, sems
):
    moves = [
        (before_ref, frame.at[0, pl.ds(1, 16)]),
        (left_ref.at[0], frame.at[0, 0]),
        (right_ref.at[0], frame.at[0, 17]),
        (after_ref, frame.at[1, pl.ds(1, 16)]),
        (left_ref.at[5], frame.at[1, 0]),
        (right_ref.at[5], frame.at[1, 17]),
    ]
    copies = [
        pltpu.make_async_copy(src, dst, sems.at[i]) for i, (src, dst) in enumerate(moves)
    ]
    for copy in copies:
        copy.start()
    for tile in range(4):
        chans = pl.ds(8 * tile, 8)
        for edge, source in enumerate((left_ref, right_ref)):
            b = 2 * edge
            y = 15 * edge
            taps = tap_rows(
                tap_ref, chans, [9 * a + 3 * b + e for a in range(3) for e in range(3)]
            )
            for x in range(4):
                sums = [[None, None] for _ in range(3)]
                for a in range(3):
                    if not 0 <= x + a - 1 < 4:
                        continue
                    cells = [
                        source[x + a, chans, 128 * side : 128 * side + 128]
                        for side in range(2)
                    ]
                    add_taps(sums, taps, 9 * a + 3 * b, cells)
                out_ref[x, y, chans, :] = base_ref[x, y, chans, :] + shift_sum(sums)
    for copy in copies:
        copy.wait()
    for tile in range(4):
        chans = pl.ds(8 * tile, 8)
        for edge in range(2):
            a, x = 2 * edge, 3 * edge
            taps = tap_rows(tap_ref, chans, range(9 * a, 9 * a + 9))

            def row(y, carry):
                sums = [[None, None] for _ in range(3)]
                for b in range(3):
                    cells = [
                        frame[edge, y + b, chans, 128 * side : 128 * side + 128]
                        for side in range(2)
                    ]
                    add_taps(sums, taps, 9 * a + 3 * b, cells)
                out_ref[x, y, chans, :] = out_ref[x, y, chans, :] + shift_sum(sums)
                return carry

            lax.fori_loop(0, 16, row, 0, unroll=2)


VMEM = pl.BlockSpec(memory_space=pltpu.VMEM)
ANY = pl.BlockSpec(memory_space=pl.ANY)


def call(body, shapes, inputs, **kw):
    out_shape = [shape if kind is None else kind(shape, F32) for shape, kind in shapes]
    kw.setdefault("in_specs", [VMEM] * inputs)
    kw.setdefault("out_specs", [VMEM] * len(out_shape))
    return pl.pallas_call(body, out_shape=out_shape, name=body.__name__, **kw)


def near(value):
    return pltpu.with_memory_space_constraint(value, pltpu.VMEM)


def after_all(value, *others):
    return lax.optimization_barrier((value, *others))[0]


def shifted(axis, value, step):
    count = lax.axis_size(axis)
    return lax.ppermute(value, axis, [(i, (i + step) % count) for i in range(count)])


def exchange(value, axis):
    return lax.all_to_all(value, axis, split_axis=0, concat_axis=0, tiled=True)


def on_device(field, spec_weight, dw_kernel, point_weight, bias):
    tab = {
        name: tuple(jnp.asarray(half) for half in halves(value))
        for name, value in tables(32, 128, 128, 256).items()
    }
    whole = lambda *shape: pl.BlockSpec(shape, lambda i: (0,) * len(shape))
    plain, kept_near = jax.ShapeDtypeStruct, pltpu.VMEM
    cells = field.reshape(128, 16, 256)
    zchunks, first, mid, last = call(
        forward_z,
        [
            ((8, 16, 8, 128), plain),
            ((16, 32, 256), plain),
            ((2, 16, 32, 256), plain),
            ((16, 32, 256), plain),
        ],
        4,
        grid=(2,),
        in_specs=[
            pl.BlockSpec((128, 8, 128), lambda i: (0, i, 0)),
            pl.BlockSpec((128, 8, 128), lambda i: (0, i, 1)),
            whole(64, 256),
            whole(64, 256),
        ],
        out_specs=[
            pl.BlockSpec((8, 8, 8, 128), lambda i: (0, i, 0, 0)),
            pl.BlockSpec((8, 32, 256), lambda i: (i, 0, 0)),
            pl.BlockSpec((2, 8, 32, 256), lambda i: (0, i, 0, 0)),
            pl.BlockSpec((8, 32, 256), lambda i: (i, 0, 0)),
        ],
    )(cells, cells, *tab["fz"])

    zall = exchange(zchunks, "gy")
    (packed,) = call(
        weights,
        [((2, 32, 32, 128), kept_near)],
        1,
        in_specs=[ANY],
        scratch_shapes=[pltpu.VMEM((64, 136, 32), F32), pltpu.SemaphoreType.DMA],
    )(after_all(spec_weight.reshape(64, 128, 32), zchunks))
    zall, packed = lax.optimization_barrier((zall, packed))
    (ychunks,) = call(forward_y, [((32, 8, 128), plain)], 3)(near(zall), *tab["fy"])

    yall = exchange(ychunks, "gx")
    edge_first, edge_last, _ = lax.optimization_barrier((first, last, ychunks))
    before = shifted("gx", edge_last, 1)
    after = shifted("gx", edge_first, -1)
    blocks = jnp.kron(jnp.eye(4, dtype=F32), point_weight.T)
    point_high = blocks.astype(BF16)
    point_low = (blocks - lax.reduce_precision(blocks, 8, 7)).astype(BF16)
    taps = dw_kernel.reshape(32, 27)
    (base,) = call(
        own_cells,
        [((4, 16, 32, 256), kept_near)],
        7,
        in_specs=[ANY] * 3 + [VMEM] * 4,
        scratch_shapes=[pltpu.VMEM((4, 18, 32, 256), F32), pltpu.SemaphoreType.DMA((3,))],
    )(
        after_all(first, ychunks), mid, last,
        taps, point_high, point_low, bias.reshape(32, 1),
    )
    yall, base = lax.optimization_barrier((yall, base))
    (xchunks,) = call(middle, [((32, 8, 128), plain)], 6)(
        near(yall), near(packed), *tab["fx"], *tab["ix"]
    )

    xall = exchange(xchunks, "gx")
    before, after, _ = lax.optimization_barrier((before, after, xchunks))
    rows = [before[None], first[None], mid, last[None], after[None]]
    top = jnp.concatenate([r[:, 15] for r in rows], axis=0)
    bottom = jnp.concatenate([r[:, 0] for r in rows], axis=0)
    left = shifted("gy", top, 1)
    right = shifted("gy", bottom, -1)
    (back,) = call(inverse_y, [((8, 16, 8, 128), plain)], 3)(near(xall), *tab["iy"])

    ball = exchange(back, "gy")
    left, right, _ = lax.optimization_barrier((left, right, back))
    (base,) = call(
        edge_cells,
        [((4, 16, 32, 256), kept_near)],
        6,
        in_specs=[VMEM] + [ANY] * 2 + [VMEM] * 3,
        scratch_shapes=[pltpu.VMEM((2, 18, 32, 256), F32), pltpu.SemaphoreType.DMA((6,))],
        input_output_aliases={0: 0},
    )(near(base), before, after, near(left), near(right), taps)
    ball, base = lax.optimization_barrier((ball, base))
    (out,) = call(
        final,
        [((128, 16, 256), plain)],
        4,
        out_specs=[ANY],
        scratch_shapes=[
            pltpu.VMEM((2, 2, 128, 8, 128), F32), pltpu.SemaphoreType.DMA((2, 2)),
        ],
    )(near(ball), near(base), *tab["iz"])
    return out.reshape(field.shape)


def solution(mesh):
    placed = (P(None, "gx", "gy", None), P(None, None, "gx", "gy", None, None), P(), P(), P())
    return jax.shard_map(
        on_device, mesh=mesh, in_specs=placed, out_specs=P(None, "gx", "gy", None), check_vma=False
    )
```

```python
import functools

import jax
import jax.numpy as jnp
import numpy as np
from jax import lax
from jax.experimental import pallas as pl
from jax.experimental.pallas import tpu as pltpu
from jax.sharding import PartitionSpec as P

F32 = jnp.float32
BF16 = jnp.bfloat16


def halves(table):
    high = np.asarray(table, np.float32).astype(BF16)
    low = (np.asarray(table, np.float64) - high.astype(np.float64)).astype(BF16)
    return high, low


def kept(modes, length):
    index = np.arange(modes)
    return np.where(index < modes // 2, index, index + length - modes)


def angles(freqs, length):
    product = np.outer(freqs, np.arange(length)) % length
    turn = 2.0 * np.pi * product / length
    return np.cos(turn), np.sin(turn)


def tables(modes, full_x, full_y, depth):
    zc, zs = angles(np.arange(modes), depth)
    fz = np.stack([zc, -zs], axis=1).reshape(2 * modes, depth)
    weight = np.where(np.arange(modes) == 0, 1.0, 2.0)[:, None] / depth
    iz = np.stack([weight * zc, -weight * zs], axis=1).reshape(2 * modes, depth)
    yc, ys = angles(kept(modes, full_y), full_y)
    fy = np.block([[yc, ys], [-ys, yc]])
    iy = np.block([[yc.T, -ys.T], [ys.T, yc.T]]) / full_y
    xc, xs = angles(kept(modes, full_x), full_x)
    fx = np.concatenate(
        [np.stack([xc, xs], axis=2), np.stack([-xs, xc], axis=2)], axis=0
    ).reshape(2 * modes, 2 * full_x)
    ix = np.stack(
        [np.concatenate([xc.T, -xs.T], axis=1), np.concatenate([xs.T, xc.T], axis=1)]
    ) / full_x
    ix = ix.reshape(2, full_x // 4, 4, 2 * modes).transpose(2, 0, 1, 3)
    ix = ix.reshape(2 * full_x, 2 * modes)
    return {"fz": fz, "iz": iz, "fy": fy, "iy": iy, "fx": fx, "ix": ix}


def split(value):
    high = value.astype(BF16)
    return high, (value - high.astype(F32)).astype(BF16)


def mm(a, b):
    return jnp.dot(a, b, preferred_element_type=F32)


def mm_nt(a, b):
    return lax.dot_general(a, b, (((1,), (1,)), ((), ())), preferred_element_type=F32)


def mm_tn(a, b):
    return lax.dot_general(a, b, (((0,), (0,)), ((), ())), preferred_element_type=F32)


def table_dot(high_ref, low_ref, data):
    high, low = split(data)
    return mm(high_ref[...], high) + mm(high_ref[...], low) + mm(low_ref[...], high)


def forward_z(
    cells_ref, th_ref, tl_ref, out_ref, first_ref, middle_ref, last_ref, held, ready, sems, done
):
    copies = []
    for half in range(2):
        for side in range(2):
            copy = pltpu.make_async_copy(
                cells_ref.at[:, pl.ds(8 * half, 8), pl.ds(128 * side, 128)],
                held.at[half, side],
                sems.at[half, side],
            )
            copy.start()
            copies.append(copy)
    both = jnp.concatenate([th_ref[...], tl_ref[...]], axis=0)
    results = []
    for half in range(2):
        for side in range(2):
            copies[2 * half + side].wait()
        sides = [held.at[half, side].reshape(1024, 128) for side in range(2)]
        for row in range(8):
            y = 8 * half + row
            parts = [
                jnp.concatenate(
                    [side[pl.ds(x * 8 + row, 32, stride=32), :] for side in sides], axis=1
                )
                for x in range(4)
            ]
            first_ref[y] = parts[0]
            middle_ref[0, y] = parts[1]
            middle_ref[1, y] = parts[2]
            last_ref[y] = parts[3]
            high, low = split(jnp.concatenate(parts, axis=0))
            wide = mm_nt(both, high)
            total = wide[:64] + wide[64:] + mm_nt(th_ref[...], low)
            ready[:, y] = total.reshape(8, 8, 128)
        result = pltpu.make_async_copy(
            ready.at[:, pl.ds(8 * half, 8)], out_ref.at[:, pl.ds(8 * half, 8)], done.at[half]
        )
        result.start()
        results.append(result)
    for result in results:
        result.wait()


def forward_y(data_ref, th_ref, tl_ref, out_ref):
    rows = data_ref.reshape(1024, 128)
    results = []
    for k in range(4):
        parts = [rows[pl.ds(2 * k + part, 128, stride=8), :] for part in range(2)]
        results.append(table_dot(th_ref, tl_ref, jnp.concatenate(parts, axis=0)))
    out = out_ref.reshape(256, 128)
    for x in range(4):
        tile = jnp.concatenate([r[:, 32 * x : 32 * x + 32] for r in results], axis=1)
        for part in range(2):
            out[pl.ds(2 * x + part, 32, stride=8), :] = tile[32 * part : 32 * part + 32]


def middle(data_ref, weight_ref, fh_ref, fl_ref, ih_ref, il_ref, out_ref):
    spec = table_dot(fh_ref, fl_ref, data_ref[...].reshape(256, 128))
    spec_re, spec_im = spec[:32], spec[32:]
    lane = lax.broadcasted_iota(jnp.int32, (32, 128), 1)
    group = lane - lax.rem(lane, 32)
    mixed_re = jnp.zeros((32, 128), F32)
    mixed_im = jnp.zeros((32, 128), F32)
    for c in range(32):
        index = group + c
        in_re = jnp.take_along_axis(spec_re, index, axis=1)
        in_im = jnp.take_along_axis(spec_im, index, axis=1)
        w_re, w_im = weight_ref[0, c], weight_ref[1, c]
        mixed_re = mixed_re + (in_re * w_re - in_im * w_im)
        mixed_im = mixed_im + (in_re * w_im + in_im * w_re)
    back = table_dot(ih_ref, il_ref, jnp.concatenate([mixed_re, mixed_im], axis=0))
    out = out_ref.reshape(256, 128)
    for k in range(4):
        tile = jnp.concatenate(
            [back[64 * x : 64 * x + 64, 32 * k : 32 * k + 32] for x in range(4)], axis=1
        )
        for part in range(2):
            out[pl.ds(2 * k + part, 32, stride=8), :] = tile[32 * part : 32 * part + 32]


def inverse_y(data_ref, th_ref, tl_ref, out_ref):
    rows = data_ref.reshape(256, 128)
    out = out_ref.reshape(1024, 128)
    for k in range(4):
        parts = [rows[pl.ds(2 * k + part, 32, stride=8), :] for part in range(2)]
        result = table_dot(th_ref, tl_ref, jnp.concatenate(parts, axis=0))
        for part in range(2):
            out[pl.ds(2 * k + part, 128, stride=8), :] = result[128 * part : 128 * part + 128]


def final(data_ref, low_ref, high_ref, th_ref, tl_ref, out_ref, held, sems):
    table = jnp.concatenate([th_ref[...], th_ref[...], tl_ref[...]], axis=0)
    copies = []
    for half in range(2):
        slots = [held.at[half, side] for side in range(2)]
        rows = [slot.reshape(1024, 128) for slot in slots]
        for y in range(8):
            high, low = split(data_ref[:, 8 * half + y].reshape(64, 128))
            stacked = jnp.concatenate([high, low, high], axis=0)
            spectral = mm_tn(stacked, table)
            for x in range(4):
                value = spectral[32 * x : 32 * x + 32] + (low_ref, high_ref)[half][x, y]
                value = jax.nn.gelu(value)
                for side in range(2):
                    rows[side][pl.ds(x * 8 + y, 32, stride=32), :] = value[
                        :, 128 * side : 128 * side + 128
                    ]
        for side in range(2):
            copy = pltpu.make_async_copy(
                slots[side],
                out_ref.at[:, pl.ds(8 * half, 8), pl.ds(128 * side, 128)],
                sems.at[half, side],
            )
            copy.start()
            copies.append(copy)
    for copy in copies:
        copy.wait()


def weights(data_ref, out_ref):
    rows = out_ref.reshape(2048, 128)

    def body(m, carry):
        for part in range(2):
            tile = jnp.concatenate(
                [data_ref[32 * part + m, 32 * k : 32 * k + 32, :] for k in range(4)], axis=1
            )
            rows[pl.ds(1024 * part + m, 32, stride=32), :] = tile
        return carry

    lax.fori_loop(0, 32, body, 0, unroll=4)


def rims(before_ref, first_ref, middle_ref, last_ref, after_ref, top_ref, bottom_ref, sems):
    rows = [before_ref, first_ref, middle_ref.at[0], middle_ref.at[1], last_ref, after_ref]
    copies = [
        pltpu.make_async_copy(row.at[y], out_ref.at[i], sems.at[side, i])
        for side, (out_ref, y) in enumerate(((bottom_ref, 0), (top_ref, 15)))
        for i, row in enumerate(rows)
    ]
    for copy in copies:
        copy.start()
    for copy in copies:
        copy.wait()


def shift_sum(sums):
    whole = [jnp.concatenate(pair, axis=1) for pair in sums]
    return whole[1] + pltpu.roll(whole[0], 1, 1) + pltpu.roll(whole[2], 255, 1)


def add_taps(sums, tap_ref, chans, first, load):
    cells = [load(slice(128 * side, 128 * side + 128)) for side in range(2)]
    for e in range(3):
        tap = tap_ref[first + e, chans, :]
        for side in range(2):
            term = tap * cells[side]
            old = sums[e][side]
            sums[e][side] = term if old is None else old + term


def own_lines(half, planes, tap_ref, ph_ref, pl_ref, bias_ref, out_ref):
    point = jnp.concatenate([ph_ref[...], pl_ref[...], ph_ref[...]], axis=1)
    bias = jnp.concatenate([bias_ref[...]] * 4, axis=0)

    def line(row, shifts):
        y = row + 8 * half
        data = jnp.concatenate([plane[y] for plane in planes], axis=0)
        high, low = split(data)
        value = mm(point, jnp.concatenate([high, high, low], axis=0)) + bias
        for tile in range(4):
            chans = slice(8 * tile, 8 * tile + 8)
            for x in range(4):
                sums = [[None, None] for _ in range(3)]
                for a in range(max(0, 1 - x), min(3, 5 - x)):
                    plane = planes[x + a - 1]
                    for b in shifts:
                        load = lambda lanes: plane[y + b - 1, chans, lanes]
                        add_taps(sums, tap_ref, chans, 9 * a + 3 * b, load)
                own = 32 * x + 8 * tile
                out_ref[x, row, chans, :] = value[own : own + 8] + shift_sum(sums)

    def body(row, carry):
        line(row, (0, 1, 2))
        return carry

    if half == 0:
        line(0, (1, 2))
        lax.fori_loop(1, 8, body, 0)
    else:
        lax.fori_loop(0, 7, body, 0)
        line(7, (0, 1))


def own_cells_low(
    first_ref, middle_ref, last_ref, dw_ref, ph_ref, pl_ref, bias_ref, out_ref, tap_ref
):
    for i in range(27):
        tap_ref[i] = jnp.broadcast_to(dw_ref[:, i : i + 1], (32, 128))
    planes = [first_ref, middle_ref.at[0], middle_ref.at[1], last_ref]
    own_lines(0, planes, tap_ref, ph_ref, pl_ref, bias_ref, out_ref)


def own_cells_high(
    first_ref, middle_ref, last_ref, tap_ref, ph_ref, pl_ref, bias_ref, out_ref
):
    planes = [first_ref, middle_ref.at[0], middle_ref.at[1], last_ref]
    own_lines(1, planes, tap_ref, ph_ref, pl_ref, bias_ref, out_ref)


def edge_cells(
    low_ref, high_ref, before_ref, after_ref, left_ref, right_ref, tap_ref, out_low_ref, out_high_ref
):
    for tile in range(4):
        chans = slice(8 * tile, 8 * tile + 8)
        for b, y, source, base_ref, out_ref in (
            (0, 0, left_ref, low_ref, out_low_ref),
            (2, 7, right_ref, high_ref, out_high_ref),
        ):
            for x in range(4):
                sums = [[None, None] for _ in range(3)]
                for a in range(max(0, 1 - x), min(3, 5 - x)):
                    load = lambda lanes: source[x + a, chans, lanes]
                    add_taps(sums, tap_ref, chans, 9 * a + 3 * b, load)
                out_ref[x, y, chans, :] = base_ref[x, y, chans, :] + shift_sum(sums)

    def line(out_ref, row, before_rows, after_rows):
        for a, x, rows in ((0, 0, before_rows), (2, 3, after_rows)):
            for tile in range(4):
                chans = slice(8 * tile, 8 * tile + 8)
                sums = [[None, None] for _ in range(3)]
                for b in range(3):
                    plane, at = rows[b]
                    load = lambda lanes: plane[at, chans, lanes]
                    add_taps(sums, tap_ref, chans, 9 * a + 3 * b, load)
                out_ref[x, row, chans, :] = out_ref[x, row, chans, :] + shift_sum(sums)

    def near_rows(plane, edge, y):
        low = (left_ref, edge) if y == 0 else (plane, y - 1)
        high = (right_ref, edge) if y == 15 else (plane, y + 1)
        return [low, (plane, y), high]

    for half, out_ref in enumerate((out_low_ref, out_high_ref)):

        def body(row, carry):
            y = row + 8 * half
            both = ([(plane, y + b - 1) for b in range(3)] for plane in (before_ref, after_ref))
            line(out_ref, row, *both)
            return carry

        lax.fori_loop(1 - half, 8 - half, body, 0)
        y = 15 * half
        line(out_ref, 7 * half, near_rows(before_ref, 0, y), near_rows(after_ref, 5, y))


VMEM = pl.BlockSpec(memory_space=pltpu.VMEM)
ANY = pl.BlockSpec(memory_space=pl.ANY)
HBM = pl.BlockSpec(memory_space=pltpu.HBM)


def call(body, shapes, inputs, microseconds=0, **kw):
    out_shape = [shape if kind is None else kind(shape, F32) for shape, kind in shapes]
    kw.setdefault("in_specs", [VMEM] * inputs)
    kw.setdefault("out_specs", [VMEM] * len(out_shape))
    kw["compiler_params"] = pltpu.CompilerParams(vmem_limit_bytes=16 * 2**20)
    kw["cost_estimate"] = pl.CostEstimate(
        flops=1_000_000_000 * microseconds, transcendentals=0, bytes_accessed=0
    )
    return pl.pallas_call(body, out_shape=out_shape, name=body.__name__, **kw)


def near(value):
    return pltpu.with_memory_space_constraint(value, pltpu.VMEM)


def after_all(value, *others):
    return lax.optimization_barrier((value, *others))[0]


def shifted(axis, value, step):
    count = lax.axis_size(axis)
    return lax.ppermute(value, axis, [(i, (i + step) % count) for i in range(count)])


def exchange(value, axis):
    return lax.all_to_all(value, axis, split_axis=0, concat_axis=0, tiled=True)


def on_device(field, spec_weight, dw_kernel, point_weight, bias):
    tab = {
        name: tuple(near(jnp.asarray(half)) for half in halves(value))
        for name, value in tables(32, 128, 128, 256).items()
    }
    plain, kept_near = jax.ShapeDtypeStruct, pltpu.VMEM
    dma = pltpu.SemaphoreType.DMA

    far = functools.partial(pltpu.with_memory_space_constraint, memory_space=pltpu.HBM)
    cells = far(field.reshape(128, 16, 256))
    zchunks, first, mid, last = call(
        forward_z,
        [
            ((8, 16, 8, 128), plain),
            ((16, 32, 256), kept_near),
            ((2, 16, 32, 256), kept_near),
            ((16, 32, 256), kept_near),
        ],
        3,
        in_specs=[HBM] + [VMEM] * 2,
        out_specs=[ANY] + [VMEM] * 3,
        scratch_shapes=[
            pltpu.VMEM((2, 2, 128, 8, 128), F32),
            pltpu.VMEM((8, 16, 8, 128), F32),
            dma((2, 2)),
            dma((2,)),
        ],
    )(cells, *tab["fz"])

    blocks = jnp.kron(jnp.eye(4, dtype=F32), point_weight.T)
    point_high = blocks.astype(BF16)
    point_low = (blocks - lax.reduce_precision(blocks, 8, 7)).astype(BF16)
    shared = (point_high, point_low, bias.reshape(32, 1))
    own_rows = tuple(near(rows) for rows in (first, mid, last))

    zall = exchange(zchunks, "gy")
    (packed,) = call(weights, [((2, 32, 32, 128), plain)], 1, 3)(
        near(after_all(spec_weight.reshape(64, 128, 32), zchunks))
    )
    base_low, taps = call(
        own_cells_low, [((4, 8, 32, 256), plain), ((27, 32, 128), plain)], 7, 3
    )(*own_rows, dw_kernel.reshape(32, 27), *shared)
    zall, packed, base_low = lax.optimization_barrier((zall, packed, base_low))
    (ychunks,) = call(forward_y, [((32, 8, 128), plain)], 3)(near(zall), *tab["fy"])

    yall = exchange(ychunks, "gx")
    first, last, taps, _ = lax.optimization_barrier((first, last, taps, ychunks))
    before = shifted("gx", last, 1)
    after = shifted("gx", first, -1)
    (base_high,) = call(own_cells_high, [((4, 8, 32, 256), plain)], 7, 8)(
        *own_rows, near(taps), *shared
    )
    yall, base_high = lax.optimization_barrier((yall, base_high))
    (xchunks,) = call(middle, [((32, 8, 128), plain)], 6)(
        near(yall), near(packed), *tab["fx"], *tab["ix"]
    )

    xall = exchange(xchunks, "gx")
    before, after, _ = lax.optimization_barrier((before, after, xchunks))
    top, bottom = call(
        rims,
        [((6, 32, 256), plain)] * 2,
        5,
        in_specs=[ANY] * 5,
        out_specs=[ANY] * 2,
        scratch_shapes=[dma((2, 6))],
    )(before, first, mid, last, after)
    left = shifted("gy", top, 1)
    right = shifted("gy", bottom, -1)
    xall, top, bottom = lax.optimization_barrier((xall, top, bottom))
    (back,) = call(inverse_y, [((8, 16, 8, 128), plain)], 3)(near(xall), *tab["iy"])

    ball = exchange(back, "gy")
    left, right, _ = lax.optimization_barrier((left, right, back))
    base_low, base_high = call(
        edge_cells,
        [((4, 8, 32, 256), kept_near)] * 2,
        7,
        40,
        input_output_aliases={0: 0, 1: 1},
    )(*(near(value) for value in (base_low, base_high, before, after, left, right, taps)))
    ball, base_low, base_high = lax.optimization_barrier((ball, base_low, base_high))
    (out,) = call(
        final,
        [((128, 16, 256), plain)],
        5,
        out_specs=[ANY],
        scratch_shapes=[pltpu.VMEM((2, 2, 128, 8, 128), F32), dma((2, 2))],
    )(near(ball), near(base_low), near(base_high), *tab["iz"])
    return out.reshape(field.shape)


def solution(mesh):
    placed = (P(None, "gx", "gy", None), P(None, None, "gx", "gy", None, None), P(), P(), P())
    return jax.shard_map(
        on_device, mesh=mesh, in_specs=placed, out_specs=P(None, "gx", "gy", None), check_vma=False
    )
```

```python
import functools

import jax
import jax.numpy as jnp
import numpy as np
from jax import lax
from jax.experimental import pallas as pl
from jax.experimental.pallas import tpu as pltpu
from jax.sharding import PartitionSpec as P

F32 = jnp.float32
BF16 = jnp.bfloat16


def halves(table):
    high = np.asarray(table, np.float32).astype(BF16)
    low = (np.asarray(table, np.float64) - high.astype(np.float64)).astype(BF16)
    return high, low


def kept(modes, length):
    index = np.arange(modes)
    return np.where(index < modes // 2, index, index + length - modes)


def angles(freqs, length):
    product = np.outer(freqs, np.arange(length)) % length
    turn = 2.0 * np.pi * product / length
    return np.cos(turn), np.sin(turn)


def tables(modes, full_x, full_y, depth):
    zc, zs = angles(np.arange(modes), depth)
    fz = np.stack([zc, -zs], axis=1).reshape(2 * modes, depth)
    weight = np.where(np.arange(modes) == 0, 1.0, 2.0)[:, None] / depth
    iz = np.stack([weight * zc, -weight * zs], axis=1).reshape(2 * modes, depth)
    yc, ys = angles(kept(modes, full_y), full_y)
    fy = np.block([[yc, ys], [-ys, yc]])
    iy = np.block([[yc.T, -ys.T], [ys.T, yc.T]]) / full_y
    xc, xs = angles(kept(modes, full_x), full_x)
    fx = np.concatenate(
        [np.stack([xc, xs], axis=2), np.stack([-xs, xc], axis=2)], axis=0
    ).reshape(2 * modes, 2 * full_x)
    ix = np.stack(
        [np.concatenate([xc.T, -xs.T], axis=1), np.concatenate([xs.T, xc.T], axis=1)]
    ) / full_x
    ix = ix.reshape(2, full_x // 4, 4, 2 * modes).transpose(2, 0, 1, 3)
    ix = ix.reshape(2 * full_x, 2 * modes)
    return {"fz": fz, "iz": iz, "fy": fy, "iy": iy, "fx": fx, "ix": ix}


def split(value):
    high = value.astype(BF16)
    return high, (value - high.astype(F32)).astype(BF16)


def mm(a, b):
    return jnp.dot(a, b, preferred_element_type=F32)


def mm_nt(a, b):
    return lax.dot_general(a, b, (((1,), (1,)), ((), ())), preferred_element_type=F32)


def mm_tn(a, b):
    return lax.dot_general(a, b, (((0,), (0,)), ((), ())), preferred_element_type=F32)


def table_dot(table_ref, data):
    high, low = split(data)
    return mm(table_ref[0], high) + mm(table_ref[0], low) + mm(table_ref[1], high)


def field_copies(cells_ref, held, sems):
    return [
        [
            pltpu.make_async_copy(
                cells_ref.at[:, pl.ds(8 * half, 8), pl.ds(128 * side, 128)],
                held.at[half, side],
                sems.at[half, side],
            )
            for side in range(2)
        ]
        for half in range(2)
    ]


def field_rows(held, y):
    sides = [held.at[y // 8, side].reshape(1024, 128) for side in range(2)]
    return [
        jnp.concatenate(
            [side[pl.ds(x * 8 + y % 8, 32, stride=32), :] for side in sides], axis=1
        )
        for x in range(4)
    ]


def start_all(copies):
    for copy in copies:
        copy.start()


def wait_all(copies):
    for copy in copies:
        copy.wait()


def forward_z(
    cells_ref, table_ref, out_ref, first_ref, last_ref, held, both, ready, firsts, lasts, sems, done
):
    load = pltpu.make_async_copy(table_ref, both, done.at[6])
    load.start()
    copies = field_copies(cells_ref, held, sems)
    start_all(copies[0] + copies[1])
    load.wait()
    results = []
    for half in range(2):
        wait_all(copies[half])
        span = pl.ds(8 * half, 8)
        for y in range(8 * half, 8 * half + 8):
            parts = field_rows(held, y)
            firsts[y] = parts[0]
            lasts[y] = parts[3]
            high, low = split(jnp.concatenate(parts, axis=0))
            wide = mm_nt(both[...], high)
            total = wide[:64] + wide[64:] + mm_nt(both[:64], low)
            ready[:, y] = total.reshape(8, 8, 128)
        moves = [
            (ready.at[:, span], out_ref.at[:, span]),
            (firsts.at[span], first_ref.at[span]),
            (lasts.at[span], last_ref.at[span]),
        ]
        for i, (src, dst) in enumerate(moves):
            results.append(pltpu.make_async_copy(src, dst, done.at[3 * half + i]))
            results[-1].start()
    wait_all(results)


def forward_y(data_ref, table_ref, out_ref):
    rows = data_ref.reshape(1024, 128)
    results = []
    for k in range(4):
        parts = [rows[pl.ds(2 * k + part, 128, stride=8), :] for part in range(2)]
        results.append(table_dot(table_ref, jnp.concatenate(parts, axis=0)))
    out = out_ref.reshape(256, 128)
    for x in range(4):
        tile = jnp.concatenate([r[:, 32 * x : 32 * x + 32] for r in results], axis=1)
        for part in range(2):
            out[pl.ds(2 * x + part, 32, stride=8), :] = tile[32 * part : 32 * part + 32]


def middle(data_ref, weight_ref, forward_ref, inverse_hbm, out_ref, inverse_ref, sem):
    load = pltpu.make_async_copy(inverse_hbm, inverse_ref, sem)
    load.start()
    spec = table_dot(forward_ref, data_ref[...].reshape(256, 128))
    spec_re, spec_im = spec[:32], spec[32:]
    lane = lax.broadcasted_iota(jnp.int32, (32, 128), 1)
    group = lane - lax.rem(lane, 32)
    mixed_re = jnp.zeros((32, 128), F32)
    mixed_im = jnp.zeros((32, 128), F32)
    for c in range(32):
        index = group + c
        in_re = jnp.take_along_axis(spec_re, index, axis=1)
        in_im = jnp.take_along_axis(spec_im, index, axis=1)
        w_re, w_im = weight_ref[0, c], weight_ref[1, c]
        mixed_re = mixed_re + (in_re * w_re - in_im * w_im)
        mixed_im = mixed_im + (in_re * w_im + in_im * w_re)
    load.wait()
    back = table_dot(inverse_ref, jnp.concatenate([mixed_re, mixed_im], axis=0))
    out = out_ref.reshape(256, 128)
    for k in range(4):
        tile = jnp.concatenate(
            [back[64 * x : 64 * x + 64, 32 * k : 32 * k + 32] for x in range(4)], axis=1
        )
        for part in range(2):
            out[pl.ds(2 * k + part, 32, stride=8), :] = tile[32 * part : 32 * part + 32]


def inverse_y(data_ref, table_ref, out_ref):
    rows = data_ref.reshape(256, 128)
    out = out_ref.reshape(1024, 128)
    for k in range(4):
        parts = [rows[pl.ds(2 * k + part, 32, stride=8), :] for part in range(2)]
        result = table_dot(table_ref, jnp.concatenate(parts, axis=0))
        for part in range(2):
            out[pl.ds(2 * k + part, 128, stride=8), :] = result[128 * part : 128 * part + 128]


def final(data_ref, base_ref, table_ref, out_ref, held, sems):
    table = jnp.concatenate([table_ref[0], table_ref[0], table_ref[1]], axis=0)
    copies = []
    for half in range(2):
        slots = [held.at[half, side] for side in range(2)]
        rows = [slot.reshape(1024, 128) for slot in slots]
        for y in range(8):
            high, low = split(data_ref[:, 8 * half + y].reshape(64, 128))
            stacked = jnp.concatenate([high, low, high], axis=0)
            spectral = mm_tn(stacked, table)
            for x in range(4):
                value = spectral[32 * x : 32 * x + 32] + base_ref[x, 8 * half + y]
                value = jax.nn.gelu(value)
                for side in range(2):
                    rows[side][pl.ds(x * 8 + y, 32, stride=32), :] = value[
                        :, 128 * side : 128 * side + 128
                    ]
        for side in range(2):
            copy = pltpu.make_async_copy(
                slots[side],
                out_ref.at[:, pl.ds(8 * half, 8), pl.ds(128 * side, 128)],
                sems.at[half, side],
            )
            copy.start()
            copies.append(copy)
    for copy in copies:
        copy.wait()


def weights(data_ref, out_ref, held, sems):
    copies = [
        pltpu.make_async_copy(
            data_ref.at[:, pl.ds(4 * i, 4)], held.at[:, pl.ds(4 * i, 4)], sems.at[i]
        )
        for i in range(8)
    ]
    for copy in copies:
        copy.start()
    rows = out_ref.reshape(2048, 128)
    for i in range(8):
        copies[i].wait()
        for m in range(4 * i, 4 * i + 4):
            for part in range(2):
                tile = jnp.concatenate(
                    [held[part, m, 32 * k : 32 * k + 32, :] for k in range(4)], axis=1
                )
                rows[pl.ds(1024 * part + m, 32, stride=32), :] = tile


def rims(rows_ref, before_ref, after_ref, top_ref, bottom_ref, sems):
    copies = []
    for side, out_ref in enumerate((bottom_ref, top_ref)):
        moves = [
            (rows_ref.at[side], out_ref.at[pl.ds(1, 4)]),
            (before_ref.at[15 * side], out_ref.at[0]),
            (after_ref.at[15 * side], out_ref.at[5]),
        ]
        copies += [
            pltpu.make_async_copy(src, dst, sems.at[side, i]) for i, (src, dst) in enumerate(moves)
        ]
    start_all(copies)
    wait_all(copies)


def shift_sum(sums):
    whole = [jnp.concatenate(pair, axis=1) for pair in sums]
    return whole[1] + pltpu.roll(whole[0], 1, 1) + pltpu.roll(whole[2], 255, 1)


def add_taps(sums, tap_ref, chans, first, load):
    cells = [load(slice(128 * side, 128 * side + 128)) for side in range(2)]
    for e in range(3):
        tap = tap_ref[first + e, chans, :]
        for side in range(2):
            term = tap * cells[side]
            old = sums[e][side]
            sums[e][side] = term if old is None else old + term


def spread_taps(dw_ref, tap_ref):
    rows = jnp.concatenate([dw_ref[a, b] for a in range(3) for b in range(3)], axis=0)
    columns = rows.T
    for i in range(27):
        tap_ref[i] = jnp.broadcast_to(columns[:, i : i + 1], (32, 128))


def own_cells(
    cells_ref, dw_ref, point_ref, bias_ref, out_ref, rim_ref, held, planes, tap_ref, sems
):
    copies = field_copies(cells_ref, held, sems)
    start_all(copies[0] + copies[1])
    spread_taps(dw_ref, tap_ref)
    channel_map = jnp.concatenate([jnp.concatenate([point_ref[...].T] * 4, axis=1)] * 4, axis=0)
    row = lax.broadcasted_iota(jnp.int32, (128, 128), 0)
    column = lax.broadcasted_iota(jnp.int32, (128, 128), 1)
    same = lax.div(row, 32) == lax.div(column, 32)
    high, low = split(jnp.where(same, channel_map, 0.0))
    point = jnp.concatenate([high, low, high], axis=1)
    bias = jnp.broadcast_to(bias_ref[...], (32, 32)).T[:, :1]
    bias = jnp.concatenate([bias] * 4, axis=0)
    for half in range(2):
        wait_all(copies[half])
        for y in range(8 * half, 8 * half + 8):
            parts = field_rows(held, y)
            for x in range(4):
                planes[x, y] = parts[x]
                if y % 15 == 0:
                    rim_ref[half, x] = parts[x]

    def line(y, shifts):
        high, low = split(planes[:, y].reshape(128, 256))
        value = mm(point, jnp.concatenate([high, high, low], axis=0)) + bias
        for tile in range(4):
            chans = slice(8 * tile, 8 * tile + 8)
            for x in range(4):
                sums = [[None, None] for _ in range(3)]
                for a in range(max(0, 1 - x), min(3, 5 - x)):
                    for b in shifts:
                        load = lambda lanes: planes[x + a - 1, y + b - 1, chans, lanes]
                        add_taps(sums, tap_ref, chans, 9 * a + 3 * b, load)
                own = 32 * x + 8 * tile
                out_ref[x, y, chans, :] = value[own : own + 8] + shift_sum(sums)

    def body(y, carry):
        line(y, (0, 1, 2))
        return carry

    line(0, (1, 2))
    lax.fori_loop(1, 15, body, 0)
    line(15, (0, 1))


def edge_cells(
    base_ref, before_hbm, after_hbm, left_hbm, right_hbm, dw_ref,
    out_ref, before_ref, after_ref, left_ref, right_ref, tap_ref, sems
):
    moves = [
        (left_hbm, left_ref), (right_hbm, right_ref), (before_hbm, before_ref), (after_hbm, after_ref)
    ]
    copies = [
        pltpu.make_async_copy(src, dst, sems.at[i]) for i, (src, dst) in enumerate(moves)
    ]
    for copy in copies:
        copy.start()
    spread_taps(dw_ref, tap_ref)
    for i, (b, y, source) in enumerate(((0, 0, left_ref), (2, 15, right_ref))):
        copies[i].wait()
        for tile in range(4):
            chans = slice(8 * tile, 8 * tile + 8)
            for x in range(4):
                sums = [[None, None] for _ in range(3)]
                for a in range(max(0, 1 - x), min(3, 5 - x)):
                    load = lambda lanes: source[x + a, chans, lanes]
                    add_taps(sums, tap_ref, chans, 9 * a + 3 * b, load)
                out_ref[x, y, chans, :] = base_ref[x, y, chans, :] + shift_sum(sums)
    copies[2].wait()
    copies[3].wait()

    def line(y, before_rows, after_rows):
        for a, x, rows in ((0, 0, before_rows), (2, 3, after_rows)):
            for tile in range(4):
                chans = slice(8 * tile, 8 * tile + 8)
                sums = [[None, None] for _ in range(3)]
                for b in range(3):
                    plane, at = rows[b]
                    load = lambda lanes: plane[at, chans, lanes]
                    add_taps(sums, tap_ref, chans, 9 * a + 3 * b, load)
                out_ref[x, y, chans, :] = out_ref[x, y, chans, :] + shift_sum(sums)

    def near_rows(plane, edge, y):
        low = (left_ref, edge) if y == 0 else (plane, y - 1)
        high = (right_ref, edge) if y == 15 else (plane, y + 1)
        return [low, (plane, y), high]

    def body(y, carry):
        line(y, *([(plane, y + b - 1) for b in range(3)] for plane in (before_ref, after_ref)))
        return carry

    lax.fori_loop(1, 15, body, 0, unroll=2)
    for y in (0, 15):
        line(y, near_rows(before_ref, 0, y), near_rows(after_ref, 5, y))


VMEM = pl.BlockSpec(memory_space=pltpu.VMEM)
ANY = pl.BlockSpec(memory_space=pl.ANY)
HBM = pl.BlockSpec(memory_space=pltpu.HBM)


def call(body, shapes, inputs, microseconds=0, **kw):
    out_shape = [shape if kind is None else kind(shape, F32) for shape, kind in shapes]
    kw.setdefault("in_specs", [VMEM] * inputs)
    kw.setdefault("out_specs", [VMEM] * len(out_shape))
    kw["compiler_params"] = pltpu.CompilerParams(vmem_limit_bytes=16 * 2**20)
    kw["cost_estimate"] = pl.CostEstimate(
        flops=1_000_000_000 * microseconds, transcendentals=0, bytes_accessed=0
    )
    return pl.pallas_call(body, out_shape=out_shape, name=body.__name__, **kw)


def near(value):
    return pltpu.with_memory_space_constraint(value, pltpu.VMEM)


def after_all(value, *others):
    return lax.optimization_barrier((value, *others))[0]


def shifted(axis, value, step):
    count = lax.axis_size(axis)
    return lax.ppermute(value, axis, [(i, (i + step) % count) for i in range(count)])


def exchange(value, axis):
    return lax.all_to_all(value, axis, split_axis=0, concat_axis=0, tiled=True)


def on_device(field, spec_weight, dw_kernel, point_weight, bias):
    tab = {
        name: np.stack(halves(value)) for name, value in tables(32, 128, 128, 256).items()
    }
    plain, kept_near = jax.ShapeDtypeStruct, pltpu.VMEM
    dma = pltpu.SemaphoreType.DMA
    far = functools.partial(pltpu.with_memory_space_constraint, memory_space=pltpu.HBM)
    cells = far(field.reshape(128, 16, 256))
    zchunks, first, last = call(
        forward_z,
        [((8, 16, 8, 128), plain), ((16, 32, 256), plain), ((16, 32, 256), plain)],
        2,
        in_specs=[HBM] * 2,
        out_specs=[ANY] * 3,
        scratch_shapes=[
            pltpu.VMEM((2, 2, 128, 8, 128), F32),
            pltpu.VMEM((128, 256), BF16),
            pltpu.VMEM((8, 16, 8, 128), F32),
            pltpu.VMEM((16, 32, 256), F32),
            pltpu.VMEM((16, 32, 256), F32),
            dma((2, 2)),
            dma((7,)),
        ],
    )(cells, far(jnp.asarray(tab["fz"].reshape(128, 256))))
    taps = dw_kernel.transpose(1, 2, 3, 0)

    zall = exchange(zchunks, "gy")
    (packed,) = call(
        weights,
        [((2, 32, 32, 128), kept_near)],
        1,
        3,
        in_specs=[HBM],
        scratch_shapes=[pltpu.VMEM((2, 32, 128, 32), F32), dma((8,))],
    )(far(after_all(spec_weight.reshape(2, 32, 128, 32), zchunks)))
    zall, packed = lax.optimization_barrier((zall, packed))
    (ychunks,) = call(forward_y, [((32, 8, 128), plain)], 2)(
        near(zall), near(jnp.asarray(tab["fy"]))
    )

    yall = exchange(ychunks, "gx")
    first, last, taps_now, _ = lax.optimization_barrier((first, last, taps, ychunks))
    before = shifted("gx", last, 1)
    after = shifted("gx", first, -1)
    base, own_rims = call(
        own_cells,
        [((4, 16, 32, 256), kept_near), ((2, 4, 32, 256), plain)],
        4,
        8,
        in_specs=[HBM] + [VMEM] * 3,
        scratch_shapes=[
            pltpu.VMEM((2, 2, 128, 8, 128), F32),
            pltpu.VMEM((4, 16, 32, 256), F32),
            pltpu.VMEM((27, 32, 128), F32),
            dma((2, 2)),
        ],
    )(cells, taps_now, point_weight, bias.reshape(1, 32))
    yall, base = lax.optimization_barrier((yall, base))
    (xchunks,) = call(
        middle,
        [((32, 8, 128), plain)],
        4,
        in_specs=[VMEM] * 3 + [ANY],
        scratch_shapes=[pltpu.VMEM((2, 256, 64), BF16), dma],
    )(near(yall), near(packed), near(jnp.asarray(tab["fx"])), far(jnp.asarray(tab["ix"])))

    xall = exchange(xchunks, "gx")
    before, after, _ = lax.optimization_barrier((before, after, xchunks))
    before, after = far(before), far(after)
    top, bottom = call(
        rims,
        [((6, 32, 256), plain)] * 2,
        3,
        in_specs=[ANY] * 3,
        out_specs=[ANY] * 2,
        scratch_shapes=[dma((2, 3))],
    )(own_rims, before, after)
    left = shifted("gy", top, 1)
    right = shifted("gy", bottom, -1)
    xall, top, bottom = lax.optimization_barrier((xall, top, bottom))
    (back,) = call(inverse_y, [((8, 16, 8, 128), plain)], 2)(
        near(xall), near(jnp.asarray(tab["iy"]))
    )

    ball = exchange(back, "gy")
    left, right, _ = lax.optimization_barrier((left, right, back))
    (base,) = call(
        edge_cells,
        [((4, 16, 32, 256), kept_near)],
        6,
        40,
        in_specs=[VMEM] + [ANY] * 4 + [VMEM],
        scratch_shapes=[
            pltpu.VMEM((16, 32, 256), F32),
            pltpu.VMEM((16, 32, 256), F32),
            pltpu.VMEM((6, 32, 256), F32),
            pltpu.VMEM((6, 32, 256), F32),
            pltpu.VMEM((27, 32, 128), F32),
            dma((4,)),
        ],
        input_output_aliases={0: 0},
    )(near(base), before, after, far(left), far(right), taps)
    ball, base = lax.optimization_barrier((ball, base))
    (out,) = call(
        final,
        [((128, 16, 256), plain)],
        3,
        out_specs=[ANY],
        scratch_shapes=[pltpu.VMEM((2, 2, 128, 8, 128), F32), dma((2, 2))],
    )(near(ball), near(base), near(jnp.asarray(tab["iz"])))
    return out.reshape(field.shape)


def solution(mesh):
    placed = (P(None, "gx", "gy", None), P(None, None, "gx", "gy", None, None), P(), P(), P())
    return jax.shard_map(
        on_device, mesh=mesh, in_specs=placed, out_specs=P(None, "gx", "gy", None), check_vma=False
    )
```

```python
import functools

import jax
import jax.numpy as jnp
import numpy as np
from jax import lax
from jax.experimental import pallas as pl
from jax.experimental.pallas import tpu as pltpu
from jax.sharding import PartitionSpec as P

F32 = jnp.float32
BF16 = jnp.bfloat16


def halves(table):
    high = np.asarray(table, np.float32).astype(BF16)
    low = (np.asarray(table, np.float64) - high.astype(np.float64)).astype(BF16)
    return high, low


def kept(modes, length):
    index = np.arange(modes)
    return np.where(index < modes // 2, index, index + length - modes)


def angles(freqs, length):
    product = np.outer(freqs, np.arange(length)) % length
    turn = 2.0 * np.pi * product / length
    return np.cos(turn), np.sin(turn)


def tables(modes, full_x, full_y, depth):
    zc, zs = angles(np.arange(modes), depth)
    fz = np.stack([zc, -zs], axis=1).reshape(2 * modes, depth)
    weight = np.where(np.arange(modes) == 0, 1.0, 2.0)[:, None] / depth
    iz = np.stack([weight * zc, -weight * zs], axis=1).reshape(2 * modes, depth)
    yc, ys = angles(kept(modes, full_y), full_y)
    fy = np.block([[yc, ys], [-ys, yc]])
    iy = np.block([[yc.T, -ys.T], [ys.T, yc.T]]) / full_y
    xc, xs = angles(kept(modes, full_x), full_x)
    fx = np.concatenate(
        [np.stack([xc, xs], axis=2), np.stack([-xs, xc], axis=2)], axis=0
    ).reshape(2 * modes, 2 * full_x)
    ix = np.stack(
        [np.concatenate([xc.T, -xs.T], axis=1), np.concatenate([xs.T, xc.T], axis=1)]
    ) / full_x
    ix = ix.reshape(2, full_x // 4, 4, 2 * modes).transpose(2, 0, 1, 3)
    ix = ix.reshape(2 * full_x, 2 * modes)
    return {"fz": fz, "iz": iz, "fy": fy, "iy": iy, "fx": fx, "ix": ix}


def split(value):
    high = value.astype(BF16)
    return high, (value - high.astype(F32)).astype(BF16)


def mm(a, b):
    return jnp.dot(a, b, preferred_element_type=F32)


def mm_nt(a, b):
    return lax.dot_general(a, b, (((1,), (1,)), ((), ())), preferred_element_type=F32)


def mm_tn(a, b):
    return lax.dot_general(a, b, (((0,), (0,)), ((), ())), preferred_element_type=F32)


def table_dot(table_ref, data):
    high, low = split(data)
    return mm(table_ref[0], high) + mm(table_ref[0], low) + mm(table_ref[1], high)


def field_copies(cells_ref, held, sems):
    return [
        [
            pltpu.make_async_copy(
                cells_ref.at[:, pl.ds(8 * half, 8), pl.ds(128 * side, 128)],
                held.at[half, side],
                sems.at[half, side],
            )
            for side in range(2)
        ]
        for half in range(2)
    ]


def field_rows(held, y):
    sides = [held.at[y // 8, side].reshape(1024, 128) for side in range(2)]
    return [
        jnp.concatenate(
            [side[pl.ds(x * 8 + y % 8, 32, stride=32), :] for side in sides], axis=1
        )
        for x in range(4)
    ]


def start_all(copies):
    for copy in copies:
        copy.start()


def wait_all(copies):
    for copy in copies:
        copy.wait()


def forward_z(cells_ref, table_ref, out_ref, held, both, ready, sems, done):
    load = pltpu.make_async_copy(table_ref, both, done.at[2])
    load.start()
    copies = field_copies(cells_ref, held, sems)
    start_all(copies[0] + copies[1])
    load.wait()
    results = []
    for half in range(2):
        wait_all(copies[half])
        span = pl.ds(8 * half, 8)
        for y in range(8 * half, 8 * half + 8):
            high, low = split(jnp.concatenate(field_rows(held, y), axis=0))
            wide = mm_nt(both[...], high)
            total = wide[:64] + wide[64:] + mm_nt(both[:64], low)
            ready[:, y] = total.reshape(8, 8, 128)
        results.append(
            pltpu.make_async_copy(ready.at[:, span], out_ref.at[:, span], done.at[half])
        )
        results[-1].start()
    wait_all(results)


def forward_y(data_ref, table_ref, out_ref):
    rows = data_ref.reshape(1024, 128)
    results = []
    for k in range(4):
        parts = [rows[pl.ds(2 * k + part, 128, stride=8), :] for part in range(2)]
        results.append(table_dot(table_ref, jnp.concatenate(parts, axis=0)))
    out = out_ref.reshape(256, 128)
    for x in range(4):
        tile = jnp.concatenate([r[:, 32 * x : 32 * x + 32] for r in results], axis=1)
        for part in range(2):
            out[pl.ds(2 * x + part, 32, stride=8), :] = tile[32 * part : 32 * part + 32]


def middle(
    data_ref, weight_ref, forward_hbm, inverse_hbm, out_ref, forward_ref, inverse_ref, sems
):
    first_load = pltpu.make_async_copy(forward_hbm, forward_ref, sems.at[0])
    load = pltpu.make_async_copy(inverse_hbm, inverse_ref, sems.at[1])
    first_load.start()
    load.start()
    first_load.wait()
    spec = table_dot(forward_ref, data_ref[...].reshape(256, 128))
    spec_re, spec_im = spec[:32], spec[32:]
    lane = lax.broadcasted_iota(jnp.int32, (32, 128), 1)
    group = lane - lax.rem(lane, 32)
    mixed_re = jnp.zeros((32, 128), F32)
    mixed_im = jnp.zeros((32, 128), F32)
    for c in range(32):
        index = group + c
        in_re = jnp.take_along_axis(spec_re, index, axis=1)
        in_im = jnp.take_along_axis(spec_im, index, axis=1)
        w_re, w_im = weight_ref[0, c], weight_ref[1, c]
        mixed_re = mixed_re + (in_re * w_re - in_im * w_im)
        mixed_im = mixed_im + (in_re * w_im + in_im * w_re)
    load.wait()
    back = table_dot(inverse_ref, jnp.concatenate([mixed_re, mixed_im], axis=0))
    out = out_ref.reshape(256, 128)
    for k in range(4):
        tile = jnp.concatenate(
            [back[64 * x : 64 * x + 64, 32 * k : 32 * k + 32] for x in range(4)], axis=1
        )
        for part in range(2):
            out[pl.ds(2 * k + part, 32, stride=8), :] = tile[32 * part : 32 * part + 32]


def inverse_y(data_ref, table_ref, out_ref):
    rows = data_ref.reshape(256, 128)
    out = out_ref.reshape(1024, 128)
    for k in range(4):
        parts = [rows[pl.ds(2 * k + part, 32, stride=8), :] for part in range(2)]
        result = table_dot(table_ref, jnp.concatenate(parts, axis=0))
        for part in range(2):
            out[pl.ds(2 * k + part, 128, stride=8), :] = result[128 * part : 128 * part + 128]


def final(data_ref, base_ref, table_ref, out_ref, held, sems):
    table = jnp.concatenate([table_ref[0], table_ref[0], table_ref[1]], axis=0)
    copies = []
    for half in range(2):
        slots = [held.at[half, side] for side in range(2)]
        rows = [slot.reshape(1024, 128) for slot in slots]
        for y in range(8):
            high, low = split(data_ref[:, 8 * half + y].reshape(64, 128))
            stacked = jnp.concatenate([high, low, high], axis=0)
            spectral = mm_tn(stacked, table)
            for x in range(4):
                value = spectral[32 * x : 32 * x + 32] + base_ref[x, 8 * half + y]
                value = jax.nn.gelu(value)
                for side in range(2):
                    rows[side][pl.ds(x * 8 + y, 32, stride=32), :] = value[
                        :, 128 * side : 128 * side + 128
                    ]
        for side in range(2):
            copy = pltpu.make_async_copy(
                slots[side],
                out_ref.at[:, pl.ds(8 * half, 8), pl.ds(128 * side, 128)],
                sems.at[half, side],
            )
            copy.start()
            copies.append(copy)
    for copy in copies:
        copy.wait()


def weights(data_ref, out_ref, held, sems):
    copies = [
        pltpu.make_async_copy(
            data_ref.at[:, pl.ds(4 * i, 4)], held.at[:, pl.ds(4 * i, 4)], sems.at[i]
        )
        for i in range(8)
    ]
    for copy in copies:
        copy.start()
    rows = out_ref.reshape(2048, 128)
    for i in range(8):
        copies[i].wait()
        for m in range(4 * i, 4 * i + 4):
            for part in range(2):
                tile = jnp.concatenate(
                    [held[part, m, 32 * k : 32 * k + 32, :] for k in range(4)], axis=1
                )
                rows[pl.ds(1024 * part + m, 32, stride=32), :] = tile


def rims(rows_ref, before_ref, after_ref, top_ref, bottom_ref, sems):
    copies = []
    for side, out_ref in enumerate((bottom_ref, top_ref)):
        moves = [
            (rows_ref.at[side], out_ref.at[pl.ds(1, 4)]),
            (before_ref.at[15 * side], out_ref.at[0]),
            (after_ref.at[15 * side], out_ref.at[5]),
        ]
        copies += [
            pltpu.make_async_copy(src, dst, sems.at[side, i]) for i, (src, dst) in enumerate(moves)
        ]
    start_all(copies)
    wait_all(copies)


def shift_sum(sums):
    whole = [jnp.concatenate(pair, axis=1) for pair in sums]
    return whole[1] + pltpu.roll(whole[0], 1, 1) + pltpu.roll(whole[2], 255, 1)


def add_taps(sums, tap_ref, chans, first, load):
    cells = [load(slice(128 * side, 128 * side + 128)) for side in range(2)]
    for e in range(3):
        tap = tap_ref[first + e, chans, :]
        for side in range(2):
            term = tap * cells[side]
            old = sums[e][side]
            sums[e][side] = term if old is None else old + term


def spread_taps(dw_ref, tap_ref):
    rows = jnp.concatenate([dw_ref[a, b] for a in range(3) for b in range(3)], axis=0)
    columns = rows.T
    for i in range(27):
        tap_ref[i] = jnp.broadcast_to(columns[:, i : i + 1], (32, 128))


def own_cells(
    cells_ref, dw_hbm, point_hbm, bias_hbm, out_ref, first_ref, last_ref, rim_ref,
    held, planes, tap_ref, dw_ref, point_ref, bias_ref, sems, small
):
    loads = [
        pltpu.make_async_copy(src, dst, small.at[i])
        for i, (src, dst) in enumerate(
            ((dw_hbm, dw_ref), (point_hbm, point_ref), (bias_hbm, bias_ref))
        )
    ]
    copies = field_copies(cells_ref, held, sems)
    start_all(loads + copies[0] + copies[1])
    wait_all(loads)
    spread_taps(dw_ref, tap_ref)
    channel_map = jnp.concatenate([jnp.concatenate([point_ref[...].T] * 4, axis=1)] * 4, axis=0)
    row = lax.broadcasted_iota(jnp.int32, (128, 128), 0)
    column = lax.broadcasted_iota(jnp.int32, (128, 128), 1)
    same = lax.div(row, 32) == lax.div(column, 32)
    high, low = split(jnp.where(same, channel_map, 0.0))
    point = jnp.concatenate([high, low, high], axis=1)
    bias = jnp.broadcast_to(bias_ref[...], (32, 32)).T[:, :1]
    bias = jnp.concatenate([bias] * 4, axis=0)

    def line(y, shifts):
        high, low = split(planes[:, y].reshape(128, 256))
        value = mm(point, jnp.concatenate([high, high, low], axis=0)) + bias
        for tile in range(4):
            chans = slice(8 * tile, 8 * tile + 8)
            for x in range(4):
                sums = [[None, None] for _ in range(3)]
                for a in range(max(0, 1 - x), min(3, 5 - x)):
                    for b in shifts:
                        load = lambda lanes: planes[x + a - 1, y + b - 1, chans, lanes]
                        add_taps(sums, tap_ref, chans, 9 * a + 3 * b, load)
                own = 32 * x + 8 * tile
                out_ref[x, y, chans, :] = value[own : own + 8] + shift_sum(sums)

    def body(y, carry):
        line(y, (0, 1, 2))
        return carry

    def fill(half):
        wait_all(copies[half])
        for y in range(8 * half, 8 * half + 8):
            for x, part in enumerate(field_rows(held, y)):
                planes[x, y] = part

    fill(0)
    line(0, (1, 2))
    lax.fori_loop(1, 7, body, 0)
    fill(1)
    moves = [
        (planes.at[0], first_ref),
        (planes.at[3], last_ref),
        (planes.at[:, 0], rim_ref.at[0]),
        (planes.at[:, 15], rim_ref.at[1]),
    ]
    results = [
        pltpu.make_async_copy(src, dst, small.at[3 + i]) for i, (src, dst) in enumerate(moves)
    ]
    start_all(results)
    lax.fori_loop(7, 15, body, 0)
    line(15, (0, 1))
    wait_all(results)


def edge_cells(
    base_ref, before_hbm, after_hbm, left_ref, right_ref, dw_hbm,
    out_ref, before_ref, after_ref, tap_ref, dw_ref, sems
):
    moves = [(dw_hbm, dw_ref), (before_hbm, before_ref), (after_hbm, after_ref)]
    copies = [
        pltpu.make_async_copy(src, dst, sems.at[i]) for i, (src, dst) in enumerate(moves)
    ]
    start_all(copies)
    copies[0].wait()
    spread_taps(dw_ref, tap_ref)
    for b, y, source in ((0, 0, left_ref), (2, 15, right_ref)):
        for tile in range(4):
            chans = slice(8 * tile, 8 * tile + 8)
            for x in range(4):
                sums = [[None, None] for _ in range(3)]
                for a in range(max(0, 1 - x), min(3, 5 - x)):
                    load = lambda lanes: source[x + a, chans, lanes]
                    add_taps(sums, tap_ref, chans, 9 * a + 3 * b, load)
                out_ref[x, y, chans, :] = base_ref[x, y, chans, :] + shift_sum(sums)
    wait_all(copies[1:])

    def line(y, before_rows, after_rows):
        for a, x, rows in ((0, 0, before_rows), (2, 3, after_rows)):
            for tile in range(4):
                chans = slice(8 * tile, 8 * tile + 8)
                sums = [[None, None] for _ in range(3)]
                for b in range(3):
                    plane, at = rows[b]
                    load = lambda lanes: plane[at, chans, lanes]
                    add_taps(sums, tap_ref, chans, 9 * a + 3 * b, load)
                out_ref[x, y, chans, :] = out_ref[x, y, chans, :] + shift_sum(sums)

    def near_rows(plane, edge, y):
        low = (left_ref, edge) if y == 0 else (plane, y - 1)
        high = (right_ref, edge) if y == 15 else (plane, y + 1)
        return [low, (plane, y), high]

    def body(y, carry):
        line(y, *([(plane, y + b - 1) for b in range(3)] for plane in (before_ref, after_ref)))
        return carry

    lax.fori_loop(1, 15, body, 0, unroll=2)
    for y in (0, 15):
        line(y, near_rows(before_ref, 0, y), near_rows(after_ref, 5, y))


VMEM = pl.BlockSpec(memory_space=pltpu.VMEM)
ANY = pl.BlockSpec(memory_space=pl.ANY)
HBM = pl.BlockSpec(memory_space=pltpu.HBM)


def call(body, shapes, inputs, microseconds=0, **kw):
    out_shape = [shape if kind is None else kind(shape, F32) for shape, kind in shapes]
    kw.setdefault("in_specs", [VMEM] * inputs)
    kw.setdefault("out_specs", [VMEM] * len(out_shape))
    kw["compiler_params"] = pltpu.CompilerParams(vmem_limit_bytes=16 * 2**20)
    kw["cost_estimate"] = pl.CostEstimate(
        flops=1_000_000_000 * microseconds, transcendentals=0, bytes_accessed=0
    )
    return pl.pallas_call(body, out_shape=out_shape, name=body.__name__, **kw)


def near(value):
    return pltpu.with_memory_space_constraint(value, pltpu.VMEM)


def after_all(value, *others):
    return lax.optimization_barrier((value, *others))[0]


def shifted(axis, value, step):
    count = lax.axis_size(axis)
    return lax.ppermute(value, axis, [(i, (i + step) % count) for i in range(count)])


def exchange(value, axis):
    return lax.all_to_all(value, axis, split_axis=0, concat_axis=0, tiled=True)


def on_device(field, spec_weight, dw_kernel, point_weight, bias):
    tab = {
        name: np.stack(halves(value)) for name, value in tables(32, 128, 128, 256).items()
    }
    plain, kept_near = jax.ShapeDtypeStruct, pltpu.VMEM
    dma = pltpu.SemaphoreType.DMA
    far = functools.partial(pltpu.with_memory_space_constraint, memory_space=pltpu.HBM)
    cells = far(field.reshape(128, 16, 256))
    (zchunks,) = call(
        forward_z,
        [((8, 16, 8, 128), plain)],
        2,
        in_specs=[HBM] * 2,
        out_specs=[ANY],
        scratch_shapes=[
            pltpu.VMEM((2, 2, 128, 8, 128), F32),
            pltpu.VMEM((128, 256), BF16),
            pltpu.VMEM((8, 16, 8, 128), F32),
            dma((2, 2)),
            dma((3,)),
        ],
    )(cells, far(jnp.asarray(tab["fz"].reshape(128, 256))))
    taps = dw_kernel.transpose(1, 2, 3, 0)

    zall = exchange(zchunks, "gy")
    base, first, last, own_rims = call(
        own_cells,
        [
            ((4, 16, 32, 256), kept_near),
            ((16, 32, 256), pltpu.HBM),
            ((16, 32, 256), pltpu.HBM),
            ((2, 4, 32, 256), pltpu.HBM),
        ],
        4,
        8,
        in_specs=[HBM] * 4,
        out_specs=[VMEM] + [HBM] * 3,
        scratch_shapes=[
            pltpu.VMEM((2, 2, 128, 8, 128), F32),
            pltpu.VMEM((4, 16, 32, 256), F32),
            pltpu.VMEM((27, 32, 128), F32),
            pltpu.VMEM((3, 3, 3, 32), F32),
            pltpu.VMEM((32, 32), F32),
            pltpu.VMEM((1, 32), F32),
            dma((2, 2)),
            dma((7,)),
        ],
    )(far(after_all(cells, zchunks)), far(taps), far(point_weight), far(bias.reshape(1, 32)))
    zall, base = lax.optimization_barrier((zall, base))
    (ychunks,) = call(forward_y, [((32, 8, 128), plain)], 2)(
        near(zall), near(jnp.asarray(tab["fy"]))
    )

    yall = exchange(ychunks, "gx")
    first, last, pairs, _ = lax.optimization_barrier((first, last, spec_weight, ychunks))
    before = shifted("gx", far(last), 1)
    after = shifted("gx", far(first), -1)
    (packed,) = call(
        weights,
        [((2, 32, 32, 128), kept_near)],
        1,
        8,
        in_specs=[HBM],
        scratch_shapes=[pltpu.VMEM((2, 32, 128, 32), F32), dma((8,))],
    )(far(pairs.reshape(2, 32, 128, 32)))
    yall, packed = lax.optimization_barrier((yall, packed))
    (xchunks,) = call(
        middle,
        [((32, 8, 128), plain)],
        4,
        in_specs=[VMEM] * 2 + [ANY] * 2,
        scratch_shapes=[
            pltpu.VMEM((2, 64, 256), BF16),
            pltpu.VMEM((2, 256, 64), BF16),
            dma((2,)),
        ],
    )(near(yall), near(packed), far(jnp.asarray(tab["fx"])), far(jnp.asarray(tab["ix"])))

    xall = exchange(xchunks, "gx")
    before, after, _ = lax.optimization_barrier((before, after, xchunks))
    before, after = far(before), far(after)
    top, bottom = call(
        rims,
        [((6, 32, 256), pltpu.HBM)] * 2,
        3,
        2,
        in_specs=[HBM] * 3,
        out_specs=[HBM] * 2,
        scratch_shapes=[dma((2, 3))],
    )(far(own_rims), before, after)
    left = shifted("gy", top, 1)
    right = shifted("gy", bottom, -1)
    xall, top, bottom = lax.optimization_barrier((xall, top, bottom))
    (back,) = call(inverse_y, [((8, 16, 8, 128), plain)], 2)(
        near(xall), near(jnp.asarray(tab["iy"]))
    )

    ball = exchange(back, "gy")
    left, right, _ = lax.optimization_barrier((left, right, back))
    (base,) = call(
        edge_cells,
        [((4, 16, 32, 256), kept_near)],
        6,
        40,
        in_specs=[VMEM] + [ANY] * 2 + [VMEM] * 2 + [ANY],
        scratch_shapes=[
            pltpu.VMEM((16, 32, 256), F32),
            pltpu.VMEM((16, 32, 256), F32),
            pltpu.VMEM((27, 32, 128), F32),
            pltpu.VMEM((3, 3, 3, 32), F32),
            dma((3,)),
        ],
        input_output_aliases={0: 0},
    )(near(base), before, after, near(left), near(right), far(taps))
    ball, base = lax.optimization_barrier((ball, base))
    (out,) = call(
        final,
        [((128, 16, 256), plain)],
        3,
        out_specs=[ANY],
        scratch_shapes=[pltpu.VMEM((2, 2, 128, 8, 128), F32), dma((2, 2))],
    )(near(ball), near(base), near(jnp.asarray(tab["iz"])))
    return out.reshape(field.shape)


def solution(mesh):
    placed = (P(None, "gx", "gy", None), P(None, None, "gx", "gy", None, None), P(), P(), P())
    return jax.shard_map(
        on_device, mesh=mesh, in_specs=placed, out_specs=P(None, "gx", "gy", None), check_vma=False
    )
```

```python
import functools

import jax
import jax.numpy as jnp
import numpy as np
from jax import lax
from jax.experimental import pallas as pl
from jax.experimental.pallas import tpu as pltpu
from jax.sharding import PartitionSpec as P

F32 = jnp.float32
BF16 = jnp.bfloat16


def halves(table):
    high = np.asarray(table, np.float32).astype(BF16)
    low = (np.asarray(table, np.float64) - high.astype(np.float64)).astype(BF16)
    return high, low


def kept(modes, length):
    index = np.arange(modes)
    return np.where(index < modes // 2, index, index + length - modes)


def angles(freqs, length):
    product = np.outer(freqs, np.arange(length)) % length
    turn = 2.0 * np.pi * product / length
    return np.cos(turn), np.sin(turn)


def tables(modes, full_x, full_y, depth):
    zc, zs = angles(np.arange(modes), depth)
    fz = np.stack([zc, -zs], axis=1).reshape(2 * modes, depth)
    weight = np.where(np.arange(modes) == 0, 1.0, 2.0)[:, None] / depth
    iz = np.stack([weight * zc, -weight * zs], axis=1).reshape(2 * modes, depth)
    yc, ys = angles(kept(modes, full_y), full_y)
    fy = np.block([[yc, ys], [-ys, yc]])
    iy = np.block([[yc.T, -ys.T], [ys.T, yc.T]]) / full_y
    xc, xs = angles(kept(modes, full_x), full_x)
    fx = np.concatenate(
        [np.stack([xc, xs], axis=2), np.stack([-xs, xc], axis=2)], axis=0
    ).reshape(2 * modes, 2 * full_x)
    ix = np.stack(
        [np.concatenate([xc.T, -xs.T], axis=1), np.concatenate([xs.T, xc.T], axis=1)]
    ) / full_x
    ix = ix.reshape(2, full_x // 4, 4, 2 * modes).transpose(2, 0, 1, 3)
    ix = ix.reshape(2 * full_x, 2 * modes)
    return {"fz": fz, "iz": iz, "fy": fy, "iy": iy, "fx": fx, "ix": ix}


def split(value):
    high = value.astype(BF16)
    return high, (value - high.astype(F32)).astype(BF16)


def mm(a, b):
    return jnp.dot(a, b, preferred_element_type=F32)


def mm_nt(a, b):
    return lax.dot_general(a, b, (((1,), (1,)), ((), ())), preferred_element_type=F32)


def mm_tn(a, b):
    return lax.dot_general(a, b, (((0,), (0,)), ((), ())), preferred_element_type=F32)


def table_dot(table_ref, data):
    high, low = split(data)
    return mm(table_ref[0], high) + mm(table_ref[0], low) + mm(table_ref[1], high)


def field_copies(cells_ref, held, sems):
    return [
        [
            pltpu.make_async_copy(
                cells_ref.at[:, pl.ds(8 * half, 8), pl.ds(128 * side, 128)],
                held.at[half, side],
                sems.at[half, side],
            )
            for side in range(2)
        ]
        for half in range(2)
    ]


def field_rows(held, y):
    sides = [held.at[y // 8, side].reshape(1024, 128) for side in range(2)]
    return [
        jnp.concatenate(
            [side[pl.ds(x * 8 + y % 8, 32, stride=32), :] for side in sides], axis=1
        )
        for x in range(4)
    ]


def start_all(copies):
    for copy in copies:
        copy.start()


def wait_all(copies):
    for copy in copies:
        copy.wait()


def forward_z(cells_ref, table_ref, out_ref, held, both, ready, sems, done):
    load = pltpu.make_async_copy(table_ref, both, done.at[2])
    load.start()
    copies = field_copies(cells_ref, held, sems)
    start_all(copies[0] + copies[1])
    load.wait()
    results = []
    for half in range(2):
        wait_all(copies[half])
        span = pl.ds(8 * half, 8)
        for y in range(8 * half, 8 * half + 8):
            high, low = split(jnp.concatenate(field_rows(held, y), axis=0))
            wide = mm_nt(both[...], high)
            total = wide[:64] + wide[64:] + mm_nt(both[:64], low)
            ready[:, y] = total.reshape(8, 8, 128)
        results.append(
            pltpu.make_async_copy(ready.at[:, span], out_ref.at[:, span], done.at[half])
        )
        results[-1].start()
    wait_all(results)


def forward_y(data_ref, table_ref, out_ref):
    rows = data_ref.reshape(1024, 128)
    results = []
    for k in range(4):
        parts = [rows[pl.ds(2 * k + part, 128, stride=8), :] for part in range(2)]
        results.append(table_dot(table_ref, jnp.concatenate(parts, axis=0)))
    out = out_ref.reshape(256, 128)
    for x in range(4):
        tile = jnp.concatenate([r[:, 32 * x : 32 * x + 32] for r in results], axis=1)
        for part in range(2):
            out[pl.ds(2 * x + part, 32, stride=8), :] = tile[32 * part : 32 * part + 32]


def middle(
    data_ref, weight_ref, forward_hbm, inverse_hbm, out_ref, forward_ref, inverse_ref, sems
):
    first_load = pltpu.make_async_copy(forward_hbm, forward_ref, sems.at[0])
    load = pltpu.make_async_copy(inverse_hbm, inverse_ref, sems.at[1])
    first_load.start()
    load.start()
    first_load.wait()
    spec = table_dot(forward_ref, data_ref[...].reshape(256, 128))
    spec_re, spec_im = spec[:32], spec[32:]
    lane = lax.broadcasted_iota(jnp.int32, (32, 128), 1)
    group = lane - lax.rem(lane, 32)
    mixed_re = jnp.zeros((32, 128), F32)
    mixed_im = jnp.zeros((32, 128), F32)
    for c in range(32):
        index = group + c
        in_re = jnp.take_along_axis(spec_re, index, axis=1)
        in_im = jnp.take_along_axis(spec_im, index, axis=1)
        w_re, w_im = weight_ref[0, c], weight_ref[1, c]
        mixed_re = mixed_re + (in_re * w_re - in_im * w_im)
        mixed_im = mixed_im + (in_re * w_im + in_im * w_re)
    load.wait()
    back = table_dot(inverse_ref, jnp.concatenate([mixed_re, mixed_im], axis=0))
    out = out_ref.reshape(256, 128)
    for k in range(4):
        tile = jnp.concatenate(
            [back[64 * x : 64 * x + 64, 32 * k : 32 * k + 32] for x in range(4)], axis=1
        )
        for part in range(2):
            out[pl.ds(2 * k + part, 32, stride=8), :] = tile[32 * part : 32 * part + 32]


def inverse_y(data_ref, table_ref, out_ref):
    rows = data_ref.reshape(256, 128)
    out = out_ref.reshape(1024, 128)
    for k in range(4):
        parts = [rows[pl.ds(2 * k + part, 32, stride=8), :] for part in range(2)]
        result = table_dot(table_ref, jnp.concatenate(parts, axis=0))
        for part in range(2):
            out[pl.ds(2 * k + part, 128, stride=8), :] = result[128 * part : 128 * part + 128]


def final(data_ref, base_ref, table_ref, out_ref, held, sems):
    table = jnp.concatenate([table_ref[0], table_ref[0], table_ref[1]], axis=0)
    copies = []
    for half in range(2):
        slots = [held.at[half, side] for side in range(2)]
        rows = [slot.reshape(1024, 128) for slot in slots]
        for y in range(8):
            high, low = split(data_ref[:, 8 * half + y].reshape(64, 128))
            stacked = jnp.concatenate([high, low, high], axis=0)
            spectral = mm_tn(stacked, table)
            for x in range(4):
                value = spectral[32 * x : 32 * x + 32] + base_ref[x, 8 * half + y]
                value = jax.nn.gelu(value)
                for side in range(2):
                    rows[side][pl.ds(x * 8 + y, 32, stride=32), :] = value[
                        :, 128 * side : 128 * side + 128
                    ]
        for side in range(2):
            copy = pltpu.make_async_copy(
                slots[side],
                out_ref.at[:, pl.ds(8 * half, 8), pl.ds(128 * side, 128)],
                sems.at[half, side],
            )
            copy.start()
            copies.append(copy)
    for copy in copies:
        copy.wait()


def weights(data_ref, out_ref, held, sems):
    copies = [
        pltpu.make_async_copy(
            data_ref.at[:, pl.ds(4 * i, 4)], held.at[:, pl.ds(4 * i, 4)], sems.at[i]
        )
        for i in range(8)
    ]
    for copy in copies:
        copy.start()
    rows = out_ref.reshape(2048, 128)
    for i in range(8):
        copies[i].wait()
        for m in range(4 * i, 4 * i + 4):
            for part in range(2):
                tile = jnp.concatenate(
                    [held[part, m, 32 * k : 32 * k + 32, :] for k in range(4)], axis=1
                )
                rows[pl.ds(1024 * part + m, 32, stride=32), :] = tile


def rims(rows_ref, before_ref, after_ref, top_ref, bottom_ref, sems):
    copies = []
    for side, out_ref in enumerate((bottom_ref, top_ref)):
        moves = [
            (rows_ref.at[side], out_ref.at[pl.ds(1, 4)]),
            (before_ref.at[15 * side], out_ref.at[0]),
            (after_ref.at[15 * side], out_ref.at[5]),
        ]
        copies += [
            pltpu.make_async_copy(src, dst, sems.at[side, i]) for i, (src, dst) in enumerate(moves)
        ]
    start_all(copies)
    wait_all(copies)


def shift_sum(sums):
    whole = [jnp.concatenate(pair, axis=1) for pair in sums]
    return whole[1] + pltpu.roll(whole[0], 1, 1) + pltpu.roll(whole[2], 255, 1)


def add_taps(sums, tap_ref, chans, first, load):
    cells = [load(slice(128 * side, 128 * side + 128)) for side in range(2)]
    for e in range(3):
        tap = tap_ref[first + e, chans, :]
        for side in range(2):
            term = tap * cells[side]
            old = sums[e][side]
            sums[e][side] = term if old is None else old + term


def spread_taps(dw_ref, tap_ref):
    rows = jnp.concatenate([dw_ref[a, b] for a in range(3) for b in range(3)], axis=0)
    columns = rows.T
    for i in range(27):
        tap_ref[i] = jnp.broadcast_to(columns[:, i : i + 1], (32, 128))


def own_cells(
    cells_ref, dw_hbm, point_hbm, bias_hbm, out_ref, first_ref, last_ref, rim_ref,
    held, planes, tap_ref, dw_ref, point_ref, bias_ref, sems, small
):
    loads = [
        pltpu.make_async_copy(src, dst, small.at[i])
        for i, (src, dst) in enumerate(
            ((dw_hbm, dw_ref), (point_hbm, point_ref), (bias_hbm, bias_ref))
        )
    ]
    copies = field_copies(cells_ref, held, sems)
    start_all(loads + copies[0] + copies[1])
    wait_all(loads)
    spread_taps(dw_ref, tap_ref)
    channel_map = jnp.concatenate([jnp.concatenate([point_ref[...].T] * 4, axis=1)] * 4, axis=0)
    row = lax.broadcasted_iota(jnp.int32, (128, 128), 0)
    column = lax.broadcasted_iota(jnp.int32, (128, 128), 1)
    same = lax.div(row, 32) == lax.div(column, 32)
    high, low = split(jnp.where(same, channel_map, 0.0))
    point = jnp.concatenate([high, low, high], axis=1)
    bias = jnp.broadcast_to(bias_ref[...], (32, 32)).T[:, :1]
    bias = jnp.concatenate([bias] * 4, axis=0)

    def line(y, shifts):
        high, low = split(planes[:, y].reshape(128, 256))
        value = mm(point, jnp.concatenate([high, high, low], axis=0)) + bias
        for tile in range(4):
            chans = slice(8 * tile, 8 * tile + 8)
            for x in range(4):
                sums = [[None, None] for _ in range(3)]
                for a in range(max(0, 1 - x), min(3, 5 - x)):
                    for b in shifts:
                        load = lambda lanes: planes[x + a - 1, y + b - 1, chans, lanes]
                        add_taps(sums, tap_ref, chans, 9 * a + 3 * b, load)
                own = 32 * x + 8 * tile
                out_ref[x, y, chans, :] = value[own : own + 8] + shift_sum(sums)

    def body(y, carry):
        line(y, (0, 1, 2))
        return carry

    def fill(half):
        wait_all(copies[half])
        for y in range(8 * half, 8 * half + 8):
            for x, part in enumerate(field_rows(held, y)):
                planes[x, y] = part

    fill(0)
    line(0, (1, 2))
    lax.fori_loop(1, 7, body, 0)
    fill(1)
    moves = [
        (planes.at[0], first_ref),
        (planes.at[3], last_ref),
        (planes.at[:, 0], rim_ref.at[0]),
        (planes.at[:, 15], rim_ref.at[1]),
    ]
    results = [
        pltpu.make_async_copy(src, dst, small.at[3 + i]) for i, (src, dst) in enumerate(moves)
    ]
    start_all(results)
    lax.fori_loop(7, 15, body, 0)
    line(15, (0, 1))
    wait_all(results)


def edge_cells(
    base_ref, before_hbm, after_hbm, left_ref, right_ref, dw_hbm,
    out_ref, before_ref, after_ref, tap_ref, dw_ref, sems
):
    moves = [(dw_hbm, dw_ref), (before_hbm, before_ref), (after_hbm, after_ref)]
    copies = [
        pltpu.make_async_copy(src, dst, sems.at[i]) for i, (src, dst) in enumerate(moves)
    ]
    start_all(copies)
    copies[0].wait()
    spread_taps(dw_ref, tap_ref)
    for b, y, source in ((0, 0, left_ref), (2, 15, right_ref)):
        for tile in range(4):
            chans = slice(8 * tile, 8 * tile + 8)
            for x in range(4):
                sums = [[None, None] for _ in range(3)]
                for a in range(max(0, 1 - x), min(3, 5 - x)):
                    load = lambda lanes: source[x + a, chans, lanes]
                    add_taps(sums, tap_ref, chans, 9 * a + 3 * b, load)
                out_ref[x, y, chans, :] = base_ref[x, y, chans, :] + shift_sum(sums)
    wait_all(copies[1:])

    def line(y, before_rows, after_rows):
        for a, x, rows in ((0, 0, before_rows), (2, 3, after_rows)):
            for tile in range(4):
                chans = slice(8 * tile, 8 * tile + 8)
                sums = [[None, None] for _ in range(3)]
                for b in range(3):
                    plane, at = rows[b]
                    load = lambda lanes: plane[at, chans, lanes]
                    add_taps(sums, tap_ref, chans, 9 * a + 3 * b, load)
                out_ref[x, y, chans, :] = out_ref[x, y, chans, :] + shift_sum(sums)

    def near_rows(plane, edge, y):
        low = (left_ref, edge) if y == 0 else (plane, y - 1)
        high = (right_ref, edge) if y == 15 else (plane, y + 1)
        return [low, (plane, y), high]

    def body(y, carry):
        line(y, *([(plane, y + b - 1) for b in range(3)] for plane in (before_ref, after_ref)))
        return carry

    lax.fori_loop(1, 15, body, 0, unroll=2)
    for y in (0, 15):
        line(y, near_rows(before_ref, 0, y), near_rows(after_ref, 5, y))


VMEM = pl.BlockSpec(memory_space=pltpu.VMEM)
ANY = pl.BlockSpec(memory_space=pl.ANY)
HBM = pl.BlockSpec(memory_space=pltpu.HBM)


def call(body, shapes, inputs, microseconds=0, **kw):
    out_shape = [shape if kind is None else kind(shape, F32) for shape, kind in shapes]
    kw.setdefault("in_specs", [VMEM] * inputs)
    kw.setdefault("out_specs", [VMEM] * len(out_shape))
    kw["compiler_params"] = pltpu.CompilerParams(vmem_limit_bytes=16 * 2**20)
    kw["cost_estimate"] = pl.CostEstimate(
        flops=1_000_000_000 * microseconds, transcendentals=0, bytes_accessed=0
    )
    return pl.pallas_call(body, out_shape=out_shape, name=body.__name__, **kw)


def near(value):
    return pltpu.with_memory_space_constraint(value, pltpu.VMEM)


def after_all(value, *others):
    return lax.optimization_barrier((value, *others))[0]


def shifted(axis, value, step):
    count = lax.axis_size(axis)
    return lax.ppermute(value, axis, [(i, (i + step) % count) for i in range(count)])


def exchange(value, axis):
    return lax.all_to_all(value, axis, split_axis=0, concat_axis=0, tiled=True)


def on_device(field, spec_weight, dw_kernel, point_weight, bias):
    tab = {
        name: np.stack(halves(value)) for name, value in tables(32, 128, 128, 256).items()
    }
    plain, kept_near = jax.ShapeDtypeStruct, pltpu.VMEM
    dma = pltpu.SemaphoreType.DMA
    far = functools.partial(pltpu.with_memory_space_constraint, memory_space=pltpu.HBM)
    cells = far(field.reshape(128, 16, 256))
    (zchunks,) = call(
        forward_z,
        [((8, 16, 8, 128), plain)],
        2,
        in_specs=[HBM] * 2,
        out_specs=[ANY],
        scratch_shapes=[
            pltpu.VMEM((2, 2, 128, 8, 128), F32),
            pltpu.VMEM((128, 256), BF16),
            pltpu.VMEM((8, 16, 8, 128), F32),
            dma((2, 2)),
            dma((3,)),
        ],
    )(cells, far(jnp.asarray(tab["fz"].reshape(128, 256))))
    taps = dw_kernel.transpose(1, 2, 3, 0)

    zall = exchange(zchunks, "gy")
    base, first, last, own_rims = call(
        own_cells,
        [
            ((4, 16, 32, 256), kept_near),
            ((16, 32, 256), pltpu.HBM),
            ((16, 32, 256), pltpu.HBM),
            ((2, 4, 32, 256), pltpu.HBM),
        ],
        4,
        8,
        in_specs=[HBM] * 4,
        out_specs=[VMEM] + [HBM] * 3,
        scratch_shapes=[
            pltpu.VMEM((2, 2, 128, 8, 128), F32),
            pltpu.VMEM((4, 16, 32, 256), F32),
            pltpu.VMEM((27, 32, 128), F32),
            pltpu.VMEM((3, 3, 3, 32), F32),
            pltpu.VMEM((32, 32), F32),
            pltpu.VMEM((1, 32), F32),
            dma((2, 2)),
            dma((7,)),
        ],
    )(far(after_all(cells, zchunks)), far(taps), far(point_weight), far(bias.reshape(1, 32)))
    zall, base = lax.optimization_barrier((zall, base))
    (ychunks,) = call(forward_y, [((32, 8, 128), plain)], 2)(
        near(zall), near(jnp.asarray(tab["fy"]))
    )

    yall = exchange(ychunks, "gx")
    first, last, pairs, _ = lax.optimization_barrier((first, last, spec_weight, ychunks))
    before = shifted("gx", far(last), 1)
    after = shifted("gx", far(first), -1)
    (packed,) = call(
        weights,
        [((2, 32, 32, 128), kept_near)],
        1,
        8,
        in_specs=[HBM],
        scratch_shapes=[pltpu.VMEM((2, 32, 128, 32), F32), dma((8,))],
    )(far(pairs.reshape(2, 32, 128, 32)))
    yall, packed = lax.optimization_barrier((yall, packed))
    (xchunks,) = call(
        middle,
        [((32, 8, 128), plain)],
        4,
        in_specs=[VMEM] * 2 + [ANY] * 2,
        scratch_shapes=[
            pltpu.VMEM((2, 64, 256), BF16),
            pltpu.VMEM((2, 256, 64), BF16),
            dma((2,)),
        ],
    )(near(yall), near(packed), far(jnp.asarray(tab["fx"])), far(jnp.asarray(tab["ix"])))

    xall = exchange(xchunks, "gx")
    before, after, _ = lax.optimization_barrier((before, after, xchunks))
    before, after = far(before), far(after)
    top, bottom = call(
        rims,
        [((6, 32, 256), kept_near)] * 2,
        3,
        2,
        in_specs=[HBM] * 3,
        scratch_shapes=[dma((2, 3))],
    )(far(own_rims), before, after)
    left = shifted("gy", top, 1)
    right = shifted("gy", bottom, -1)
    xall, top, bottom = lax.optimization_barrier((xall, top, bottom))
    (back,) = call(inverse_y, [((8, 16, 8, 128), plain)], 2)(
        near(xall), near(jnp.asarray(tab["iy"]))
    )

    ball = exchange(back, "gy")
    left, right, _ = lax.optimization_barrier((left, right, back))
    (base,) = call(
        edge_cells,
        [((4, 16, 32, 256), kept_near)],
        6,
        40,
        in_specs=[VMEM] + [ANY] * 2 + [VMEM] * 2 + [ANY],
        scratch_shapes=[
            pltpu.VMEM((16, 32, 256), F32),
            pltpu.VMEM((16, 32, 256), F32),
            pltpu.VMEM((27, 32, 128), F32),
            pltpu.VMEM((3, 3, 3, 32), F32),
            dma((3,)),
        ],
        input_output_aliases={0: 0},
    )(near(base), before, after, near(left), near(right), far(taps))
    ball, base = lax.optimization_barrier((ball, base))
    (out,) = call(
        final,
        [((128, 16, 256), plain)],
        3,
        out_specs=[ANY],
        scratch_shapes=[pltpu.VMEM((2, 2, 128, 8, 128), F32), dma((2, 2))],
    )(near(ball), near(base), near(jnp.asarray(tab["iz"])))
    return out.reshape(field.shape)


def solution(mesh):
    placed = (P(None, "gx", "gy", None), P(None, None, "gx", "gy", None, None), P(), P(), P())
    return jax.shard_map(
        on_device, mesh=mesh, in_specs=placed, out_specs=P(None, "gx", "gy", None), check_vma=False
    )
```

```python
import functools

import jax
import jax.numpy as jnp
import numpy as np
from jax import lax
from jax.experimental import pallas as pl
from jax.experimental.pallas import tpu as pltpu
from jax.sharding import PartitionSpec as P

F32 = jnp.float32
BF16 = jnp.bfloat16


def halves(table):
    high = np.asarray(table, np.float32).astype(BF16)
    low = (np.asarray(table, np.float64) - high.astype(np.float64)).astype(BF16)
    return high, low


def kept(modes, length):
    index = np.arange(modes)
    return np.where(index < modes // 2, index, index + length - modes)


def angles(freqs, length):
    product = np.outer(freqs, np.arange(length)) % length
    turn = 2.0 * np.pi * product / length
    return np.cos(turn), np.sin(turn)


def tables(modes, full_x, full_y, depth):
    zc, zs = angles(np.arange(modes), depth)
    fz = np.stack([zc, -zs], axis=1).reshape(2 * modes, depth)
    weight = np.where(np.arange(modes) == 0, 1.0, 2.0)[:, None] / depth
    iz = np.stack([weight * zc, -weight * zs], axis=1).reshape(2 * modes, depth)
    yc, ys = angles(kept(modes, full_y), full_y)
    fy = np.block([[yc, ys], [-ys, yc]])
    iy = np.block([[yc.T, -ys.T], [ys.T, yc.T]]) / full_y
    xc, xs = angles(kept(modes, full_x), full_x)
    fx = np.concatenate(
        [np.stack([xc, xs], axis=2), np.stack([-xs, xc], axis=2)], axis=0
    ).reshape(2 * modes, 2 * full_x)
    ix = np.stack(
        [np.concatenate([xc.T, -xs.T], axis=1), np.concatenate([xs.T, xc.T], axis=1)]
    ) / full_x
    ix = ix.reshape(2, full_x // 4, 4, 2 * modes).transpose(2, 0, 1, 3)
    ix = ix.reshape(2 * full_x, 2 * modes)
    return {"fz": fz, "iz": iz, "fy": fy, "iy": iy, "fx": fx, "ix": ix}


def split(value):
    high = value.astype(BF16)
    return high, (value - high.astype(F32)).astype(BF16)


def mm(a, b):
    return jnp.dot(a, b, preferred_element_type=F32)


def mm_nt(a, b):
    return lax.dot_general(a, b, (((1,), (1,)), ((), ())), preferred_element_type=F32)


def mm_tn(a, b):
    return lax.dot_general(a, b, (((0,), (0,)), ((), ())), preferred_element_type=F32)


def table_dot(table_ref, data):
    high, low = split(data)
    return mm(table_ref[0], high) + mm(table_ref[0], low) + mm(table_ref[1], high)


def field_copies(cells_ref, held, sems):
    return [
        [
            pltpu.make_async_copy(
                cells_ref.at[:, pl.ds(8 * half, 8), pl.ds(128 * side, 128)],
                held.at[half, side],
                sems.at[half, side],
            )
            for side in range(2)
        ]
        for half in range(2)
    ]


def field_rows(held, y):
    sides = [held.at[y // 8, side].reshape(1024, 128) for side in range(2)]
    return [
        jnp.concatenate(
            [side[pl.ds(x * 8 + y % 8, 32, stride=32), :] for side in sides], axis=1
        )
        for x in range(4)
    ]


def start_all(copies):
    for copy in copies:
        copy.start()


def wait_all(copies):
    for copy in copies:
        copy.wait()


def forward_z(cells_ref, table_ref, out_ref, held, both, ready, sems, done):
    load = pltpu.make_async_copy(table_ref, both, done.at[2])
    load.start()
    copies = field_copies(cells_ref, held, sems)
    start_all(copies[0] + copies[1])
    load.wait()
    results = []
    for half in range(2):
        wait_all(copies[half])
        span = pl.ds(8 * half, 8)
        for y in range(8 * half, 8 * half + 8):
            high, low = split(jnp.concatenate(field_rows(held, y), axis=0))
            wide = mm_nt(both[...], high)
            total = wide[:64] + wide[64:] + mm_nt(both[:64], low)
            ready[:, y] = total.reshape(8, 8, 128)
        results.append(
            pltpu.make_async_copy(ready.at[:, span], out_ref.at[:, span], done.at[half])
        )
        results[-1].start()
    wait_all(results)


def forward_y(data_ref, table_ref, out_ref):
    rows = data_ref.reshape(1024, 128)
    results = []
    for k in range(4):
        parts = [rows[pl.ds(2 * k + part, 128, stride=8), :] for part in range(2)]
        results.append(table_dot(table_ref, jnp.concatenate(parts, axis=0)))
    out = out_ref.reshape(256, 128)
    for x in range(4):
        tile = jnp.concatenate([r[:, 32 * x : 32 * x + 32] for r in results], axis=1)
        for part in range(2):
            out[pl.ds(2 * x + part, 32, stride=8), :] = tile[32 * part : 32 * part + 32]


def middle(
    data_ref, weight_ref, forward_ref, inverse_hbm, out_ref, inverse_ref, sem
):
    load = pltpu.make_async_copy(inverse_hbm, inverse_ref, sem)
    load.start()
    spec = table_dot(forward_ref, data_ref[...].reshape(256, 128))
    spec_re, spec_im = spec[:32], spec[32:]
    lane = lax.broadcasted_iota(jnp.int32, (32, 128), 1)
    group = lane - lax.rem(lane, 32)
    mixed_re = jnp.zeros((32, 128), F32)
    mixed_im = jnp.zeros((32, 128), F32)
    for c in range(32):
        index = group + c
        in_re = jnp.take_along_axis(spec_re, index, axis=1)
        in_im = jnp.take_along_axis(spec_im, index, axis=1)
        w_re, w_im = weight_ref[0, c], weight_ref[1, c]
        mixed_re = mixed_re + (in_re * w_re - in_im * w_im)
        mixed_im = mixed_im + (in_re * w_im + in_im * w_re)
    load.wait()
    back = table_dot(inverse_ref, jnp.concatenate([mixed_re, mixed_im], axis=0))
    out = out_ref.reshape(256, 128)
    for k in range(4):
        tile = jnp.concatenate(
            [back[64 * x : 64 * x + 64, 32 * k : 32 * k + 32] for x in range(4)], axis=1
        )
        for part in range(2):
            out[pl.ds(2 * k + part, 32, stride=8), :] = tile[32 * part : 32 * part + 32]


def inverse_y(data_ref, table_ref, out_ref):
    rows = data_ref.reshape(256, 128)
    out = out_ref.reshape(1024, 128)
    for k in range(4):
        parts = [rows[pl.ds(2 * k + part, 32, stride=8), :] for part in range(2)]
        result = table_dot(table_ref, jnp.concatenate(parts, axis=0))
        for part in range(2):
            out[pl.ds(2 * k + part, 128, stride=8), :] = result[128 * part : 128 * part + 128]


def final(data_ref, base_ref, table_ref, out_ref, held, sems):
    table = jnp.concatenate([table_ref[0], table_ref[0], table_ref[1]], axis=0)
    copies = []
    for half in range(2):
        slots = [held.at[half, side] for side in range(2)]
        rows = [slot.reshape(1024, 128) for slot in slots]
        for y in range(8):
            high, low = split(data_ref[:, 8 * half + y].reshape(64, 128))
            stacked = jnp.concatenate([high, low, high], axis=0)
            spectral = mm_tn(stacked, table)
            for x in range(4):
                value = spectral[32 * x : 32 * x + 32] + base_ref[x, 8 * half + y]
                value = jax.nn.gelu(value)
                for side in range(2):
                    rows[side][pl.ds(x * 8 + y, 32, stride=32), :] = value[
                        :, 128 * side : 128 * side + 128
                    ]
        for side in range(2):
            copy = pltpu.make_async_copy(
                slots[side],
                out_ref.at[:, pl.ds(8 * half, 8), pl.ds(128 * side, 128)],
                sems.at[half, side],
            )
            copy.start()
            copies.append(copy)
    for copy in copies:
        copy.wait()


def weights(data_ref, out_ref, held, sems):
    copies = [
        pltpu.make_async_copy(
            data_ref.at[:, pl.ds(4 * i, 4)], held.at[:, pl.ds(4 * i, 4)], sems.at[i]
        )
        for i in range(8)
    ]
    for copy in copies:
        copy.start()
    rows = out_ref.reshape(2048, 128)
    for i in range(8):
        copies[i].wait()
        for m in range(4 * i, 4 * i + 4):
            for part in range(2):
                tile = jnp.concatenate(
                    [held[part, m, 32 * k : 32 * k + 32, :] for k in range(4)], axis=1
                )
                rows[pl.ds(1024 * part + m, 32, stride=32), :] = tile


def rims(rows_ref, before_ref, after_ref, top_ref, bottom_ref, sems):
    copies = []
    for side, out_ref in enumerate((bottom_ref, top_ref)):
        moves = [
            (rows_ref.at[side], out_ref.at[pl.ds(1, 4)]),
            (before_ref.at[15 * side], out_ref.at[0]),
            (after_ref.at[15 * side], out_ref.at[5]),
        ]
        copies += [
            pltpu.make_async_copy(src, dst, sems.at[side, i]) for i, (src, dst) in enumerate(moves)
        ]
    start_all(copies)
    wait_all(copies)


def shift_sum(sums):
    whole = [jnp.concatenate(pair, axis=1) for pair in sums]
    return whole[1] + pltpu.roll(whole[0], 1, 1) + pltpu.roll(whole[2], 255, 1)


def add_taps(sums, tap_ref, chans, first, load):
    cells = [load(slice(128 * side, 128 * side + 128)) for side in range(2)]
    for e in range(3):
        tap = tap_ref[first + e, chans, :]
        for side in range(2):
            term = tap * cells[side]
            old = sums[e][side]
            sums[e][side] = term if old is None else old + term


def spread_taps(dw_ref, tap_ref):
    rows = jnp.concatenate([dw_ref[a, b] for a in range(3) for b in range(3)], axis=0)
    columns = rows.T
    for i in range(27):
        tap_ref[i] = jnp.broadcast_to(columns[:, i : i + 1], (32, 128))


def own_cells(
    cells_ref, dw_hbm, point_hbm, bias_hbm, out_ref, first_ref, last_ref, rim_ref,
    held, planes, tap_ref, dw_ref, point_ref, bias_ref, sems, small
):
    loads = [
        pltpu.make_async_copy(src, dst, small.at[i])
        for i, (src, dst) in enumerate(
            ((dw_hbm, dw_ref), (point_hbm, point_ref), (bias_hbm, bias_ref))
        )
    ]
    copies = field_copies(cells_ref, held, sems)
    start_all(loads + copies[0] + copies[1])
    wait_all(loads)
    spread_taps(dw_ref, tap_ref)
    channel_map = jnp.concatenate([jnp.concatenate([point_ref[...].T] * 4, axis=1)] * 4, axis=0)
    row = lax.broadcasted_iota(jnp.int32, (128, 128), 0)
    column = lax.broadcasted_iota(jnp.int32, (128, 128), 1)
    same = lax.div(row, 32) == lax.div(column, 32)
    high, low = split(jnp.where(same, channel_map, 0.0))
    point = jnp.concatenate([high, low, high], axis=1)
    bias = jnp.broadcast_to(bias_ref[...], (32, 32)).T[:, :1]
    bias = jnp.concatenate([bias] * 4, axis=0)

    def line(y, shifts):
        high, low = split(planes[:, y].reshape(128, 256))
        value = mm(point, jnp.concatenate([high, high, low], axis=0)) + bias
        for tile in range(4):
            chans = slice(8 * tile, 8 * tile + 8)
            for x in range(4):
                sums = [[None, None] for _ in range(3)]
                for a in range(max(0, 1 - x), min(3, 5 - x)):
                    for b in shifts:
                        load = lambda lanes: planes[x + a - 1, y + b - 1, chans, lanes]
                        add_taps(sums, tap_ref, chans, 9 * a + 3 * b, load)
                own = 32 * x + 8 * tile
                out_ref[x, y, chans, :] = value[own : own + 8] + shift_sum(sums)

    def body(y, carry):
        line(y, (0, 1, 2))
        return carry

    def fill(half):
        wait_all(copies[half])
        for y in range(8 * half, 8 * half + 8):
            for x, part in enumerate(field_rows(held, y)):
                planes[x, y] = part

    fill(0)
    line(0, (1, 2))
    lax.fori_loop(1, 7, body, 0)
    fill(1)
    moves = [
        (planes.at[0], first_ref),
        (planes.at[3], last_ref),
        (planes.at[:, 0], rim_ref.at[0]),
        (planes.at[:, 15], rim_ref.at[1]),
    ]
    results = [
        pltpu.make_async_copy(src, dst, small.at[3 + i]) for i, (src, dst) in enumerate(moves)
    ]
    start_all(results)
    lax.fori_loop(7, 15, body, 0)
    line(15, (0, 1))
    wait_all(results)


def edge_cells(
    base_ref, before_hbm, after_hbm, left_ref, right_ref, dw_hbm,
    out_ref, before_ref, after_ref, tap_ref, dw_ref, sems
):
    moves = [(dw_hbm, dw_ref), (before_hbm, before_ref), (after_hbm, after_ref)]
    copies = [
        pltpu.make_async_copy(src, dst, sems.at[i]) for i, (src, dst) in enumerate(moves)
    ]
    start_all(copies)
    copies[0].wait()
    spread_taps(dw_ref, tap_ref)
    for b, y, source in ((0, 0, left_ref), (2, 15, right_ref)):
        for tile in range(4):
            chans = slice(8 * tile, 8 * tile + 8)
            for x in range(4):
                sums = [[None, None] for _ in range(3)]
                for a in range(max(0, 1 - x), min(3, 5 - x)):
                    load = lambda lanes: source[x + a, chans, lanes]
                    add_taps(sums, tap_ref, chans, 9 * a + 3 * b, load)
                out_ref[x, y, chans, :] = base_ref[x, y, chans, :] + shift_sum(sums)
    wait_all(copies[1:])

    def line(y, before_rows, after_rows):
        for a, x, rows in ((0, 0, before_rows), (2, 3, after_rows)):
            for tile in range(4):
                chans = slice(8 * tile, 8 * tile + 8)
                sums = [[None, None] for _ in range(3)]
                for b in range(3):
                    plane, at = rows[b]
                    load = lambda lanes: plane[at, chans, lanes]
                    add_taps(sums, tap_ref, chans, 9 * a + 3 * b, load)
                out_ref[x, y, chans, :] = out_ref[x, y, chans, :] + shift_sum(sums)

    def near_rows(plane, edge, y):
        low = (left_ref, edge) if y == 0 else (plane, y - 1)
        high = (right_ref, edge) if y == 15 else (plane, y + 1)
        return [low, (plane, y), high]

    def body(y, carry):
        line(y, *([(plane, y + b - 1) for b in range(3)] for plane in (before_ref, after_ref)))
        return carry

    lax.fori_loop(1, 15, body, 0, unroll=2)
    for y in (0, 15):
        line(y, near_rows(before_ref, 0, y), near_rows(after_ref, 5, y))


VMEM = pl.BlockSpec(memory_space=pltpu.VMEM)
ANY = pl.BlockSpec(memory_space=pl.ANY)
HBM = pl.BlockSpec(memory_space=pltpu.HBM)


def call(body, shapes, inputs, microseconds=0, **kw):
    out_shape = [shape if kind is None else kind(shape, F32) for shape, kind in shapes]
    kw.setdefault("in_specs", [VMEM] * inputs)
    kw.setdefault("out_specs", [VMEM] * len(out_shape))
    kw["compiler_params"] = pltpu.CompilerParams(vmem_limit_bytes=16 * 2**20)
    kw["cost_estimate"] = pl.CostEstimate(
        flops=1_000_000_000 * microseconds, transcendentals=0, bytes_accessed=0
    )
    return pl.pallas_call(body, out_shape=out_shape, name=body.__name__, **kw)


def near(value):
    return pltpu.with_memory_space_constraint(value, pltpu.VMEM)


def after_all(value, *others):
    return lax.optimization_barrier((value, *others))[0]


def shifted(axis, value, step):
    count = lax.axis_size(axis)
    return lax.ppermute(value, axis, [(i, (i + step) % count) for i in range(count)])


def exchange(value, axis):
    return lax.all_to_all(value, axis, split_axis=0, concat_axis=0, tiled=True)


def on_device(field, spec_weight, dw_kernel, point_weight, bias):
    tab = {
        name: np.stack(halves(value)) for name, value in tables(32, 128, 128, 256).items()
    }
    plain, kept_near = jax.ShapeDtypeStruct, pltpu.VMEM
    dma = pltpu.SemaphoreType.DMA
    far = functools.partial(pltpu.with_memory_space_constraint, memory_space=pltpu.HBM)
    cells = far(field.reshape(128, 16, 256))
    (zchunks,) = call(
        forward_z,
        [((8, 16, 8, 128), plain)],
        2,
        in_specs=[HBM] * 2,
        out_specs=[ANY],
        scratch_shapes=[
            pltpu.VMEM((2, 2, 128, 8, 128), F32),
            pltpu.VMEM((128, 256), BF16),
            pltpu.VMEM((8, 16, 8, 128), F32),
            dma((2, 2)),
            dma((3,)),
        ],
    )(cells, far(jnp.asarray(tab["fz"].reshape(128, 256))))
    taps = dw_kernel.transpose(1, 2, 3, 0)

    zall = exchange(zchunks, "gy")
    base, first, last, own_rims = call(
        own_cells,
        [
            ((4, 16, 32, 256), kept_near),
            ((16, 32, 256), pltpu.HBM),
            ((16, 32, 256), pltpu.HBM),
            ((2, 4, 32, 256), pltpu.HBM),
        ],
        4,
        8,
        in_specs=[HBM] * 4,
        out_specs=[VMEM] + [HBM] * 3,
        scratch_shapes=[
            pltpu.VMEM((2, 2, 128, 8, 128), F32),
            pltpu.VMEM((4, 16, 32, 256), F32),
            pltpu.VMEM((27, 32, 128), F32),
            pltpu.VMEM((3, 3, 3, 32), F32),
            pltpu.VMEM((32, 32), F32),
            pltpu.VMEM((1, 32), F32),
            dma((2, 2)),
            dma((7,)),
        ],
    )(far(after_all(cells, zchunks)), far(taps), far(point_weight), far(bias.reshape(1, 32)))
    zall, base = lax.optimization_barrier((zall, base))
    (ychunks,) = call(forward_y, [((32, 8, 128), plain)], 2)(
        near(zall), near(jnp.asarray(tab["fy"]))
    )

    yall = exchange(ychunks, "gx")
    (packed,) = call(
        weights,
        [((2, 32, 32, 128), kept_near)],
        1,
        8,
        in_specs=[HBM],
        scratch_shapes=[pltpu.VMEM((2, 32, 128, 32), F32), dma((8,))],
    )(far(after_all(spec_weight, ychunks).reshape(2, 32, 128, 32)))
    first, last, packed = lax.optimization_barrier((first, last, packed))
    before = shifted("gx", far(last), 1)
    after = shifted("gx", far(first), -1)
    yall, packed = lax.optimization_barrier((yall, packed))
    (xchunks,) = call(
        middle,
        [((32, 8, 128), plain)],
        4,
        3,
        in_specs=[VMEM] * 3 + [ANY],
        scratch_shapes=[pltpu.VMEM((2, 256, 64), BF16), dma],
    )(near(yall), near(packed), near(jnp.asarray(tab["fx"])), far(jnp.asarray(tab["ix"])))

    xall = exchange(xchunks, "gx")
    before, after, _ = lax.optimization_barrier((before, after, xchunks))
    before, after = far(before), far(after)
    top, bottom = call(
        rims,
        [((6, 32, 256), kept_near)] * 2,
        3,
        2,
        in_specs=[HBM] * 3,
        scratch_shapes=[dma((2, 3))],
    )(far(own_rims), before, after)
    left = shifted("gy", top, 1)
    right = shifted("gy", bottom, -1)
    xall, top, bottom = lax.optimization_barrier((xall, top, bottom))
    (back,) = call(inverse_y, [((8, 16, 8, 128), plain)], 2)(
        near(xall), near(jnp.asarray(tab["iy"]))
    )

    ball = exchange(back, "gy")
    left, right, _ = lax.optimization_barrier((left, right, back))
    (base,) = call(
        edge_cells,
        [((4, 16, 32, 256), kept_near)],
        6,
        40,
        in_specs=[VMEM] + [ANY] * 2 + [VMEM] * 2 + [ANY],
        scratch_shapes=[
            pltpu.VMEM((16, 32, 256), F32),
            pltpu.VMEM((16, 32, 256), F32),
            pltpu.VMEM((27, 32, 128), F32),
            pltpu.VMEM((3, 3, 3, 32), F32),
            dma((3,)),
        ],
        input_output_aliases={0: 0},
    )(near(base), before, after, near(left), near(right), far(taps))
    ball, base = lax.optimization_barrier((ball, base))
    (out,) = call(
        final,
        [((128, 16, 256), plain)],
        3,
        out_specs=[ANY],
        scratch_shapes=[pltpu.VMEM((2, 2, 128, 8, 128), F32), dma((2, 2))],
    )(near(ball), near(base), near(jnp.asarray(tab["iz"])))
    return out.reshape(field.shape)


def solution(mesh):
    placed = (P(None, "gx", "gy", None), P(None, None, "gx", "gy", None, None), P(), P(), P())
    return jax.shard_map(
        on_device, mesh=mesh, in_specs=placed, out_specs=P(None, "gx", "gy", None), check_vma=False
    )
```

```python
import functools

import jax
import jax.numpy as jnp
import numpy as np
from jax import lax
from jax.experimental import pallas as pl
from jax.experimental.pallas import tpu as pltpu
from jax.sharding import PartitionSpec as P

F32 = jnp.float32
BF16 = jnp.bfloat16


def halves(table):
    high = np.asarray(table, np.float32).astype(BF16)
    low = (np.asarray(table, np.float64) - high.astype(np.float64)).astype(BF16)
    return high, low


def kept(modes, length):
    index = np.arange(modes)
    return np.where(index < modes // 2, index, index + length - modes)


def angles(freqs, length):
    product = np.outer(freqs, np.arange(length)) % length
    turn = 2.0 * np.pi * product / length
    return np.cos(turn), np.sin(turn)


def tables(modes, full_x, full_y, depth):
    zc, zs = angles(np.arange(modes), depth)
    fz = np.stack([zc, -zs], axis=1).reshape(2 * modes, depth)
    weight = np.where(np.arange(modes) == 0, 1.0, 2.0)[:, None] / depth
    iz = np.stack([weight * zc, -weight * zs], axis=1).reshape(2 * modes, depth)
    yc, ys = angles(kept(modes, full_y), full_y)
    fy = np.block([[yc, ys], [-ys, yc]])
    iy = np.block([[yc.T, -ys.T], [ys.T, yc.T]]) / full_y
    xc, xs = angles(kept(modes, full_x), full_x)
    fx = np.concatenate(
        [np.stack([xc, xs], axis=2), np.stack([-xs, xc], axis=2)], axis=0
    ).reshape(2 * modes, 2 * full_x)
    ix = np.stack(
        [np.concatenate([xc.T, -xs.T], axis=1), np.concatenate([xs.T, xc.T], axis=1)]
    ) / full_x
    ix = ix.reshape(2, full_x // 4, 4, 2 * modes).transpose(2, 0, 1, 3)
    ix = ix.reshape(2 * full_x, 2 * modes)
    return {"fz": fz, "iz": iz, "fy": fy, "iy": iy, "fx": fx, "ix": ix}


def split(value):
    high = value.astype(BF16)
    return high, (value - high.astype(F32)).astype(BF16)


def mm(a, b):
    return jnp.dot(a, b, preferred_element_type=F32)


def mm_nt(a, b):
    return lax.dot_general(a, b, (((1,), (1,)), ((), ())), preferred_element_type=F32)


def mm_tn(a, b):
    return lax.dot_general(a, b, (((0,), (0,)), ((), ())), preferred_element_type=F32)


def table_dot(table_ref, data):
    high, low = split(data)
    return mm(table_ref[0], high) + mm(table_ref[0], low) + mm(table_ref[1], high)


def field_copies(cells_ref, held, sems):
    return [
        [
            pltpu.make_async_copy(
                cells_ref.at[:, pl.ds(8 * half, 8), pl.ds(128 * side, 128)],
                held.at[half, side],
                sems.at[half, side],
            )
            for side in range(2)
        ]
        for half in range(2)
    ]


def field_rows(held, y):
    sides = [held.at[y // 8, side].reshape(1024, 128) for side in range(2)]
    return [
        jnp.concatenate(
            [side[pl.ds(x * 8 + y % 8, 32, stride=32), :] for side in sides], axis=1
        )
        for x in range(4)
    ]


def start_all(copies):
    for copy in copies:
        copy.start()


def wait_all(copies):
    for copy in copies:
        copy.wait()


def forward_z(cells_ref, table_ref, out_ref, held, both, ready, sems, done):
    load = pltpu.make_async_copy(table_ref, both, done.at[2])
    load.start()
    copies = field_copies(cells_ref, held, sems)
    start_all(copies[0] + copies[1])
    load.wait()
    results = []
    for half in range(2):
        wait_all(copies[half])
        span = pl.ds(8 * half, 8)
        for y in range(8 * half, 8 * half + 8):
            high, low = split(jnp.concatenate(field_rows(held, y), axis=0))
            wide = mm_nt(both[...], high)
            total = wide[:64] + wide[64:] + mm_nt(both[:64], low)
            ready[:, y] = total.reshape(8, 8, 128)
        results.append(
            pltpu.make_async_copy(ready.at[:, span], out_ref.at[:, span], done.at[half])
        )
        results[-1].start()
    wait_all(results)


def forward_y(data_ref, table_ref, out_ref):
    rows = data_ref.reshape(1024, 128)
    results = []
    for k in range(4):
        parts = [rows[pl.ds(2 * k + part, 128, stride=8), :] for part in range(2)]
        results.append(table_dot(table_ref, jnp.concatenate(parts, axis=0)))
    out = out_ref.reshape(256, 128)
    for x in range(4):
        tile = jnp.concatenate([r[:, 32 * x : 32 * x + 32] for r in results], axis=1)
        for part in range(2):
            out[pl.ds(2 * x + part, 32, stride=8), :] = tile[32 * part : 32 * part + 32]


def middle(
    data_ref, weight_ref, forward_ref, inverse_hbm, out_ref, inverse_ref, sem
):
    load = pltpu.make_async_copy(inverse_hbm, inverse_ref, sem)
    load.start()
    spec = table_dot(forward_ref, data_ref[...].reshape(256, 128))
    spec_re, spec_im = spec[:32], spec[32:]
    lane = lax.broadcasted_iota(jnp.int32, (32, 128), 1)
    group = lane - lax.rem(lane, 32)
    mixed_re = jnp.zeros((32, 128), F32)
    mixed_im = jnp.zeros((32, 128), F32)
    for c in range(32):
        index = group + c
        in_re = jnp.take_along_axis(spec_re, index, axis=1)
        in_im = jnp.take_along_axis(spec_im, index, axis=1)
        w_re, w_im = weight_ref[0, c], weight_ref[1, c]
        mixed_re = mixed_re + (in_re * w_re - in_im * w_im)
        mixed_im = mixed_im + (in_re * w_im + in_im * w_re)
    load.wait()
    back = table_dot(inverse_ref, jnp.concatenate([mixed_re, mixed_im], axis=0))
    out = out_ref.reshape(256, 128)
    for k in range(4):
        tile = jnp.concatenate(
            [back[64 * x : 64 * x + 64, 32 * k : 32 * k + 32] for x in range(4)], axis=1
        )
        for part in range(2):
            out[pl.ds(2 * k + part, 32, stride=8), :] = tile[32 * part : 32 * part + 32]


def inverse_y(data_ref, table_ref, out_ref):
    rows = data_ref.reshape(256, 128)
    out = out_ref.reshape(1024, 128)
    for k in range(4):
        parts = [rows[pl.ds(2 * k + part, 32, stride=8), :] for part in range(2)]
        result = table_dot(table_ref, jnp.concatenate(parts, axis=0))
        for part in range(2):
            out[pl.ds(2 * k + part, 128, stride=8), :] = result[128 * part : 128 * part + 128]


def final(data_ref, base_ref, table_ref, out_ref, held, sems):
    table = jnp.concatenate([table_ref[0], table_ref[0], table_ref[1]], axis=0)
    copies = []
    for half in range(2):
        slots = [held.at[half, side] for side in range(2)]
        rows = [slot.reshape(1024, 128) for slot in slots]
        for y in range(8):
            high, low = split(data_ref[:, 8 * half + y].reshape(64, 128))
            stacked = jnp.concatenate([high, low, high], axis=0)
            spectral = mm_tn(stacked, table)
            for x in range(4):
                value = spectral[32 * x : 32 * x + 32] + base_ref[x, 8 * half + y]
                value = jax.nn.gelu(value)
                for side in range(2):
                    rows[side][pl.ds(x * 8 + y, 32, stride=32), :] = value[
                        :, 128 * side : 128 * side + 128
                    ]
        for side in range(2):
            copy = pltpu.make_async_copy(
                slots[side],
                out_ref.at[:, pl.ds(8 * half, 8), pl.ds(128 * side, 128)],
                sems.at[half, side],
            )
            copy.start()
            copies.append(copy)
    for copy in copies:
        copy.wait()


def weights(data_ref, out_ref, held, sems):
    copies = [
        pltpu.make_async_copy(
            data_ref.at[:, pl.ds(4 * i, 4)], held.at[:, pl.ds(4 * i, 4)], sems.at[i]
        )
        for i in range(8)
    ]
    for copy in copies:
        copy.start()
    rows = out_ref.reshape(2048, 128)
    for i in range(8):
        copies[i].wait()
        for m in range(4 * i, 4 * i + 4):
            for part in range(2):
                tile = jnp.concatenate(
                    [held[part, m, 32 * k : 32 * k + 32, :] for k in range(4)], axis=1
                )
                rows[pl.ds(1024 * part + m, 32, stride=32), :] = tile


def rims(rows_ref, before_ref, after_ref, top_ref, bottom_ref, sems):
    copies = []
    for side, out_ref in enumerate((bottom_ref, top_ref)):
        moves = [
            (rows_ref.at[side], out_ref.at[pl.ds(1, 4)]),
            (before_ref.at[15 * side], out_ref.at[0]),
            (after_ref.at[15 * side], out_ref.at[5]),
        ]
        copies += [
            pltpu.make_async_copy(src, dst, sems.at[side, i]) for i, (src, dst) in enumerate(moves)
        ]
    start_all(copies)
    wait_all(copies)


def shift_sum(sums):
    whole = [jnp.concatenate(pair, axis=1) for pair in sums]
    return whole[1] + pltpu.roll(whole[0], 1, 1) + pltpu.roll(whole[2], 255, 1)


def add_taps(sums, tap_ref, chans, first, load):
    cells = [load(slice(128 * side, 128 * side + 128)) for side in range(2)]
    for e in range(3):
        tap = tap_ref[first + e, chans, :]
        for side in range(2):
            term = tap * cells[side]
            old = sums[e][side]
            sums[e][side] = term if old is None else old + term


def spread_taps(dw_ref, tap_ref):
    rows = jnp.concatenate([dw_ref[a, b] for a in range(3) for b in range(3)], axis=0)
    columns = rows.T
    for i in range(27):
        tap_ref[i] = jnp.broadcast_to(columns[:, i : i + 1], (32, 128))


def own_cells(
    cells_ref, dw_hbm, point_hbm, bias_hbm, out_ref, first_ref, third_ref, last_ref, rim_ref,
    held, planes, tap_ref, dw_ref, point_ref, bias_ref, sems, small
):
    loads = [
        pltpu.make_async_copy(src, dst, small.at[i])
        for i, (src, dst) in enumerate(
            ((dw_hbm, dw_ref), (point_hbm, point_ref), (bias_hbm, bias_ref))
        )
    ]
    copies = field_copies(cells_ref, held, sems)
    start_all(loads + copies[0] + copies[1])
    wait_all(loads)
    spread_taps(dw_ref, tap_ref)
    channel_map = jnp.concatenate([jnp.concatenate([point_ref[...].T] * 4, axis=1)] * 4, axis=0)
    row = lax.broadcasted_iota(jnp.int32, (128, 128), 0)
    column = lax.broadcasted_iota(jnp.int32, (128, 128), 1)
    same = lax.div(row, 32) == lax.div(column, 32)
    high, low = split(jnp.where(same, channel_map, 0.0))
    point = jnp.concatenate([high, low, high], axis=1)
    bias = jnp.broadcast_to(bias_ref[...], (32, 32)).T[:, :1]
    bias = jnp.concatenate([bias] * 4, axis=0)

    def line(y, shifts):
        high, low = split(planes[:, y].reshape(128, 256))
        value = mm(point, jnp.concatenate([high, high, low], axis=0)) + bias
        for tile in range(4):
            chans = slice(8 * tile, 8 * tile + 8)
            for x in range(3):
                sums = [[None, None] for _ in range(3)]
                for a in range(max(0, 1 - x), 3):
                    for b in shifts:
                        load = lambda lanes: planes[x + a - 1, y + b - 1, chans, lanes]
                        add_taps(sums, tap_ref, chans, 9 * a + 3 * b, load)
                own = 32 * x + 8 * tile
                out_ref[x, y, chans, :] = value[own : own + 8] + shift_sum(sums)
        out_ref[3, y] = value[96:]

    def body(y, carry):
        line(y, (0, 1, 2))
        return carry

    def fill(half):
        wait_all(copies[half])
        for y in range(8 * half, 8 * half + 8):
            for x, part in enumerate(field_rows(held, y)):
                planes[x, y] = part

    fill(0)
    line(0, (1, 2))
    lax.fori_loop(1, 7, body, 0)
    fill(1)
    moves = [
        (planes.at[0], first_ref),
        (planes.at[2], third_ref),
        (planes.at[3], last_ref),
        (planes.at[:, 0], rim_ref.at[0]),
        (planes.at[:, 15], rim_ref.at[1]),
    ]
    results = [
        pltpu.make_async_copy(src, dst, small.at[3 + i]) for i, (src, dst) in enumerate(moves)
    ]
    start_all(results)
    lax.fori_loop(7, 15, body, 0)
    line(15, (0, 1))
    wait_all(results)


def edge_cells(
    base_ref, before_hbm, third_hbm, last_hbm, after_hbm, left_ref, right_ref, dw_hbm,
    out_ref, before_ref, third_ref, last_ref, after_ref, tap_ref, dw_ref, sems
):
    moves = [
        (dw_hbm, dw_ref),
        (before_hbm, before_ref),
        (third_hbm, third_ref),
        (last_hbm, last_ref),
        (after_hbm, after_ref),
    ]
    copies = [
        pltpu.make_async_copy(src, dst, sems.at[i]) for i, (src, dst) in enumerate(moves)
    ]
    start_all(copies)
    copies[0].wait()
    spread_taps(dw_ref, tap_ref)
    for b, y, source in ((0, 0, left_ref), (2, 15, right_ref)):
        for tile in range(4):
            chans = slice(8 * tile, 8 * tile + 8)
            for x in range(4):
                sums = [[None, None] for _ in range(3)]
                for a in range(max(0, 1 - x), min(3, 5 - x)):
                    load = lambda lanes: source[x + a, chans, lanes]
                    add_taps(sums, tap_ref, chans, 9 * a + 3 * b, load)
                out_ref[x, y, chans, :] = base_ref[x, y, chans, :] + shift_sum(sums)
    wait_all(copies[1:])

    def line(y, before_rows, after_rows, shifts):
        for a, x, rows in ((0, 0, before_rows), (2, 3, after_rows)):
            for tile in range(4):
                chans = slice(8 * tile, 8 * tile + 8)
                sums = [[None, None] for _ in range(3)]
                for b in range(3):
                    plane, at = rows[b]
                    load = lambda lanes: plane[at, chans, lanes]
                    add_taps(sums, tap_ref, chans, 9 * a + 3 * b, load)
                for own, plane in enumerate((third_ref, last_ref) if x == 3 else ()):
                    for b in shifts:
                        load = lambda lanes: plane[y + b - 1, chans, lanes]
                        add_taps(sums, tap_ref, chans, 9 * own + 3 * b, load)
                out_ref[x, y, chans, :] = out_ref[x, y, chans, :] + shift_sum(sums)

    def near_rows(plane, edge, y):
        low = (left_ref, edge) if y == 0 else (plane, y - 1)
        high = (right_ref, edge) if y == 15 else (plane, y + 1)
        return [low, (plane, y), high]

    def body(y, carry):
        rows = [[(plane, y + b - 1) for b in range(3)] for plane in (before_ref, after_ref)]
        line(y, *rows, (0, 1, 2))
        return carry

    lax.fori_loop(1, 15, body, 0, unroll=2)
    for y, shifts in ((0, (1, 2)), (15, (0, 1))):
        line(y, near_rows(before_ref, 0, y), near_rows(after_ref, 5, y), shifts)


VMEM = pl.BlockSpec(memory_space=pltpu.VMEM)
ANY = pl.BlockSpec(memory_space=pl.ANY)
HBM = pl.BlockSpec(memory_space=pltpu.HBM)


def call(body, shapes, inputs, microseconds=0, **kw):
    out_shape = [shape if kind is None else kind(shape, F32) for shape, kind in shapes]
    kw.setdefault("in_specs", [VMEM] * inputs)
    kw.setdefault("out_specs", [VMEM] * len(out_shape))
    kw["compiler_params"] = pltpu.CompilerParams(vmem_limit_bytes=16 * 2**20)
    kw["cost_estimate"] = pl.CostEstimate(
        flops=1_000_000_000 * microseconds, transcendentals=0, bytes_accessed=0
    )
    return pl.pallas_call(body, out_shape=out_shape, name=body.__name__, **kw)


def near(value):
    return pltpu.with_memory_space_constraint(value, pltpu.VMEM)


def after_all(value, *others):
    return lax.optimization_barrier((value, *others))[0]


def shifted(axis, value, step):
    count = lax.axis_size(axis)
    return lax.ppermute(value, axis, [(i, (i + step) % count) for i in range(count)])


def exchange(value, axis):
    return lax.all_to_all(value, axis, split_axis=0, concat_axis=0, tiled=True)


def on_device(field, spec_weight, dw_kernel, point_weight, bias):
    tab = {
        name: np.stack(halves(value)) for name, value in tables(32, 128, 128, 256).items()
    }
    plain, kept_near = jax.ShapeDtypeStruct, pltpu.VMEM
    dma = pltpu.SemaphoreType.DMA
    far = functools.partial(pltpu.with_memory_space_constraint, memory_space=pltpu.HBM)
    cells = far(field.reshape(128, 16, 256))
    (zchunks,) = call(
        forward_z,
        [((8, 16, 8, 128), plain)],
        2,
        in_specs=[HBM] * 2,
        out_specs=[ANY],
        scratch_shapes=[
            pltpu.VMEM((2, 2, 128, 8, 128), F32),
            pltpu.VMEM((128, 256), BF16),
            pltpu.VMEM((8, 16, 8, 128), F32),
            dma((2, 2)),
            dma((3,)),
        ],
    )(cells, far(jnp.asarray(tab["fz"].reshape(128, 256))))
    taps = dw_kernel.transpose(1, 2, 3, 0)

    zall = exchange(zchunks, "gy")
    base, first, third, last, own_rims = call(
        own_cells,
        [
            ((4, 16, 32, 256), kept_near),
            ((16, 32, 256), pltpu.HBM),
            ((16, 32, 256), pltpu.HBM),
            ((16, 32, 256), pltpu.HBM),
            ((2, 4, 32, 256), pltpu.HBM),
        ],
        4,
        8,
        in_specs=[HBM] * 4,
        out_specs=[VMEM] + [HBM] * 4,
        scratch_shapes=[
            pltpu.VMEM((2, 2, 128, 8, 128), F32),
            pltpu.VMEM((4, 16, 32, 256), F32),
            pltpu.VMEM((27, 32, 128), F32),
            pltpu.VMEM((3, 3, 3, 32), F32),
            pltpu.VMEM((32, 32), F32),
            pltpu.VMEM((1, 32), F32),
            dma((2, 2)),
            dma((8,)),
        ],
    )(far(after_all(cells, zchunks)), far(taps), far(point_weight), far(bias.reshape(1, 32)))
    zall, base = lax.optimization_barrier((zall, base))
    (ychunks,) = call(forward_y, [((32, 8, 128), plain)], 2)(
        near(zall), near(jnp.asarray(tab["fy"]))
    )

    yall = exchange(ychunks, "gx")
    (packed,) = call(
        weights,
        [((2, 32, 32, 128), kept_near)],
        1,
        8,
        in_specs=[HBM],
        scratch_shapes=[pltpu.VMEM((2, 32, 128, 32), F32), dma((8,))],
    )(far(after_all(spec_weight, ychunks).reshape(2, 32, 128, 32)))
    first, last, packed = lax.optimization_barrier((first, last, packed))
    before = shifted("gx", far(last), 1)
    after = shifted("gx", far(first), -1)
    yall, packed = lax.optimization_barrier((yall, packed))
    (xchunks,) = call(
        middle,
        [((32, 8, 128), plain)],
        4,
        3,
        in_specs=[VMEM] * 3 + [ANY],
        scratch_shapes=[pltpu.VMEM((2, 256, 64), BF16), dma],
    )(near(yall), near(packed), near(jnp.asarray(tab["fx"])), far(jnp.asarray(tab["ix"])))

    xall = exchange(xchunks, "gx")
    before, after, _ = lax.optimization_barrier((before, after, xchunks))
    before, after = far(before), far(after)
    top, bottom = call(
        rims,
        [((6, 32, 256), kept_near)] * 2,
        3,
        2,
        in_specs=[HBM] * 3,
        scratch_shapes=[dma((2, 3))],
    )(far(own_rims), before, after)
    left = shifted("gy", top, 1)
    right = shifted("gy", bottom, -1)
    xall, top, bottom = lax.optimization_barrier((xall, top, bottom))
    (back,) = call(inverse_y, [((8, 16, 8, 128), plain)], 2)(
        near(xall), near(jnp.asarray(tab["iy"]))
    )

    ball = exchange(back, "gy")
    left, right, _ = lax.optimization_barrier((left, right, back))
    (base,) = call(
        edge_cells,
        [((4, 16, 32, 256), kept_near)],
        8,
        40,
        in_specs=[VMEM] + [ANY] * 4 + [VMEM] * 2 + [ANY],
        scratch_shapes=[pltpu.VMEM((16, 32, 256), F32)] * 4
        + [pltpu.VMEM((27, 32, 128), F32), pltpu.VMEM((3, 3, 3, 32), F32), dma((5,))],
        input_output_aliases={0: 0},
    )(
        near(base), before, far(third), far(last), after, near(left), near(right), far(taps)
    )
    ball, base = lax.optimization_barrier((ball, base))
    (out,) = call(
        final,
        [((128, 16, 256), plain)],
        3,
        out_specs=[ANY],
        scratch_shapes=[pltpu.VMEM((2, 2, 128, 8, 128), F32), dma((2, 2))],
    )(near(ball), near(base), near(jnp.asarray(tab["iz"])))
    return out.reshape(field.shape)


def solution(mesh):
    placed = (P(None, "gx", "gy", None), P(None, None, "gx", "gy", None, None), P(), P(), P())
    return jax.shard_map(
        on_device, mesh=mesh, in_specs=placed, out_specs=P(None, "gx", "gy", None), check_vma=False
    )
```

```python
import functools

import jax
import jax.numpy as jnp
import numpy as np
from jax import lax
from jax.experimental import pallas as pl
from jax.experimental.pallas import tpu as pltpu
from jax.sharding import PartitionSpec as P

F32 = jnp.float32
BF16 = jnp.bfloat16


def halves(table):
    high = np.asarray(table, np.float32).astype(BF16)
    low = (np.asarray(table, np.float64) - high.astype(np.float64)).astype(BF16)
    return high, low


def kept(modes, length):
    index = np.arange(modes)
    return np.where(index < modes // 2, index, index + length - modes)


def angles(freqs, length):
    product = np.outer(freqs, np.arange(length)) % length
    turn = 2.0 * np.pi * product / length
    return np.cos(turn), np.sin(turn)


def tables(modes, full_x, full_y, depth):
    zc, zs = angles(np.arange(modes), depth)
    fz = np.stack([zc, -zs], axis=1).reshape(2 * modes, depth)
    weight = np.where(np.arange(modes) == 0, 1.0, 2.0)[:, None] / depth
    iz = np.stack([weight * zc, -weight * zs], axis=1).reshape(2 * modes, depth)
    yc, ys = angles(kept(modes, full_y), full_y)
    fy = np.block([[yc, ys], [-ys, yc]])
    iy = np.block([[yc.T, -ys.T], [ys.T, yc.T]]) / full_y
    xc, xs = angles(kept(modes, full_x), full_x)
    fx = np.concatenate(
        [np.stack([xc, xs], axis=2), np.stack([-xs, xc], axis=2)], axis=0
    ).reshape(2 * modes, 2 * full_x)
    ix = np.stack(
        [np.concatenate([xc.T, -xs.T], axis=1), np.concatenate([xs.T, xc.T], axis=1)]
    ) / full_x
    ix = ix.reshape(2, full_x // 4, 4, 2 * modes).transpose(2, 0, 1, 3)
    ix = ix.reshape(2 * full_x, 2 * modes)
    return {"fz": fz, "iz": iz, "fy": fy, "iy": iy, "fx": fx, "ix": ix}


def split(value):
    high = value.astype(BF16)
    return high, (value - high.astype(F32)).astype(BF16)


def mm(a, b):
    return jnp.dot(a, b, preferred_element_type=F32)


def mm_nt(a, b):
    return lax.dot_general(a, b, (((1,), (1,)), ((), ())), preferred_element_type=F32)


def mm_tn(a, b):
    return lax.dot_general(a, b, (((0,), (0,)), ((), ())), preferred_element_type=F32)


def table_dot(table_ref, data):
    high, low = split(data)
    return mm(table_ref[0], high) + mm(table_ref[0], low) + mm(table_ref[1], high)


def field_copies(cells_ref, held, sems):
    return [
        [
            pltpu.make_async_copy(
                cells_ref.at[:, pl.ds(8 * half, 8), pl.ds(128 * side, 128)],
                held.at[half, side],
                sems.at[half, side],
            )
            for side in range(2)
        ]
        for half in range(2)
    ]


def field_rows(held, y):
    sides = [held.at[y // 8, side].reshape(1024, 128) for side in range(2)]
    return [
        jnp.concatenate(
            [side[pl.ds(x * 8 + y % 8, 32, stride=32), :] for side in sides], axis=1
        )
        for x in range(4)
    ]


def start_all(copies):
    for copy in copies:
        copy.start()


def wait_all(copies):
    for copy in copies:
        copy.wait()


def forward_z(cells_ref, table_ref, out_ref, held, both, ready, sems, done):
    load = pltpu.make_async_copy(table_ref, both, done.at[2])
    load.start()
    copies = field_copies(cells_ref, held, sems)
    start_all(copies[0] + copies[1])
    load.wait()
    results = []
    for half in range(2):
        wait_all(copies[half])
        span = pl.ds(8 * half, 8)
        for y in range(8 * half, 8 * half + 8):
            high, low = split(jnp.concatenate(field_rows(held, y), axis=0))
            wide = mm_nt(both[...], high)
            total = wide[:64] + wide[64:] + mm_nt(both[:64], low)
            ready[:, y] = total.reshape(8, 8, 128)
        results.append(
            pltpu.make_async_copy(ready.at[:, span], out_ref.at[:, span], done.at[half])
        )
        results[-1].start()
    wait_all(results)


def forward_y(data_ref, table_ref, out_ref):
    rows = data_ref.reshape(1024, 128)
    results = []
    for k in range(4):
        parts = [rows[pl.ds(2 * k + part, 128, stride=8), :] for part in range(2)]
        results.append(table_dot(table_ref, jnp.concatenate(parts, axis=0)))
    out = out_ref.reshape(256, 128)
    for x in range(4):
        tile = jnp.concatenate([r[:, 32 * x : 32 * x + 32] for r in results], axis=1)
        for part in range(2):
            out[pl.ds(2 * x + part, 32, stride=8), :] = tile[32 * part : 32 * part + 32]


def middle(
    data_ref, weight_ref, forward_ref, inverse_hbm, out_ref, inverse_ref, sem
):
    load = pltpu.make_async_copy(inverse_hbm, inverse_ref, sem)
    load.start()
    spec = table_dot(forward_ref, data_ref[...].reshape(256, 128))
    spec_re, spec_im = spec[:32], spec[32:]
    lane = lax.broadcasted_iota(jnp.int32, (32, 128), 1)
    group = lane - lax.rem(lane, 32)
    mixed_re = jnp.zeros((32, 128), F32)
    mixed_im = jnp.zeros((32, 128), F32)
    for c in range(32):
        index = group + c
        in_re = jnp.take_along_axis(spec_re, index, axis=1)
        in_im = jnp.take_along_axis(spec_im, index, axis=1)
        w_re, w_im = weight_ref[0, c], weight_ref[1, c]
        mixed_re = mixed_re + (in_re * w_re - in_im * w_im)
        mixed_im = mixed_im + (in_re * w_im + in_im * w_re)
    load.wait()
    back = table_dot(inverse_ref, jnp.concatenate([mixed_re, mixed_im], axis=0))
    out = out_ref.reshape(256, 128)
    for k in range(4):
        tile = jnp.concatenate(
            [back[64 * x : 64 * x + 64, 32 * k : 32 * k + 32] for x in range(4)], axis=1
        )
        for part in range(2):
            out[pl.ds(2 * k + part, 32, stride=8), :] = tile[32 * part : 32 * part + 32]


def inverse_y(data_ref, table_ref, out_ref):
    rows = data_ref.reshape(256, 128)
    out = out_ref.reshape(1024, 128)
    for k in range(4):
        parts = [rows[pl.ds(2 * k + part, 32, stride=8), :] for part in range(2)]
        result = table_dot(table_ref, jnp.concatenate(parts, axis=0))
        for part in range(2):
            out[pl.ds(2 * k + part, 128, stride=8), :] = result[128 * part : 128 * part + 128]


def final(data_ref, base_ref, table_ref, out_ref, held, sems):
    table = jnp.concatenate([table_ref[0], table_ref[0], table_ref[1]], axis=0)
    copies = []
    for half in range(2):
        slots = [held.at[half, side] for side in range(2)]
        rows = [slot.reshape(1024, 128) for slot in slots]
        for y in range(8):
            high, low = split(data_ref[:, 8 * half + y].reshape(64, 128))
            stacked = jnp.concatenate([high, low, high], axis=0)
            spectral = mm_tn(stacked, table)
            for x in range(4):
                value = spectral[32 * x : 32 * x + 32] + base_ref[x, 8 * half + y]
                value = jax.nn.gelu(value)
                for side in range(2):
                    rows[side][pl.ds(x * 8 + y, 32, stride=32), :] = value[
                        :, 128 * side : 128 * side + 128
                    ]
        for side in range(2):
            copy = pltpu.make_async_copy(
                slots[side],
                out_ref.at[:, pl.ds(8 * half, 8), pl.ds(128 * side, 128)],
                sems.at[half, side],
            )
            copy.start()
            copies.append(copy)
    for copy in copies:
        copy.wait()


def weights(data_ref, out_ref, held, sems):
    copies = [
        pltpu.make_async_copy(
            data_ref.at[:, pl.ds(4 * i, 4)], held.at[:, pl.ds(4 * i, 4)], sems.at[i]
        )
        for i in range(8)
    ]
    for copy in copies:
        copy.start()
    rows = out_ref.reshape(2048, 128)
    for i in range(8):
        copies[i].wait()
        for m in range(4 * i, 4 * i + 4):
            for part in range(2):
                tile = jnp.concatenate(
                    [held[part, m, 32 * k : 32 * k + 32, :] for k in range(4)], axis=1
                )
                rows[pl.ds(1024 * part + m, 32, stride=32), :] = tile


def rims(rows_ref, before_ref, after_ref, top_ref, bottom_ref, sems):
    copies = []
    for side, out_ref in enumerate((bottom_ref, top_ref)):
        moves = [
            (rows_ref.at[side], out_ref.at[pl.ds(1, 4)]),
            (before_ref.at[15 * side], out_ref.at[0]),
            (after_ref.at[15 * side], out_ref.at[5]),
        ]
        copies += [
            pltpu.make_async_copy(src, dst, sems.at[side, i]) for i, (src, dst) in enumerate(moves)
        ]
    start_all(copies)
    wait_all(copies)


def shift_sum(sums):
    whole = [jnp.concatenate(pair, axis=1) for pair in sums]
    return whole[1] + pltpu.roll(whole[0], 1, 1) + pltpu.roll(whole[2], 255, 1)


def add_taps(sums, tap_ref, chans, first, load):
    cells = [load(slice(128 * side, 128 * side + 128)) for side in range(2)]
    for e in range(3):
        tap = tap_ref[first + e, chans, :]
        for side in range(2):
            term = tap * cells[side]
            old = sums[e][side]
            sums[e][side] = term if old is None else old + term


def spread_taps(dw_ref, tap_ref):
    rows = jnp.concatenate([dw_ref[a, b] for a in range(3) for b in range(3)], axis=0)
    columns = rows.T
    for i in range(27):
        tap_ref[i] = jnp.broadcast_to(columns[:, i : i + 1], (32, 128))


def own_cells(
    cells_ref, dw_hbm, point_hbm, bias_hbm, out_ref, first_ref, third_ref, last_ref, rim_ref,
    held, planes, tap_ref, dw_ref, point_ref, bias_ref, sems, small
):
    loads = [
        pltpu.make_async_copy(src, dst, small.at[i])
        for i, (src, dst) in enumerate(
            ((dw_hbm, dw_ref), (point_hbm, point_ref), (bias_hbm, bias_ref))
        )
    ]
    copies = field_copies(cells_ref, held, sems)
    start_all(loads + copies[0] + copies[1])
    wait_all(loads)
    spread_taps(dw_ref, tap_ref)
    channel_map = jnp.concatenate([jnp.concatenate([point_ref[...].T] * 4, axis=1)] * 4, axis=0)
    row = lax.broadcasted_iota(jnp.int32, (128, 128), 0)
    column = lax.broadcasted_iota(jnp.int32, (128, 128), 1)
    same = lax.div(row, 32) == lax.div(column, 32)
    high, low = split(jnp.where(same, channel_map, 0.0))
    point = jnp.concatenate([high, low, high], axis=1)
    bias = jnp.broadcast_to(bias_ref[...], (32, 32)).T[:, :1]
    bias = jnp.concatenate([bias] * 4, axis=0)

    def line(y, shifts):
        high, low = split(planes[:, y].reshape(128, 256))
        value = mm(point, jnp.concatenate([high, high, low], axis=0)) + bias
        for tile in range(4):
            chans = slice(8 * tile, 8 * tile + 8)
            for x in range(3):
                sums = [[None, None] for _ in range(3)]
                for a in range(max(0, 1 - x), 3):
                    for b in shifts:
                        load = lambda lanes: planes[x + a - 1, y + b - 1, chans, lanes]
                        add_taps(sums, tap_ref, chans, 9 * a + 3 * b, load)
                own = 32 * x + 8 * tile
                out_ref[x, y, chans, :] = value[own : own + 8] + shift_sum(sums)
        out_ref[3, y] = value[96:]

    def body(y, carry):
        line(y, (0, 1, 2))
        return carry

    def fill(half):
        wait_all(copies[half])
        for y in range(8 * half, 8 * half + 8):
            for x, part in enumerate(field_rows(held, y)):
                planes[x, y] = part

    fill(0)
    line(0, (1, 2))
    lax.fori_loop(1, 7, body, 0)
    fill(1)
    moves = [
        (planes.at[0], first_ref),
        (planes.at[2], third_ref),
        (planes.at[3], last_ref),
        (planes.at[:, 0], rim_ref.at[0]),
        (planes.at[:, 15], rim_ref.at[1]),
    ]
    results = [
        pltpu.make_async_copy(src, dst, small.at[3 + i]) for i, (src, dst) in enumerate(moves)
    ]
    start_all(results)
    lax.fori_loop(7, 15, body, 0)
    line(15, (0, 1))
    wait_all(results)


def edge_cells(
    base_ref, before_hbm, third_hbm, last_hbm, after_hbm, left_ref, right_ref, dw_hbm,
    out_ref, before_ref, third_ref, last_ref, after_ref, tap_ref, dw_ref, sems
):
    moves = [
        (dw_hbm, dw_ref),
        (before_hbm, before_ref),
        (third_hbm, third_ref),
        (last_hbm, last_ref),
        (after_hbm, after_ref),
    ]
    copies = [
        pltpu.make_async_copy(src, dst, sems.at[i]) for i, (src, dst) in enumerate(moves)
    ]
    start_all(copies)
    copies[0].wait()
    spread_taps(dw_ref, tap_ref)
    for b, y, source in ((0, 0, left_ref), (2, 15, right_ref)):
        for tile in range(4):
            chans = slice(8 * tile, 8 * tile + 8)
            for x in range(4):
                sums = [[None, None] for _ in range(3)]
                for a in range(max(0, 1 - x), min(3, 5 - x)):
                    load = lambda lanes: source[x + a, chans, lanes]
                    add_taps(sums, tap_ref, chans, 9 * a + 3 * b, load)
                out_ref[x, y, chans, :] = base_ref[x, y, chans, :] + shift_sum(sums)
    wait_all(copies[1:])

    def line(y, before_rows, after_rows, shifts):
        for a, x, rows in ((0, 0, before_rows), (2, 3, after_rows)):
            for tile in range(4):
                chans = slice(8 * tile, 8 * tile + 8)
                sums = [[None, None] for _ in range(3)]
                for b in range(3):
                    plane, at = rows[b]
                    load = lambda lanes: plane[at, chans, lanes]
                    add_taps(sums, tap_ref, chans, 9 * a + 3 * b, load)
                for own, plane in enumerate((third_ref, last_ref) if x == 3 else ()):
                    for b in shifts:
                        load = lambda lanes: plane[y + b - 1, chans, lanes]
                        add_taps(sums, tap_ref, chans, 9 * own + 3 * b, load)
                out_ref[x, y, chans, :] = out_ref[x, y, chans, :] + shift_sum(sums)

    def near_rows(plane, edge, y):
        low = (left_ref, edge) if y == 0 else (plane, y - 1)
        high = (right_ref, edge) if y == 15 else (plane, y + 1)
        return [low, (plane, y), high]

    def body(y, carry):
        rows = [[(plane, y + b - 1) for b in range(3)] for plane in (before_ref, after_ref)]
        line(y, *rows, (0, 1, 2))
        return carry

    lax.fori_loop(1, 15, body, 0, unroll=2)
    for y, shifts in ((0, (1, 2)), (15, (0, 1))):
        line(y, near_rows(before_ref, 0, y), near_rows(after_ref, 5, y), shifts)


VMEM = pl.BlockSpec(memory_space=pltpu.VMEM)
ANY = pl.BlockSpec(memory_space=pl.ANY)
HBM = pl.BlockSpec(memory_space=pltpu.HBM)


def call(body, shapes, inputs, microseconds=0, **kw):
    out_shape = [shape if kind is None else kind(shape, F32) for shape, kind in shapes]
    kw.setdefault("in_specs", [VMEM] * inputs)
    kw.setdefault("out_specs", [VMEM] * len(out_shape))
    kw["compiler_params"] = pltpu.CompilerParams(vmem_limit_bytes=16 * 2**20)
    kw["cost_estimate"] = pl.CostEstimate(
        flops=1_000_000_000 * microseconds, transcendentals=0, bytes_accessed=0
    )
    return pl.pallas_call(body, out_shape=out_shape, name=body.__name__, **kw)


def near(value):
    return pltpu.with_memory_space_constraint(value, pltpu.VMEM)


def after_all(value, *others):
    return lax.optimization_barrier((value, *others))[0]


def shifted(axis, value, step):
    count = lax.axis_size(axis)
    return lax.ppermute(value, axis, [(i, (i + step) % count) for i in range(count)])


def exchange(value, axis):
    return lax.all_to_all(value, axis, split_axis=0, concat_axis=0, tiled=True)


def on_device(field, spec_weight, dw_kernel, point_weight, bias):
    tab = {
        name: np.stack(halves(value)) for name, value in tables(32, 128, 128, 256).items()
    }
    plain, kept_near = jax.ShapeDtypeStruct, pltpu.VMEM
    dma = pltpu.SemaphoreType.DMA
    far = functools.partial(pltpu.with_memory_space_constraint, memory_space=pltpu.HBM)
    cells = far(field.reshape(128, 16, 256))
    (zchunks,) = call(
        forward_z,
        [((8, 16, 8, 128), plain)],
        2,
        in_specs=[HBM] * 2,
        out_specs=[ANY],
        scratch_shapes=[
            pltpu.VMEM((2, 2, 128, 8, 128), F32),
            pltpu.VMEM((128, 256), BF16),
            pltpu.VMEM((8, 16, 8, 128), F32),
            dma((2, 2)),
            dma((3,)),
        ],
    )(cells, far(jnp.asarray(tab["fz"].reshape(128, 256))))
    taps = dw_kernel.transpose(1, 2, 3, 0)

    zall = exchange(zchunks, "gy")
    base, first, third, last, own_rims = call(
        own_cells,
        [
            ((4, 16, 32, 256), kept_near),
            ((16, 32, 256), pltpu.HBM),
            ((16, 32, 256), pltpu.HBM),
            ((16, 32, 256), pltpu.HBM),
            ((2, 4, 32, 256), pltpu.HBM),
        ],
        4,
        8,
        in_specs=[HBM] * 4,
        out_specs=[VMEM] + [HBM] * 4,
        scratch_shapes=[
            pltpu.VMEM((2, 2, 128, 8, 128), F32),
            pltpu.VMEM((4, 16, 32, 256), F32),
            pltpu.VMEM((27, 32, 128), F32),
            pltpu.VMEM((3, 3, 3, 32), F32),
            pltpu.VMEM((32, 32), F32),
            pltpu.VMEM((1, 32), F32),
            dma((2, 2)),
            dma((8,)),
        ],
    )(far(after_all(cells, zchunks)), far(taps), far(point_weight), far(bias.reshape(1, 32)))
    zall, base = lax.optimization_barrier((zall, base))
    (ychunks,) = call(forward_y, [((32, 8, 128), plain)], 2)(
        near(zall), near(jnp.asarray(tab["fy"]))
    )

    yall = exchange(ychunks, "gx")
    (packed,) = call(
        weights,
        [((2, 32, 32, 128), kept_near)],
        1,
        0,
        in_specs=[HBM],
        scratch_shapes=[pltpu.VMEM((2, 32, 128, 32), F32), dma((8,))],
    )(far(after_all(spec_weight, ychunks).reshape(2, 32, 128, 32)))
    first, last, _ = lax.optimization_barrier((first, last, ychunks))
    before = shifted("gx", far(last), 1)
    after = shifted("gx", far(first), -1)
    yall, packed = lax.optimization_barrier((yall, packed))
    (xchunks,) = call(
        middle,
        [((32, 8, 128), plain)],
        4,
        1,
        in_specs=[VMEM] * 3 + [ANY],
        scratch_shapes=[pltpu.VMEM((2, 256, 64), BF16), dma],
    )(near(yall), near(packed), near(jnp.asarray(tab["fx"])), far(jnp.asarray(tab["ix"])))

    xall = exchange(xchunks, "gx")
    before, after, _ = lax.optimization_barrier((before, after, xchunks))
    before, after = far(before), far(after)
    top, bottom = call(
        rims,
        [((6, 32, 256), kept_near)] * 2,
        3,
        2,
        in_specs=[HBM] * 3,
        scratch_shapes=[dma((2, 3))],
    )(far(own_rims), before, after)
    left = shifted("gy", top, 1)
    right = shifted("gy", bottom, -1)
    xall, top, bottom = lax.optimization_barrier((xall, top, bottom))
    (back,) = call(inverse_y, [((8, 16, 8, 128), plain)], 2)(
        near(xall), near(jnp.asarray(tab["iy"]))
    )

    ball = exchange(back, "gy")
    left, right, _ = lax.optimization_barrier((left, right, back))
    (base,) = call(
        edge_cells,
        [((4, 16, 32, 256), kept_near)],
        8,
        40,
        in_specs=[VMEM] + [ANY] * 4 + [VMEM] * 2 + [ANY],
        scratch_shapes=[pltpu.VMEM((16, 32, 256), F32)] * 4
        + [pltpu.VMEM((27, 32, 128), F32), pltpu.VMEM((3, 3, 3, 32), F32), dma((5,))],
        input_output_aliases={0: 0},
    )(
        near(base), before, far(third), far(last), after, near(left), near(right), far(taps)
    )
    ball, base = lax.optimization_barrier((ball, base))
    (out,) = call(
        final,
        [((128, 16, 256), plain)],
        3,
        out_specs=[ANY],
        scratch_shapes=[pltpu.VMEM((2, 2, 128, 8, 128), F32), dma((2, 2))],
    )(near(ball), near(base), near(jnp.asarray(tab["iz"])))
    return out.reshape(field.shape)


def solution(mesh):
    placed = (P(None, "gx", "gy", None), P(None, None, "gx", "gy", None, None), P(), P(), P())
    return jax.shard_map(
        on_device, mesh=mesh, in_specs=placed, out_specs=P(None, "gx", "gy", None), check_vma=False
    )
```

```python
import functools

import jax
import jax.numpy as jnp
import numpy as np
from jax import lax
from jax.experimental import pallas as pl
from jax.experimental.pallas import tpu as pltpu
from jax.sharding import PartitionSpec as P

F32 = jnp.float32
BF16 = jnp.bfloat16


def halves(table):
    high = np.asarray(table, np.float32).astype(BF16)
    low = (np.asarray(table, np.float64) - high.astype(np.float64)).astype(BF16)
    return high, low


def kept(modes, length):
    index = np.arange(modes)
    return np.where(index < modes // 2, index, index + length - modes)


def angles(freqs, length):
    product = np.outer(freqs, np.arange(length)) % length
    turn = 2.0 * np.pi * product / length
    return np.cos(turn), np.sin(turn)


def tables(modes, full_x, full_y, depth):
    zc, zs = angles(np.arange(modes), depth)
    fz = np.stack([zc, -zs], axis=1).reshape(2 * modes, depth)
    weight = np.where(np.arange(modes) == 0, 1.0, 2.0)[:, None] / depth
    iz = np.stack([weight * zc, -weight * zs], axis=1).reshape(2 * modes, depth)
    yc, ys = angles(kept(modes, full_y), full_y)
    fy = np.block([[yc, ys], [-ys, yc]])
    iy = np.block([[yc.T, -ys.T], [ys.T, yc.T]]) / full_y
    xc, xs = angles(kept(modes, full_x), full_x)
    fx = np.concatenate(
        [np.stack([xc, xs], axis=2), np.stack([-xs, xc], axis=2)], axis=0
    ).reshape(2 * modes, 2 * full_x)
    ix = np.stack(
        [np.concatenate([xc.T, -xs.T], axis=1), np.concatenate([xs.T, xc.T], axis=1)]
    ) / full_x
    ix = ix.reshape(2, full_x // 4, 4, 2 * modes).transpose(2, 0, 1, 3)
    ix = ix.reshape(2 * full_x, 2 * modes)
    return {"fz": fz, "iz": iz, "fy": fy, "iy": iy, "fx": fx, "ix": ix}


def split(value):
    high = value.astype(BF16)
    return high, (value - high.astype(F32)).astype(BF16)


def mm(a, b):
    return jnp.dot(a, b, preferred_element_type=F32)


def mm_nt(a, b):
    return lax.dot_general(a, b, (((1,), (1,)), ((), ())), preferred_element_type=F32)


def mm_tn(a, b):
    return lax.dot_general(a, b, (((0,), (0,)), ((), ())), preferred_element_type=F32)


def table_dot(table_ref, data):
    high, low = split(data)
    return mm(table_ref[0], high) + mm(table_ref[0], low) + mm(table_ref[1], high)


def field_copies(cells_ref, held, sems):
    return [
        [
            pltpu.make_async_copy(
                cells_ref.at[:, pl.ds(8 * half, 8), pl.ds(128 * side, 128)],
                held.at[half, side],
                sems.at[half, side],
            )
            for side in range(2)
        ]
        for half in range(2)
    ]


def field_rows(held, y):
    sides = [held.at[y // 8, side].reshape(1024, 128) for side in range(2)]
    return [
        jnp.concatenate(
            [side[pl.ds(x * 8 + y % 8, 32, stride=32), :] for side in sides], axis=1
        )
        for x in range(4)
    ]


def odd():
    return lax.rem(lax.axis_index("gx"), 2)


def start_all(copies):
    for copy in copies:
        copy.start()


def wait_all(copies):
    for copy in copies:
        copy.wait()


def forward_z(cells_ref, table_ref, out_ref, held, both, ready, sems, done):
    load = pltpu.make_async_copy(table_ref, both, done.at[2])
    load.start()
    copies = field_copies(cells_ref, held, sems)
    start_all(copies[0] + copies[1])
    load.wait()
    results = []
    for half in range(2):
        wait_all(copies[half])
        span = pl.ds(8 * half, 8)
        for y in range(8 * half, 8 * half + 8):
            high, low = split(jnp.concatenate(field_rows(held, y), axis=0))
            wide = mm_nt(both[...], high)
            total = wide[:64] + wide[64:] + mm_nt(both[:64], low)
            ready[:, y] = total.reshape(8, 8, 128)
        results.append(
            pltpu.make_async_copy(ready.at[:, span], out_ref.at[:, span], done.at[half])
        )
        results[-1].start()
    wait_all(results)


def forward_y(data_ref, table_ref, out_ref):
    rows = data_ref.reshape(1024, 128)
    results = []
    for k in range(4):
        parts = [rows[pl.ds(2 * k + part, 128, stride=8), :] for part in range(2)]
        results.append(table_dot(table_ref, jnp.concatenate(parts, axis=0)))
    out = out_ref.reshape(256, 128)
    for x in range(4):
        tile = jnp.concatenate([r[:, 32 * x : 32 * x + 32] for r in results], axis=1)
        for part in range(2):
            out[pl.ds(2 * x + part, 32, stride=8), :] = tile[32 * part : 32 * part + 32]


def middle(
    data_ref, weight_ref, forward_ref, inverse_hbm, out_ref, inverse_ref, sem
):
    load = pltpu.make_async_copy(inverse_hbm, inverse_ref, sem)
    load.start()
    spec = table_dot(forward_ref, data_ref[...].reshape(256, 128))
    spec_re, spec_im = spec[:32], spec[32:]
    lane = lax.broadcasted_iota(jnp.int32, (32, 128), 1)
    group = lane - lax.rem(lane, 32)
    mixed_re = jnp.zeros((32, 128), F32)
    mixed_im = jnp.zeros((32, 128), F32)
    for c in range(32):
        index = group + c
        in_re = jnp.take_along_axis(spec_re, index, axis=1)
        in_im = jnp.take_along_axis(spec_im, index, axis=1)
        w_re, w_im = weight_ref[0, c], weight_ref[1, c]
        mixed_re = mixed_re + (in_re * w_re - in_im * w_im)
        mixed_im = mixed_im + (in_re * w_im + in_im * w_re)
    load.wait()
    back = table_dot(inverse_ref, jnp.concatenate([mixed_re, mixed_im], axis=0))
    out = out_ref.reshape(256, 128)
    for k in range(4):
        tile = jnp.concatenate(
            [back[64 * x : 64 * x + 64, 32 * k : 32 * k + 32] for x in range(4)], axis=1
        )
        for part in range(2):
            out[pl.ds(2 * k + part, 32, stride=8), :] = tile[32 * part : 32 * part + 32]


def inverse_y(data_ref, table_ref, out_ref):
    rows = data_ref.reshape(256, 128)
    out = out_ref.reshape(1024, 128)
    for k in range(4):
        parts = [rows[pl.ds(2 * k + part, 32, stride=8), :] for part in range(2)]
        result = table_dot(table_ref, jnp.concatenate(parts, axis=0))
        for part in range(2):
            out[pl.ds(2 * k + part, 128, stride=8), :] = result[128 * part : 128 * part + 128]


def final(data_ref, base_ref, table_ref, out_ref, held, sems):
    table = jnp.concatenate([table_ref[0], table_ref[0], table_ref[1]], axis=0)
    copies = []
    for half in range(2):
        slots = [held.at[half, side] for side in range(2)]
        rows = [slot.reshape(1024, 128) for slot in slots]
        for y in range(8):
            high, low = split(data_ref[:, 8 * half + y].reshape(64, 128))
            stacked = jnp.concatenate([high, low, high], axis=0)
            spectral = mm_tn(stacked, table)
            for x in range(4):
                value = spectral[32 * x : 32 * x + 32] + base_ref[x, 8 * half + y]
                value = jax.nn.gelu(value)
                for side in range(2):
                    rows[side][pl.ds(x * 8 + y, 32, stride=32), :] = value[
                        :, 128 * side : 128 * side + 128
                    ]
        for side in range(2):
            copy = pltpu.make_async_copy(
                slots[side],
                out_ref.at[:, pl.ds(8 * half, 8), pl.ds(128 * side, 128)],
                sems.at[half, side],
            )
            copy.start()
            copies.append(copy)
    for copy in copies:
        copy.wait()


def weights(data_ref, out_ref, held, sems):
    copies = [
        pltpu.make_async_copy(
            data_ref.at[:, pl.ds(4 * i, 4)], held.at[:, pl.ds(4 * i, 4)], sems.at[i]
        )
        for i in range(8)
    ]
    for copy in copies:
        copy.start()
    rows = out_ref.reshape(2048, 128)
    for i in range(8):
        copies[i].wait()
        for m in range(4 * i, 4 * i + 4):
            for part in range(2):
                tile = jnp.concatenate(
                    [held[part, m, 32 * k : 32 * k + 32, :] for k in range(4)], axis=1
                )
                rows[pl.ds(1024 * part + m, 32, stride=32), :] = tile


def rims(rows_ref, inner_ref, outer_ref, top_ref, bottom_ref, sems):
    copies = []
    for side, out_ref in enumerate((bottom_ref, top_ref)):
        moves = [
            (rows_ref.at[side], out_ref.at[pl.ds(1, 4)]),
            (inner_ref.at[15 * side], out_ref.at[5 - 5 * odd()]),
            (outer_ref.at[15 * side], out_ref.at[5 * odd()]),
        ]
        copies += [
            pltpu.make_async_copy(src, dst, sems.at[side, i]) for i, (src, dst) in enumerate(moves)
        ]
    start_all(copies)
    wait_all(copies)


def shift_sum(sums):
    whole = [jnp.concatenate(pair, axis=1) for pair in sums]
    return whole[1] + pltpu.roll(whole[0], 1, 1) + pltpu.roll(whole[2], 255, 1)


def add_taps(sums, tap_ref, chans, first, load):
    cells = [load(slice(128 * side, 128 * side + 128)) for side in range(2)]
    for e in range(3):
        tap = tap_ref[first + e, chans, :]
        for side in range(2):
            term = tap * cells[side]
            old = sums[e][side]
            sums[e][side] = term if old is None else old + term


def spread_taps(dw_ref, tap_ref):
    rows = jnp.concatenate([dw_ref[a, b] for a in range(3) for b in range(3)], axis=0)
    columns = rows.T
    for i in range(27):
        tap_ref[i] = jnp.broadcast_to(columns[:, i : i + 1], (32, 128))


def own_cells(
    cells_ref, dw_hbm, point_hbm, bias_hbm, out_ref, inner_ref, outer_ref, third_ref, last_ref, rim_ref,
    held, planes, tap_ref, dw_ref, point_ref, bias_ref, sems, small
):
    loads = [
        pltpu.make_async_copy(src, dst, small.at[i])
        for i, (src, dst) in enumerate(
            ((dw_hbm, dw_ref), (point_hbm, point_ref), (bias_hbm, bias_ref))
        )
    ]
    copies = field_copies(cells_ref, held, sems)
    start_all(loads + copies[0] + copies[1])
    wait_all(loads)
    spread_taps(dw_ref, tap_ref)
    channel_map = jnp.concatenate([jnp.concatenate([point_ref[...].T] * 4, axis=1)] * 4, axis=0)
    row = lax.broadcasted_iota(jnp.int32, (128, 128), 0)
    column = lax.broadcasted_iota(jnp.int32, (128, 128), 1)
    same = lax.div(row, 32) == lax.div(column, 32)
    high, low = split(jnp.where(same, channel_map, 0.0))
    point = jnp.concatenate([high, low, high], axis=1)
    bias = jnp.broadcast_to(bias_ref[...], (32, 32)).T[:, :1]
    bias = jnp.concatenate([bias] * 4, axis=0)

    def line(y, shifts):
        high, low = split(planes[:, y].reshape(128, 256))
        value = mm(point, jnp.concatenate([high, high, low], axis=0)) + bias
        for tile in range(4):
            chans = slice(8 * tile, 8 * tile + 8)
            for x in range(3):
                sums = [[None, None] for _ in range(3)]
                for a in range(max(0, 1 - x), 3):
                    for b in shifts:
                        load = lambda lanes: planes[x + a - 1, y + b - 1, chans, lanes]
                        add_taps(sums, tap_ref, chans, 9 * a + 3 * b, load)
                own = 32 * x + 8 * tile
                out_ref[x, y, chans, :] = value[own : own + 8] + shift_sum(sums)
        out_ref[3, y] = value[96:]

    def body(y, carry):
        line(y, (0, 1, 2))
        return carry

    def fill(half):
        wait_all(copies[half])
        for y in range(8 * half, 8 * half + 8):
            for x, part in enumerate(field_rows(held, y)):
                planes[x, y] = part

    fill(0)
    line(0, (1, 2))
    lax.fori_loop(1, 7, body, 0)
    fill(1)
    moves = [
        (planes.at[3 - 3 * odd()], inner_ref),
        (planes.at[3 * odd()], outer_ref),
        (planes.at[2], third_ref),
        (planes.at[3], last_ref),
        (planes.at[:, 0], rim_ref.at[0]),
        (planes.at[:, 15], rim_ref.at[1]),
    ]
    results = [
        pltpu.make_async_copy(src, dst, small.at[3 + i]) for i, (src, dst) in enumerate(moves)
    ]
    start_all(results)
    lax.fori_loop(7, 15, body, 0)
    line(15, (0, 1))
    wait_all(results)


def edge_cells(
    base_ref, inner_hbm, outer_hbm, third_hbm, last_hbm, left_ref, right_ref, dw_hbm,
    out_ref, halo_ref, third_ref, last_ref, tap_ref, dw_ref, sems
):
    before_ref, after_ref = halo_ref.at[0], halo_ref.at[1]
    moves = [
        (dw_hbm, dw_ref),
        (inner_hbm, halo_ref.at[1 - odd()]),
        (outer_hbm, halo_ref.at[odd()]),
        (third_hbm, third_ref),
        (last_hbm, last_ref),
    ]
    copies = [
        pltpu.make_async_copy(src, dst, sems.at[i]) for i, (src, dst) in enumerate(moves)
    ]
    start_all(copies)
    copies[0].wait()
    spread_taps(dw_ref, tap_ref)
    for b, y, source in ((0, 0, left_ref), (2, 15, right_ref)):
        for tile in range(4):
            chans = slice(8 * tile, 8 * tile + 8)
            for x in range(4):
                sums = [[None, None] for _ in range(3)]
                for a in range(max(0, 1 - x), min(3, 5 - x)):
                    load = lambda lanes: source[x + a, chans, lanes]
                    add_taps(sums, tap_ref, chans, 9 * a + 3 * b, load)
                out_ref[x, y, chans, :] = base_ref[x, y, chans, :] + shift_sum(sums)
    wait_all(copies[1:])

    def line(y, before_rows, after_rows, shifts):
        for a, x, rows in ((0, 0, before_rows), (2, 3, after_rows)):
            for tile in range(4):
                chans = slice(8 * tile, 8 * tile + 8)
                sums = [[None, None] for _ in range(3)]
                for b in range(3):
                    plane, at = rows[b]
                    load = lambda lanes: plane[at, chans, lanes]
                    add_taps(sums, tap_ref, chans, 9 * a + 3 * b, load)
                for own, plane in enumerate((third_ref, last_ref) if x == 3 else ()):
                    for b in shifts:
                        load = lambda lanes: plane[y + b - 1, chans, lanes]
                        add_taps(sums, tap_ref, chans, 9 * own + 3 * b, load)
                out_ref[x, y, chans, :] = out_ref[x, y, chans, :] + shift_sum(sums)

    def near_rows(plane, edge, y):
        low = (left_ref, edge) if y == 0 else (plane, y - 1)
        high = (right_ref, edge) if y == 15 else (plane, y + 1)
        return [low, (plane, y), high]

    def body(y, carry):
        rows = [[(plane, y + b - 1) for b in range(3)] for plane in (before_ref, after_ref)]
        line(y, *rows, (0, 1, 2))
        return carry

    lax.fori_loop(1, 15, body, 0, unroll=2)
    for y, shifts in ((0, (1, 2)), (15, (0, 1))):
        line(y, near_rows(before_ref, 0, y), near_rows(after_ref, 5, y), shifts)


VMEM = pl.BlockSpec(memory_space=pltpu.VMEM)
ANY = pl.BlockSpec(memory_space=pl.ANY)
HBM = pl.BlockSpec(memory_space=pltpu.HBM)


def call(body, shapes, inputs, microseconds=0, **kw):
    out_shape = [shape if kind is None else kind(shape, F32) for shape, kind in shapes]
    kw.setdefault("in_specs", [VMEM] * inputs)
    kw.setdefault("out_specs", [VMEM] * len(out_shape))
    kw["compiler_params"] = pltpu.CompilerParams(vmem_limit_bytes=16 * 2**20)
    kw["cost_estimate"] = pl.CostEstimate(
        flops=1_000_000_000 * microseconds, transcendentals=0, bytes_accessed=0
    )
    return pl.pallas_call(body, out_shape=out_shape, name=body.__name__, **kw)


def near(value):
    return pltpu.with_memory_space_constraint(value, pltpu.VMEM)


def after_all(value, *others):
    return lax.optimization_barrier((value, *others))[0]


def shifted(axis, value, step):
    count = lax.axis_size(axis)
    return lax.ppermute(value, axis, [(i, (i + step) % count) for i in range(count)])


def swapped(axis, value, start):
    count = lax.axis_size(axis)
    pairs = [((i + start) % count, (i + start + 1) % count) for i in range(0, count, 2)]
    return lax.ppermute(value, axis, pairs + [(j, i) for i, j in pairs])


def exchange(value, axis):
    return lax.all_to_all(value, axis, split_axis=0, concat_axis=0, tiled=True)


def on_device(field, spec_weight, dw_kernel, point_weight, bias):
    tab = {
        name: np.stack(halves(value)) for name, value in tables(32, 128, 128, 256).items()
    }
    plain, kept_near = jax.ShapeDtypeStruct, pltpu.VMEM
    dma = pltpu.SemaphoreType.DMA
    far = functools.partial(pltpu.with_memory_space_constraint, memory_space=pltpu.HBM)
    cells = far(field.reshape(128, 16, 256))
    (zchunks,) = call(
        forward_z,
        [((8, 16, 8, 128), plain)],
        2,
        in_specs=[HBM] * 2,
        out_specs=[ANY],
        scratch_shapes=[
            pltpu.VMEM((2, 2, 128, 8, 128), F32),
            pltpu.VMEM((128, 256), BF16),
            pltpu.VMEM((8, 16, 8, 128), F32),
            dma((2, 2)),
            dma((3,)),
        ],
    )(cells, far(jnp.asarray(tab["fz"].reshape(128, 256))))
    taps = dw_kernel.transpose(1, 2, 3, 0)

    zall = exchange(zchunks, "gy")
    base, inner, outer, third, last, own_rims = call(
        own_cells,
        [
            ((4, 16, 32, 256), kept_near),
            ((16, 32, 256), pltpu.HBM),
            ((16, 32, 256), pltpu.HBM),
            ((16, 32, 256), pltpu.HBM),
            ((16, 32, 256), pltpu.HBM),
            ((2, 4, 32, 256), pltpu.HBM),
        ],
        4,
        8,
        in_specs=[HBM] * 4,
        out_specs=[VMEM] + [HBM] * 5,
        scratch_shapes=[
            pltpu.VMEM((2, 2, 128, 8, 128), F32),
            pltpu.VMEM((4, 16, 32, 256), F32),
            pltpu.VMEM((27, 32, 128), F32),
            pltpu.VMEM((3, 3, 3, 32), F32),
            pltpu.VMEM((32, 32), F32),
            pltpu.VMEM((1, 32), F32),
            dma((2, 2)),
            dma((9,)),
        ],
    )(far(after_all(cells, zchunks)), far(taps), far(point_weight), far(bias.reshape(1, 32)))
    zall, base = lax.optimization_barrier((zall, base))
    (ychunks,) = call(forward_y, [((32, 8, 128), plain)], 2)(
        near(zall), near(jnp.asarray(tab["fy"]))
    )

    yall = exchange(ychunks, "gx")
    (packed,) = call(
        weights,
        [((2, 32, 32, 128), kept_near)],
        1,
        8,
        in_specs=[HBM],
        scratch_shapes=[pltpu.VMEM((2, 32, 128, 32), F32), dma((8,))],
    )(far(after_all(spec_weight, ychunks).reshape(2, 32, 128, 32)))
    inner, outer, packed = lax.optimization_barrier((inner, outer, packed))
    inner = swapped("gx", far(inner), 0)
    outer = swapped("gx", far(outer), 1)
    yall, packed = lax.optimization_barrier((yall, packed))
    (xchunks,) = call(
        middle,
        [((32, 8, 128), plain)],
        4,
        3,
        in_specs=[VMEM] * 3 + [ANY],
        scratch_shapes=[pltpu.VMEM((2, 256, 64), BF16), dma],
    )(near(yall), near(packed), near(jnp.asarray(tab["fx"])), far(jnp.asarray(tab["ix"])))

    xall = exchange(xchunks, "gx")
    inner, outer, _ = lax.optimization_barrier((inner, outer, xchunks))
    inner, outer = far(inner), far(outer)
    top, bottom = call(
        rims,
        [((6, 32, 256), kept_near)] * 2,
        3,
        2,
        in_specs=[HBM] * 3,
        scratch_shapes=[dma((2, 3))],
    )(far(own_rims), inner, outer)
    left = shifted("gy", top, 1)
    right = shifted("gy", bottom, -1)
    xall, top, bottom = lax.optimization_barrier((xall, top, bottom))
    (back,) = call(inverse_y, [((8, 16, 8, 128), plain)], 2)(
        near(xall), near(jnp.asarray(tab["iy"]))
    )

    ball = exchange(back, "gy")
    left, right, _ = lax.optimization_barrier((left, right, back))
    (base,) = call(
        edge_cells,
        [((4, 16, 32, 256), kept_near)],
        8,
        40,
        in_specs=[VMEM] + [ANY] * 4 + [VMEM] * 2 + [ANY],
        scratch_shapes=[pltpu.VMEM((2, 16, 32, 256), F32)] + [pltpu.VMEM((16, 32, 256), F32)] * 2
        + [pltpu.VMEM((27, 32, 128), F32), pltpu.VMEM((3, 3, 3, 32), F32), dma((5,))],
        input_output_aliases={0: 0},
    )(
        near(base), inner, outer, far(third), far(last), near(left), near(right), far(taps)
    )
    ball, base = lax.optimization_barrier((ball, base))
    (out,) = call(
        final,
        [((128, 16, 256), plain)],
        3,
        out_specs=[ANY],
        scratch_shapes=[pltpu.VMEM((2, 2, 128, 8, 128), F32), dma((2, 2))],
    )(near(ball), near(base), near(jnp.asarray(tab["iz"])))
    return out.reshape(field.shape)


def solution(mesh):
    placed = (P(None, "gx", "gy", None), P(None, None, "gx", "gy", None, None), P(), P(), P())
    return jax.shard_map(
        on_device, mesh=mesh, in_specs=placed, out_specs=P(None, "gx", "gy", None), check_vma=False
    )
```

```python
import functools

import jax
import jax.numpy as jnp
import numpy as np
from jax import lax
from jax.experimental import pallas as pl
from jax.experimental.pallas import tpu as pltpu
from jax.sharding import PartitionSpec as P

F32 = jnp.float32
BF16 = jnp.bfloat16


def halves(table):
    high = np.asarray(table, np.float32).astype(BF16)
    low = (np.asarray(table, np.float64) - high.astype(np.float64)).astype(BF16)
    return high, low


def kept(modes, length):
    index = np.arange(modes)
    return np.where(index < modes // 2, index, index + length - modes)


def angles(freqs, length):
    product = np.outer(freqs, np.arange(length)) % length
    turn = 2.0 * np.pi * product / length
    return np.cos(turn), np.sin(turn)


def tables(modes, full_x, full_y, depth):
    zc, zs = angles(np.arange(modes), depth)
    fz = np.stack([zc, -zs], axis=1).reshape(2 * modes, depth)
    weight = np.where(np.arange(modes) == 0, 1.0, 2.0)[:, None] / depth
    iz = np.stack([weight * zc, -weight * zs], axis=1).reshape(2 * modes, depth)
    yc, ys = angles(kept(modes, full_y), full_y)
    fy = np.block([[yc, ys], [-ys, yc]])
    iy = np.block([[yc.T, -ys.T], [ys.T, yc.T]]) / full_y
    xc, xs = angles(kept(modes, full_x), full_x)
    fx = np.concatenate(
        [np.stack([xc, xs], axis=2), np.stack([-xs, xc], axis=2)], axis=0
    ).reshape(2 * modes, 2 * full_x)
    ix = np.stack(
        [np.concatenate([xc.T, -xs.T], axis=1), np.concatenate([xs.T, xc.T], axis=1)]
    ) / full_x
    ix = ix.reshape(2, full_x // 4, 4, 2 * modes).transpose(2, 0, 1, 3)
    ix = ix.reshape(2 * full_x, 2 * modes)
    return {"fz": fz, "iz": iz, "fy": fy, "iy": iy, "fx": fx, "ix": ix}


def split(value):
    high = value.astype(BF16)
    return high, (value - high.astype(F32)).astype(BF16)


def mm(a, b):
    return jnp.dot(a, b, preferred_element_type=F32)


def mm_nt(a, b):
    return lax.dot_general(a, b, (((1,), (1,)), ((), ())), preferred_element_type=F32)


def mm_tn(a, b):
    return lax.dot_general(a, b, (((0,), (0,)), ((), ())), preferred_element_type=F32)


def table_dot(table_ref, data):
    high, low = split(data)
    return mm(table_ref[0], high) + mm(table_ref[0], low) + mm(table_ref[1], high)


def field_copies(cells_ref, held, sems):
    return [
        [
            pltpu.make_async_copy(
                cells_ref.at[:, pl.ds(8 * half, 8), pl.ds(128 * side, 128)],
                held.at[half, side],
                sems.at[half, side],
            )
            for side in range(2)
        ]
        for half in range(2)
    ]


def field_rows(held, y):
    sides = [held.at[y // 8, side].reshape(1024, 128) for side in range(2)]
    return [
        jnp.concatenate(
            [side[pl.ds(x * 8 + y % 8, 32, stride=32), :] for side in sides], axis=1
        )
        for x in range(4)
    ]


def odd():
    return lax.rem(lax.axis_index("gx"), 2)


def start_all(copies):
    for copy in copies:
        copy.start()


def wait_all(copies):
    for copy in copies:
        copy.wait()


def forward_z(cells_ref, table_ref, out_ref, held, both, ready, sems, done):
    load = pltpu.make_async_copy(table_ref, both, done.at[2])
    load.start()
    copies = field_copies(cells_ref, held, sems)
    start_all(copies[0] + copies[1])
    load.wait()
    results = []
    for half in range(2):
        wait_all(copies[half])
        span = pl.ds(8 * half, 8)
        for y in range(8 * half, 8 * half + 8):
            high, low = split(jnp.concatenate(field_rows(held, y), axis=0))
            wide = mm_nt(both[...], high)
            total = wide[:64] + wide[64:] + mm_nt(both[:64], low)
            ready[:, y] = total.reshape(8, 8, 128)
        results.append(
            pltpu.make_async_copy(ready.at[:, span], out_ref.at[:, span], done.at[half])
        )
        results[-1].start()
    wait_all(results)


def forward_y(data_ref, table_ref, out_ref):
    rows = data_ref.reshape(1024, 128)
    results = []
    for k in range(4):
        parts = [rows[pl.ds(2 * k + part, 128, stride=8), :] for part in range(2)]
        results.append(table_dot(table_ref, jnp.concatenate(parts, axis=0)))
    out = out_ref.reshape(256, 128)
    for x in range(4):
        tile = jnp.concatenate([r[:, 32 * x : 32 * x + 32] for r in results], axis=1)
        for part in range(2):
            out[pl.ds(2 * x + part, 32, stride=8), :] = tile[32 * part : 32 * part + 32]


def middle(
    data_ref, weight_ref, forward_ref, inverse_hbm, out_ref, inverse_ref, sem
):
    load = pltpu.make_async_copy(inverse_hbm, inverse_ref, sem)
    load.start()
    spec = table_dot(forward_ref, data_ref[...].reshape(256, 128))
    spec_re, spec_im = spec[:32], spec[32:]
    lane = lax.broadcasted_iota(jnp.int32, (32, 128), 1)
    group = lane - lax.rem(lane, 32)
    mixed_re = jnp.zeros((32, 128), F32)
    mixed_im = jnp.zeros((32, 128), F32)
    for c in range(32):
        index = group + c
        in_re = jnp.take_along_axis(spec_re, index, axis=1)
        in_im = jnp.take_along_axis(spec_im, index, axis=1)
        w_re, w_im = weight_ref[0, c], weight_ref[1, c]
        mixed_re = mixed_re + (in_re * w_re - in_im * w_im)
        mixed_im = mixed_im + (in_re * w_im + in_im * w_re)
    load.wait()
    back = table_dot(inverse_ref, jnp.concatenate([mixed_re, mixed_im], axis=0))
    out = out_ref.reshape(256, 128)
    for k in range(4):
        tile = jnp.concatenate(
            [back[64 * x : 64 * x + 64, 32 * k : 32 * k + 32] for x in range(4)], axis=1
        )
        for part in range(2):
            out[pl.ds(2 * k + part, 32, stride=8), :] = tile[32 * part : 32 * part + 32]


def inverse_y(data_ref, table_ref, out_ref, ready, sems):
    rows = data_ref.reshape(256, 128)
    out = ready.reshape(1024, 128)
    pairs = []
    for k in range(4):
        parts = [rows[pl.ds(2 * k + part, 32, stride=8), :] for part in range(2)]
        pairs.append(split(jnp.concatenate(parts, axis=0)))
    copies = []
    for half in range(2):
        tables = [
            jnp.concatenate(
                [table_ref[i, pl.ds(128 * part + 64 * half, 64)] for part in range(2)], axis=0
            )
            for i in range(2)
        ]
        for k, (high, low) in enumerate(pairs):
            result = mm(tables[0], high) + mm(tables[0], low) + mm(tables[1], high)
            for part in range(2):
                out[pl.ds(512 * half + 2 * k + part, 64, stride=8), :] = result[
                    64 * part : 64 * part + 64
                ]
        span = pl.ds(4 * half, 4)
        copies.append(pltpu.make_async_copy(ready.at[span], out_ref.at[span], sems.at[half]))
        copies[-1].start()
    wait_all(copies)


def final(data_ref, base_ref, table_ref, out_ref, held, sems):
    table = jnp.concatenate([table_ref[0], table_ref[0], table_ref[1]], axis=0)
    copies = []
    for half in range(2):
        slots = [held.at[half, side] for side in range(2)]
        rows = [slot.reshape(1024, 128) for slot in slots]
        for y in range(8):
            high, low = split(data_ref[:, 8 * half + y].reshape(64, 128))
            stacked = jnp.concatenate([high, low, high], axis=0)
            spectral = mm_tn(stacked, table)
            for x in range(4):
                value = spectral[32 * x : 32 * x + 32] + base_ref[x, 8 * half + y]
                value = jax.nn.gelu(value)
                for side in range(2):
                    rows[side][pl.ds(x * 8 + y, 32, stride=32), :] = value[
                        :, 128 * side : 128 * side + 128
                    ]
        for side in range(2):
            copy = pltpu.make_async_copy(
                slots[side],
                out_ref.at[:, pl.ds(8 * half, 8), pl.ds(128 * side, 128)],
                sems.at[half, side],
            )
            copy.start()
            copies.append(copy)
    for copy in copies:
        copy.wait()


def weights(data_ref, out_ref, held, sems):
    copies = [
        pltpu.make_async_copy(
            data_ref.at[:, pl.ds(4 * i, 4)], held.at[:, pl.ds(4 * i, 4)], sems.at[i]
        )
        for i in range(8)
    ]
    for copy in copies:
        copy.start()
    rows = out_ref.reshape(2048, 128)
    for i in range(8):
        copies[i].wait()
        for m in range(4 * i, 4 * i + 4):
            for part in range(2):
                tile = jnp.concatenate(
                    [held[part, m, 32 * k : 32 * k + 32, :] for k in range(4)], axis=1
                )
                rows[pl.ds(1024 * part + m, 32, stride=32), :] = tile


def rims(rows_ref, inner_ref, outer_ref, top_ref, bottom_ref, sems):
    copies = []
    for side, out_ref in enumerate((bottom_ref, top_ref)):
        moves = [
            (rows_ref.at[side], out_ref.at[pl.ds(1, 4)]),
            (inner_ref.at[15 * side], out_ref.at[5 - 5 * odd()]),
            (outer_ref.at[15 * side], out_ref.at[5 * odd()]),
        ]
        copies += [
            pltpu.make_async_copy(src, dst, sems.at[side, i]) for i, (src, dst) in enumerate(moves)
        ]
    start_all(copies)
    wait_all(copies)


def shift_sum(sums):
    whole = [jnp.concatenate(pair, axis=1) for pair in sums]
    return whole[1] + pltpu.roll(whole[0], 1, 1) + pltpu.roll(whole[2], 255, 1)


def add_taps(sums, tap_ref, chans, first, load):
    cells = [load(slice(128 * side, 128 * side + 128)) for side in range(2)]
    for e in range(3):
        tap = tap_ref[first + e, chans, :]
        for side in range(2):
            term = tap * cells[side]
            old = sums[e][side]
            sums[e][side] = term if old is None else old + term


def spread_taps(dw_ref, tap_ref):
    rows = jnp.concatenate([dw_ref[a, b] for a in range(3) for b in range(3)], axis=0)
    columns = rows.T
    for i in range(27):
        tap_ref[i] = jnp.broadcast_to(columns[:, i : i + 1], (32, 128))


def own_cells(
    cells_ref, dw_hbm, point_hbm, bias_hbm, out_ref, inner_ref, outer_ref, third_ref, last_ref, rim_ref,
    held, planes, tap_ref, dw_ref, point_ref, bias_ref, sems, small
):
    loads = [
        pltpu.make_async_copy(src, dst, small.at[i])
        for i, (src, dst) in enumerate(
            ((dw_hbm, dw_ref), (point_hbm, point_ref), (bias_hbm, bias_ref))
        )
    ]
    copies = field_copies(cells_ref, held, sems)
    start_all(loads + copies[0] + copies[1])
    wait_all(loads)
    spread_taps(dw_ref, tap_ref)
    channel_map = jnp.concatenate([jnp.concatenate([point_ref[...].T] * 4, axis=1)] * 4, axis=0)
    row = lax.broadcasted_iota(jnp.int32, (128, 128), 0)
    column = lax.broadcasted_iota(jnp.int32, (128, 128), 1)
    same = lax.div(row, 32) == lax.div(column, 32)
    high, low = split(jnp.where(same, channel_map, 0.0))
    point = jnp.concatenate([high, low, high], axis=1)
    bias = jnp.broadcast_to(bias_ref[...], (32, 32)).T[:, :1]
    bias = jnp.concatenate([bias] * 4, axis=0)

    def line(y, shifts):
        high, low = split(planes[:, y].reshape(128, 256))
        value = mm(point, jnp.concatenate([high, high, low], axis=0)) + bias
        for tile in range(4):
            chans = slice(8 * tile, 8 * tile + 8)
            for x in range(3):
                sums = [[None, None] for _ in range(3)]
                for a in range(max(0, 1 - x), 3):
                    for b in shifts:
                        load = lambda lanes: planes[x + a - 1, y + b - 1, chans, lanes]
                        add_taps(sums, tap_ref, chans, 9 * a + 3 * b, load)
                own = 32 * x + 8 * tile
                out_ref[x, y, chans, :] = value[own : own + 8] + shift_sum(sums)
        out_ref[3, y] = value[96:]

    def body(y, carry):
        line(y, (0, 1, 2))
        return carry

    def fill(half):
        wait_all(copies[half])
        for y in range(8 * half, 8 * half + 8):
            for x, part in enumerate(field_rows(held, y)):
                planes[x, y] = part

    fill(0)
    line(0, (1, 2))
    lax.fori_loop(1, 7, body, 0)
    fill(1)
    moves = [
        (planes.at[3 - 3 * odd()], inner_ref),
        (planes.at[3 * odd()], outer_ref),
        (planes.at[2], third_ref),
        (planes.at[3], last_ref),
        (planes.at[:, 0], rim_ref.at[0]),
        (planes.at[:, 15], rim_ref.at[1]),
    ]
    results = [
        pltpu.make_async_copy(src, dst, small.at[3 + i]) for i, (src, dst) in enumerate(moves)
    ]
    start_all(results)
    lax.fori_loop(7, 15, body, 0)
    line(15, (0, 1))
    wait_all(results)


def edge_cells(
    base_ref, inner_hbm, outer_hbm, third_hbm, last_hbm, left_ref, right_ref, dw_hbm,
    out_ref, halo_ref, third_ref, last_ref, tap_ref, dw_ref, sems
):
    before_ref, after_ref = halo_ref.at[0], halo_ref.at[1]
    moves = [
        (dw_hbm, dw_ref),
        (inner_hbm, halo_ref.at[1 - odd()]),
        (outer_hbm, halo_ref.at[odd()]),
        (third_hbm, third_ref),
        (last_hbm, last_ref),
    ]
    copies = [
        pltpu.make_async_copy(src, dst, sems.at[i]) for i, (src, dst) in enumerate(moves)
    ]
    start_all(copies)
    copies[0].wait()
    spread_taps(dw_ref, tap_ref)
    for b, y, source in ((0, 0, left_ref), (2, 15, right_ref)):
        for tile in range(4):
            chans = slice(8 * tile, 8 * tile + 8)
            for x in range(4):
                sums = [[None, None] for _ in range(3)]
                for a in range(max(0, 1 - x), min(3, 5 - x)):
                    load = lambda lanes: source[x + a, chans, lanes]
                    add_taps(sums, tap_ref, chans, 9 * a + 3 * b, load)
                out_ref[x, y, chans, :] = base_ref[x, y, chans, :] + shift_sum(sums)
    wait_all(copies[1:])

    def line(y, before_rows, after_rows, shifts):
        for a, x, rows in ((0, 0, before_rows), (2, 3, after_rows)):
            for tile in range(4):
                chans = slice(8 * tile, 8 * tile + 8)
                sums = [[None, None] for _ in range(3)]
                for b in range(3):
                    plane, at = rows[b]
                    load = lambda lanes: plane[at, chans, lanes]
                    add_taps(sums, tap_ref, chans, 9 * a + 3 * b, load)
                for own, plane in enumerate((third_ref, last_ref) if x == 3 else ()):
                    for b in shifts:
                        load = lambda lanes: plane[y + b - 1, chans, lanes]
                        add_taps(sums, tap_ref, chans, 9 * own + 3 * b, load)
                out_ref[x, y, chans, :] = out_ref[x, y, chans, :] + shift_sum(sums)

    def near_rows(plane, edge, y):
        low = (left_ref, edge) if y == 0 else (plane, y - 1)
        high = (right_ref, edge) if y == 15 else (plane, y + 1)
        return [low, (plane, y), high]

    def body(y, carry):
        rows = [[(plane, y + b - 1) for b in range(3)] for plane in (before_ref, after_ref)]
        line(y, *rows, (0, 1, 2))
        return carry

    lax.fori_loop(1, 15, body, 0, unroll=2)
    for y, shifts in ((0, (1, 2)), (15, (0, 1))):
        line(y, near_rows(before_ref, 0, y), near_rows(after_ref, 5, y), shifts)


VMEM = pl.BlockSpec(memory_space=pltpu.VMEM)
ANY = pl.BlockSpec(memory_space=pl.ANY)
HBM = pl.BlockSpec(memory_space=pltpu.HBM)


def call(body, shapes, inputs, microseconds=0, **kw):
    out_shape = [shape if kind is None else kind(shape, F32) for shape, kind in shapes]
    kw.setdefault("in_specs", [VMEM] * inputs)
    kw.setdefault("out_specs", [VMEM] * len(out_shape))
    kw["compiler_params"] = pltpu.CompilerParams(vmem_limit_bytes=16 * 2**20)
    kw["cost_estimate"] = pl.CostEstimate(
        flops=1_000_000_000 * microseconds, transcendentals=0, bytes_accessed=0
    )
    return pl.pallas_call(body, out_shape=out_shape, name=body.__name__, **kw)


def near(value):
    return pltpu.with_memory_space_constraint(value, pltpu.VMEM)


def after_all(value, *others):
    return lax.optimization_barrier((value, *others))[0]


def shifted(axis, value, step):
    count = lax.axis_size(axis)
    return lax.ppermute(value, axis, [(i, (i + step) % count) for i in range(count)])


def swapped(axis, value, start):
    count = lax.axis_size(axis)
    pairs = [((i + start) % count, (i + start + 1) % count) for i in range(0, count, 2)]
    return lax.ppermute(value, axis, pairs + [(j, i) for i, j in pairs])


def exchange(value, axis):
    return lax.all_to_all(value, axis, split_axis=0, concat_axis=0, tiled=True)


def on_device(field, spec_weight, dw_kernel, point_weight, bias):
    tab = {
        name: np.stack(halves(value)) for name, value in tables(32, 128, 128, 256).items()
    }
    plain, kept_near = jax.ShapeDtypeStruct, pltpu.VMEM
    dma = pltpu.SemaphoreType.DMA
    far = functools.partial(pltpu.with_memory_space_constraint, memory_space=pltpu.HBM)
    cells = far(field.reshape(128, 16, 256))
    (zchunks,) = call(
        forward_z,
        [((8, 16, 8, 128), plain)],
        2,
        in_specs=[HBM] * 2,
        out_specs=[ANY],
        scratch_shapes=[
            pltpu.VMEM((2, 2, 128, 8, 128), F32),
            pltpu.VMEM((128, 256), BF16),
            pltpu.VMEM((8, 16, 8, 128), F32),
            dma((2, 2)),
            dma((3,)),
        ],
    )(cells, far(jnp.asarray(tab["fz"].reshape(128, 256))))
    taps = dw_kernel.transpose(1, 2, 3, 0)

    zall = exchange(zchunks, "gy")
    base, inner, outer, third, last, own_rims = call(
        own_cells,
        [
            ((4, 16, 32, 256), kept_near),
            ((16, 32, 256), pltpu.HBM),
            ((16, 32, 256), pltpu.HBM),
            ((16, 32, 256), pltpu.HBM),
            ((16, 32, 256), pltpu.HBM),
            ((2, 4, 32, 256), pltpu.HBM),
        ],
        4,
        8,
        in_specs=[HBM] * 4,
        out_specs=[VMEM] + [HBM] * 5,
        scratch_shapes=[
            pltpu.VMEM((2, 2, 128, 8, 128), F32),
            pltpu.VMEM((4, 16, 32, 256), F32),
            pltpu.VMEM((27, 32, 128), F32),
            pltpu.VMEM((3, 3, 3, 32), F32),
            pltpu.VMEM((32, 32), F32),
            pltpu.VMEM((1, 32), F32),
            dma((2, 2)),
            dma((9,)),
        ],
    )(far(after_all(cells, zchunks)), far(taps), far(point_weight), far(bias.reshape(1, 32)))
    zall, base = lax.optimization_barrier((zall, base))
    (ychunks,) = call(forward_y, [((32, 8, 128), plain)], 2)(
        near(zall), near(jnp.asarray(tab["fy"]))
    )

    yall = exchange(ychunks, "gx")
    (packed,) = call(
        weights,
        [((2, 32, 32, 128), kept_near)],
        1,
        8,
        in_specs=[HBM],
        scratch_shapes=[pltpu.VMEM((2, 32, 128, 32), F32), dma((8,))],
    )(far(after_all(spec_weight, ychunks).reshape(2, 32, 128, 32)))
    inner, outer, packed = lax.optimization_barrier((inner, outer, packed))
    outer = swapped("gx", far(outer), 1)
    inner = swapped("gx", far(inner), 0)
    yall, packed = lax.optimization_barrier((yall, packed))
    (xchunks,) = call(
        middle,
        [((32, 8, 128), plain)],
        4,
        3,
        in_specs=[VMEM] * 3 + [ANY],
        scratch_shapes=[pltpu.VMEM((2, 256, 64), BF16), dma],
    )(near(yall), near(packed), near(jnp.asarray(tab["fx"])), far(jnp.asarray(tab["ix"])))

    xall = exchange(xchunks, "gx")
    inner, outer, _ = lax.optimization_barrier((inner, outer, xchunks))
    inner, outer = far(inner), far(outer)
    top, bottom = call(
        rims,
        [((6, 32, 256), kept_near)] * 2,
        3,
        2,
        in_specs=[HBM] * 3,
        scratch_shapes=[dma((2, 3))],
    )(far(own_rims), inner, outer)
    left = shifted("gy", top, 1)
    right = shifted("gy", bottom, -1)
    xall, top, bottom = lax.optimization_barrier((xall, top, bottom))
    (back,) = call(
        inverse_y,
        [((8, 16, 8, 128), plain)],
        2,
        out_specs=[ANY],
        scratch_shapes=[pltpu.VMEM((8, 16, 8, 128), F32), dma((2,))],
    )(near(xall), near(jnp.asarray(tab["iy"])))

    ball = exchange(back, "gy")
    left, right, _ = lax.optimization_barrier((left, right, back))
    (base,) = call(
        edge_cells,
        [((4, 16, 32, 256), kept_near)],
        8,
        40,
        in_specs=[VMEM] + [ANY] * 4 + [VMEM] * 2 + [ANY],
        scratch_shapes=[pltpu.VMEM((2, 16, 32, 256), F32)] + [pltpu.VMEM((16, 32, 256), F32)] * 2
        + [pltpu.VMEM((27, 32, 128), F32), pltpu.VMEM((3, 3, 3, 32), F32), dma((5,))],
        input_output_aliases={0: 0},
    )(
        near(base), inner, outer, far(third), far(last), near(left), near(right), far(taps)
    )
    ball, base = lax.optimization_barrier((ball, base))
    (out,) = call(
        final,
        [((128, 16, 256), plain)],
        3,
        out_specs=[ANY],
        scratch_shapes=[pltpu.VMEM((2, 2, 128, 8, 128), F32), dma((2, 2))],
    )(near(ball), near(base), near(jnp.asarray(tab["iz"])))
    return out.reshape(field.shape)


def solution(mesh):
    placed = (P(None, "gx", "gy", None), P(None, None, "gx", "gy", None, None), P(), P(), P())
    return jax.shard_map(
        on_device, mesh=mesh, in_specs=placed, out_specs=P(None, "gx", "gy", None), check_vma=False
    )
```

```python
import functools

import jax
import jax.numpy as jnp
import numpy as np
from jax import lax
from jax.experimental import pallas as pl
from jax.experimental.pallas import tpu as pltpu
from jax.sharding import PartitionSpec as P

F32 = jnp.float32
BF16 = jnp.bfloat16


def halves(table):
    high = np.asarray(table, np.float32).astype(BF16)
    low = (np.asarray(table, np.float64) - high.astype(np.float64)).astype(BF16)
    return high, low


def kept(modes, length):
    index = np.arange(modes)
    return np.where(index < modes // 2, index, index + length - modes)


def angles(freqs, length):
    product = np.outer(freqs, np.arange(length)) % length
    turn = 2.0 * np.pi * product / length
    return np.cos(turn), np.sin(turn)


def tables(modes, full_x, full_y, depth):
    zc, zs = angles(np.arange(modes), depth)
    fz = np.stack([zc, -zs], axis=1).reshape(2 * modes, depth)
    weight = np.where(np.arange(modes) == 0, 1.0, 2.0)[:, None] / depth
    iz = np.stack([weight * zc, -weight * zs], axis=1).reshape(2 * modes, depth)
    yc, ys = angles(kept(modes, full_y), full_y)
    fy = np.block([[yc, ys], [-ys, yc]])
    iy = np.block([[yc.T, -ys.T], [ys.T, yc.T]]) / full_y
    xc, xs = angles(kept(modes, full_x), full_x)
    fx = np.concatenate(
        [np.stack([xc, xs], axis=2), np.stack([-xs, xc], axis=2)], axis=0
    ).reshape(2 * modes, 2 * full_x)
    ix = np.stack(
        [np.concatenate([xc.T, -xs.T], axis=1), np.concatenate([xs.T, xc.T], axis=1)]
    ) / full_x
    ix = ix.reshape(2, full_x // 4, 4, 2 * modes).transpose(2, 0, 1, 3)
    ix = ix.reshape(2 * full_x, 2 * modes)
    return {"fz": fz, "iz": iz, "fy": fy, "iy": iy, "fx": fx, "ix": ix}


def split(value):
    high = value.astype(BF16)
    return high, (value - high.astype(F32)).astype(BF16)


def mm(a, b):
    return jnp.dot(a, b, preferred_element_type=F32)


def mm_nt(a, b):
    return lax.dot_general(a, b, (((1,), (1,)), ((), ())), preferred_element_type=F32)


def mm_tn(a, b):
    return lax.dot_general(a, b, (((0,), (0,)), ((), ())), preferred_element_type=F32)


def table_dot(table_ref, data):
    high, low = split(data)
    return mm(table_ref[0], high) + mm(table_ref[0], low) + mm(table_ref[1], high)


def field_copies(cells_ref, held, sems):
    return [
        [
            pltpu.make_async_copy(
                cells_ref.at[:, pl.ds(8 * half, 8), pl.ds(128 * side, 128)],
                held.at[half, side],
                sems.at[half, side],
            )
            for side in range(2)
        ]
        for half in range(2)
    ]


def field_rows(held, y):
    sides = [held.at[y // 8, side].reshape(1024, 128) for side in range(2)]
    return [
        jnp.concatenate(
            [side[pl.ds(x * 8 + y % 8, 32, stride=32), :] for side in sides], axis=1
        )
        for x in range(4)
    ]


def odd(axis="gx"):
    return lax.rem(lax.axis_index(axis), 2)


def start_all(copies):
    for copy in copies:
        copy.start()


def wait_all(copies):
    for copy in copies:
        copy.wait()


def forward_z(cells_ref, table_ref, out_ref, held, both, ready, sems, done):
    load = pltpu.make_async_copy(table_ref, both, done.at[2])
    load.start()
    copies = field_copies(cells_ref, held, sems)
    start_all(copies[0] + copies[1])
    load.wait()
    results = []
    for half in range(2):
        wait_all(copies[half])
        span = pl.ds(8 * half, 8)
        for y in range(8 * half, 8 * half + 8):
            high, low = split(jnp.concatenate(field_rows(held, y), axis=0))
            wide = mm_nt(both[...], high)
            total = wide[:64] + wide[64:] + mm_nt(both[:64], low)
            ready[:, y] = total.reshape(8, 8, 128)
        results.append(
            pltpu.make_async_copy(ready.at[:, span], out_ref.at[:, span], done.at[half])
        )
        results[-1].start()
    wait_all(results)


def forward_y(data_ref, table_ref, out_ref):
    rows = data_ref.reshape(1024, 128)
    results = []
    for k in range(4):
        parts = [rows[pl.ds(2 * k + part, 128, stride=8), :] for part in range(2)]
        results.append(table_dot(table_ref, jnp.concatenate(parts, axis=0)))
    out = out_ref.reshape(256, 128)
    for x in range(4):
        tile = jnp.concatenate([r[:, 32 * x : 32 * x + 32] for r in results], axis=1)
        for part in range(2):
            out[pl.ds(2 * x + part, 32, stride=8), :] = tile[32 * part : 32 * part + 32]


def middle(
    data_ref, weight_ref, forward_ref, inverse_hbm, out_ref, inverse_ref, sem
):
    load = pltpu.make_async_copy(inverse_hbm, inverse_ref, sem)
    load.start()
    spec = table_dot(forward_ref, data_ref[...].reshape(256, 128))
    spec_re, spec_im = spec[:32], spec[32:]
    lane = lax.broadcasted_iota(jnp.int32, (32, 128), 1)
    group = lane - lax.rem(lane, 32)
    mixed_re = jnp.zeros((32, 128), F32)
    mixed_im = jnp.zeros((32, 128), F32)
    for c in range(32):
        index = group + c
        in_re = jnp.take_along_axis(spec_re, index, axis=1)
        in_im = jnp.take_along_axis(spec_im, index, axis=1)
        w_re, w_im = weight_ref[0, c], weight_ref[1, c]
        mixed_re = mixed_re + (in_re * w_re - in_im * w_im)
        mixed_im = mixed_im + (in_re * w_im + in_im * w_re)
    load.wait()
    back = table_dot(inverse_ref, jnp.concatenate([mixed_re, mixed_im], axis=0))
    out = out_ref.reshape(256, 128)
    for k in range(4):
        tile = jnp.concatenate(
            [back[64 * x : 64 * x + 64, 32 * k : 32 * k + 32] for x in range(4)], axis=1
        )
        for part in range(2):
            out[pl.ds(2 * k + part, 32, stride=8), :] = tile[32 * part : 32 * part + 32]


def inverse_y(data_ref, table_ref, out_ref, ready, sems):
    rows = data_ref.reshape(256, 128)
    out = ready.reshape(1024, 128)
    pairs = []
    for k in range(4):
        parts = [rows[pl.ds(2 * k + part, 32, stride=8), :] for part in range(2)]
        pairs.append(split(jnp.concatenate(parts, axis=0)))
    copies = []
    for half in range(2):
        tables = [
            jnp.concatenate(
                [table_ref[i, pl.ds(128 * part + 64 * half, 64)] for part in range(2)], axis=0
            )
            for i in range(2)
        ]
        for k, (high, low) in enumerate(pairs):
            result = mm(tables[0], high) + mm(tables[0], low) + mm(tables[1], high)
            for part in range(2):
                out[pl.ds(512 * half + 2 * k + part, 64, stride=8), :] = result[
                    64 * part : 64 * part + 64
                ]
        span = pl.ds(4 * half, 4)
        copies.append(pltpu.make_async_copy(ready.at[span], out_ref.at[span], sems.at[half]))
        copies[-1].start()
    wait_all(copies)


def final(data_ref, base_ref, table_ref, out_ref, held, sems):
    table = jnp.concatenate([table_ref[0], table_ref[0], table_ref[1]], axis=0)
    copies = []
    for half in range(2):
        slots = [held.at[half, side] for side in range(2)]
        rows = [slot.reshape(1024, 128) for slot in slots]
        for y in range(8):
            high, low = split(data_ref[:, 8 * half + y].reshape(64, 128))
            stacked = jnp.concatenate([high, low, high], axis=0)
            spectral = mm_tn(stacked, table)
            for x in range(4):
                value = spectral[32 * x : 32 * x + 32] + base_ref[x, 8 * half + y]
                value = jax.nn.gelu(value)
                for side in range(2):
                    rows[side][pl.ds(x * 8 + y, 32, stride=32), :] = value[
                        :, 128 * side : 128 * side + 128
                    ]
        for side in range(2):
            copy = pltpu.make_async_copy(
                slots[side],
                out_ref.at[:, pl.ds(8 * half, 8), pl.ds(128 * side, 128)],
                sems.at[half, side],
            )
            copy.start()
            copies.append(copy)
    for copy in copies:
        copy.wait()


def weights(data_ref, out_ref, held, sems):
    copies = [
        pltpu.make_async_copy(
            data_ref.at[:, pl.ds(4 * i, 4)], held.at[:, pl.ds(4 * i, 4)], sems.at[i]
        )
        for i in range(8)
    ]
    for copy in copies:
        copy.start()
    rows = out_ref.reshape(2048, 128)
    for i in range(8):
        copies[i].wait()
        for m in range(4 * i, 4 * i + 4):
            for part in range(2):
                tile = jnp.concatenate(
                    [held[part, m, 32 * k : 32 * k + 32, :] for k in range(4)], axis=1
                )
                rows[pl.ds(1024 * part + m, 32, stride=32), :] = tile


def rims(rows_ref, inner_ref, outer_ref, inner_out, outer_out, sems):
    copies = []
    for at, (out_ref, side) in enumerate(((inner_out, 1 - odd("gy")), (outer_out, odd("gy")))):
        moves = [
            (rows_ref.at[side], out_ref.at[pl.ds(1, 4)]),
            (inner_ref.at[15 * side], out_ref.at[5 - 5 * odd()]),
            (outer_ref.at[15 * side], out_ref.at[5 * odd()]),
        ]
        copies += [
            pltpu.make_async_copy(src, dst, sems.at[at, i]) for i, (src, dst) in enumerate(moves)
        ]
    start_all(copies)
    wait_all(copies)


def shift_sum(sums):
    whole = [jnp.concatenate(pair, axis=1) for pair in sums]
    return whole[1] + pltpu.roll(whole[0], 1, 1) + pltpu.roll(whole[2], 255, 1)


def add_taps(sums, tap_ref, chans, first, load):
    cells = [load(slice(128 * side, 128 * side + 128)) for side in range(2)]
    for e in range(3):
        tap = tap_ref[first + e, chans, :]
        for side in range(2):
            term = tap * cells[side]
            old = sums[e][side]
            sums[e][side] = term if old is None else old + term


def spread_taps(dw_ref, tap_ref):
    rows = jnp.concatenate([dw_ref[a, b] for a in range(3) for b in range(3)], axis=0)
    columns = rows.T
    for i in range(27):
        tap_ref[i] = jnp.broadcast_to(columns[:, i : i + 1], (32, 128))


def own_cells(
    cells_ref, dw_hbm, point_hbm, bias_hbm, out_ref, inner_ref, outer_ref, third_ref, last_ref, rim_ref,
    held, planes, tap_ref, dw_ref, point_ref, bias_ref, sems, small
):
    loads = [
        pltpu.make_async_copy(src, dst, small.at[i])
        for i, (src, dst) in enumerate(
            ((dw_hbm, dw_ref), (point_hbm, point_ref), (bias_hbm, bias_ref))
        )
    ]
    copies = field_copies(cells_ref, held, sems)
    start_all(loads + copies[0] + copies[1])
    wait_all(loads)
    spread_taps(dw_ref, tap_ref)
    channel_map = jnp.concatenate([jnp.concatenate([point_ref[...].T] * 4, axis=1)] * 4, axis=0)
    row = lax.broadcasted_iota(jnp.int32, (128, 128), 0)
    column = lax.broadcasted_iota(jnp.int32, (128, 128), 1)
    same = lax.div(row, 32) == lax.div(column, 32)
    high, low = split(jnp.where(same, channel_map, 0.0))
    point = jnp.concatenate([high, low, high], axis=1)
    bias = jnp.broadcast_to(bias_ref[...], (32, 32)).T[:, :1]
    bias = jnp.concatenate([bias] * 4, axis=0)

    def line(y, shifts):
        high, low = split(planes[:, y].reshape(128, 256))
        value = mm(point, jnp.concatenate([high, high, low], axis=0)) + bias
        for tile in range(4):
            chans = slice(8 * tile, 8 * tile + 8)
            for x in range(3):
                sums = [[None, None] for _ in range(3)]
                for a in range(max(0, 1 - x), 3):
                    for b in shifts:
                        load = lambda lanes: planes[x + a - 1, y + b - 1, chans, lanes]
                        add_taps(sums, tap_ref, chans, 9 * a + 3 * b, load)
                own = 32 * x + 8 * tile
                out_ref[x, y, chans, :] = value[own : own + 8] + shift_sum(sums)
        out_ref[3, y] = value[96:]

    def body(y, carry):
        line(y, (0, 1, 2))
        return carry

    def fill(half):
        wait_all(copies[half])
        for y in range(8 * half, 8 * half + 8):
            for x, part in enumerate(field_rows(held, y)):
                planes[x, y] = part

    fill(0)
    line(0, (1, 2))
    lax.fori_loop(1, 7, body, 0)
    fill(1)
    moves = [
        (planes.at[3 - 3 * odd()], inner_ref),
        (planes.at[3 * odd()], outer_ref),
        (planes.at[2], third_ref),
        (planes.at[3], last_ref),
        (planes.at[:, 0], rim_ref.at[0]),
        (planes.at[:, 15], rim_ref.at[1]),
    ]
    results = [
        pltpu.make_async_copy(src, dst, small.at[3 + i]) for i, (src, dst) in enumerate(moves)
    ]
    start_all(results)
    lax.fori_loop(7, 15, body, 0)
    line(15, (0, 1))
    wait_all(results)


def edge_cells(
    base_ref, inner_hbm, outer_hbm, third_hbm, last_hbm, inner_rim, outer_rim, dw_hbm,
    out_ref, halo_ref, rim_ref, third_ref, last_ref, tap_ref, dw_ref, sems
):
    before_ref, after_ref = halo_ref.at[0], halo_ref.at[1]
    left_ref, right_ref = rim_ref.at[0], rim_ref.at[1]
    moves = [
        (dw_hbm, dw_ref),
        (inner_rim, rim_ref.at[1 - odd("gy")]),
        (outer_rim, rim_ref.at[odd("gy")]),
        (inner_hbm, halo_ref.at[1 - odd()]),
        (outer_hbm, halo_ref.at[odd()]),
        (third_hbm, third_ref),
        (last_hbm, last_ref),
    ]
    copies = [
        pltpu.make_async_copy(src, dst, sems.at[i]) for i, (src, dst) in enumerate(moves)
    ]
    start_all(copies)
    wait_all(copies[:3])
    spread_taps(dw_ref, tap_ref)
    for b, y, source in ((0, 0, left_ref), (2, 15, right_ref)):
        for tile in range(4):
            chans = slice(8 * tile, 8 * tile + 8)
            for x in range(4):
                sums = [[None, None] for _ in range(3)]
                for a in range(max(0, 1 - x), min(3, 5 - x)):
                    load = lambda lanes: source[x + a, chans, lanes]
                    add_taps(sums, tap_ref, chans, 9 * a + 3 * b, load)
                out_ref[x, y, chans, :] = base_ref[x, y, chans, :] + shift_sum(sums)
    wait_all(copies[3:])

    def line(y, before_rows, after_rows, shifts):
        for a, x, rows in ((0, 0, before_rows), (2, 3, after_rows)):
            for tile in range(4):
                chans = slice(8 * tile, 8 * tile + 8)
                sums = [[None, None] for _ in range(3)]
                for b in range(3):
                    plane, at = rows[b]
                    load = lambda lanes: plane[at, chans, lanes]
                    add_taps(sums, tap_ref, chans, 9 * a + 3 * b, load)
                for own, plane in enumerate((third_ref, last_ref) if x == 3 else ()):
                    for b in shifts:
                        load = lambda lanes: plane[y + b - 1, chans, lanes]
                        add_taps(sums, tap_ref, chans, 9 * own + 3 * b, load)
                out_ref[x, y, chans, :] = out_ref[x, y, chans, :] + shift_sum(sums)

    def near_rows(plane, edge, y):
        low = (left_ref, edge) if y == 0 else (plane, y - 1)
        high = (right_ref, edge) if y == 15 else (plane, y + 1)
        return [low, (plane, y), high]

    def body(y, carry):
        rows = [[(plane, y + b - 1) for b in range(3)] for plane in (before_ref, after_ref)]
        line(y, *rows, (0, 1, 2))
        return carry

    lax.fori_loop(1, 15, body, 0, unroll=2)
    for y, shifts in ((0, (1, 2)), (15, (0, 1))):
        line(y, near_rows(before_ref, 0, y), near_rows(after_ref, 5, y), shifts)


VMEM = pl.BlockSpec(memory_space=pltpu.VMEM)
ANY = pl.BlockSpec(memory_space=pl.ANY)
HBM = pl.BlockSpec(memory_space=pltpu.HBM)


def call(body, shapes, inputs, microseconds=0, **kw):
    out_shape = [shape if kind is None else kind(shape, F32) for shape, kind in shapes]
    kw.setdefault("in_specs", [VMEM] * inputs)
    kw.setdefault("out_specs", [VMEM] * len(out_shape))
    kw["compiler_params"] = pltpu.CompilerParams(vmem_limit_bytes=16 * 2**20)
    kw["cost_estimate"] = pl.CostEstimate(
        flops=1_000_000_000 * microseconds, transcendentals=0, bytes_accessed=0
    )
    return pl.pallas_call(body, out_shape=out_shape, name=body.__name__, **kw)


def near(value):
    return pltpu.with_memory_space_constraint(value, pltpu.VMEM)


def after_all(value, *others):
    return lax.optimization_barrier((value, *others))[0]


def shifted(axis, value, step):
    count = lax.axis_size(axis)
    return lax.ppermute(value, axis, [(i, (i + step) % count) for i in range(count)])


def swapped(axis, value, start):
    count = lax.axis_size(axis)
    pairs = [((i + start) % count, (i + start + 1) % count) for i in range(0, count, 2)]
    return lax.ppermute(value, axis, pairs + [(j, i) for i, j in pairs])


def exchange(value, axis):
    return lax.all_to_all(value, axis, split_axis=0, concat_axis=0, tiled=True)


def on_device(field, spec_weight, dw_kernel, point_weight, bias):
    tab = {
        name: np.stack(halves(value)) for name, value in tables(32, 128, 128, 256).items()
    }
    plain, kept_near = jax.ShapeDtypeStruct, pltpu.VMEM
    dma = pltpu.SemaphoreType.DMA
    far = functools.partial(pltpu.with_memory_space_constraint, memory_space=pltpu.HBM)
    cells = far(field.reshape(128, 16, 256))
    (zchunks,) = call(
        forward_z,
        [((8, 16, 8, 128), plain)],
        2,
        in_specs=[HBM] * 2,
        out_specs=[ANY],
        scratch_shapes=[
            pltpu.VMEM((2, 2, 128, 8, 128), F32),
            pltpu.VMEM((128, 256), BF16),
            pltpu.VMEM((8, 16, 8, 128), F32),
            dma((2, 2)),
            dma((3,)),
        ],
    )(cells, far(jnp.asarray(tab["fz"].reshape(128, 256))))
    taps = dw_kernel.transpose(1, 2, 3, 0)

    zall = exchange(zchunks, "gy")
    base, inner, outer, third, last, own_rims = call(
        own_cells,
        [
            ((4, 16, 32, 256), kept_near),
            ((16, 32, 256), pltpu.HBM),
            ((16, 32, 256), pltpu.HBM),
            ((16, 32, 256), pltpu.HBM),
            ((16, 32, 256), pltpu.HBM),
            ((2, 4, 32, 256), pltpu.HBM),
        ],
        4,
        8,
        in_specs=[HBM] * 4,
        out_specs=[VMEM] + [HBM] * 5,
        scratch_shapes=[
            pltpu.VMEM((2, 2, 128, 8, 128), F32),
            pltpu.VMEM((4, 16, 32, 256), F32),
            pltpu.VMEM((27, 32, 128), F32),
            pltpu.VMEM((3, 3, 3, 32), F32),
            pltpu.VMEM((32, 32), F32),
            pltpu.VMEM((1, 32), F32),
            dma((2, 2)),
            dma((9,)),
        ],
    )(far(after_all(cells, zchunks)), far(taps), far(point_weight), far(bias.reshape(1, 32)))
    zall, base = lax.optimization_barrier((zall, base))
    (ychunks,) = call(forward_y, [((32, 8, 128), plain)], 2)(
        near(zall), near(jnp.asarray(tab["fy"]))
    )

    yall = exchange(ychunks, "gx")
    (packed,) = call(
        weights,
        [((2, 32, 32, 128), kept_near)],
        1,
        8,
        in_specs=[HBM],
        scratch_shapes=[pltpu.VMEM((2, 32, 128, 32), F32), dma((8,))],
    )(far(after_all(spec_weight, ychunks).reshape(2, 32, 128, 32)))
    inner, outer, packed = lax.optimization_barrier((inner, outer, packed))
    outer = swapped("gx", far(outer), 1)
    inner = swapped("gx", far(inner), 0)
    yall, packed = lax.optimization_barrier((yall, packed))
    (xchunks,) = call(
        middle,
        [((32, 8, 128), plain)],
        4,
        3,
        in_specs=[VMEM] * 3 + [ANY],
        scratch_shapes=[pltpu.VMEM((2, 256, 64), BF16), dma],
    )(near(yall), near(packed), near(jnp.asarray(tab["fx"])), far(jnp.asarray(tab["ix"])))

    xall = exchange(xchunks, "gx")
    inner, outer, _ = lax.optimization_barrier((inner, outer, xchunks))
    inner, outer = far(inner), far(outer)
    top, bottom = call(
        rims,
        [((6, 32, 256), kept_near)] * 2,
        3,
        2,
        in_specs=[HBM] * 3,
        scratch_shapes=[dma((2, 3))],
    )(far(own_rims), inner, outer)
    left = swapped("gy", top, 0)
    right = swapped("gy", bottom, 1)
    xall, top, bottom = lax.optimization_barrier((xall, top, bottom))
    (back,) = call(
        inverse_y,
        [((8, 16, 8, 128), plain)],
        2,
        out_specs=[ANY],
        scratch_shapes=[pltpu.VMEM((8, 16, 8, 128), F32), dma((2,))],
    )(near(xall), near(jnp.asarray(tab["iy"])))

    ball = exchange(back, "gy")
    left, right, _ = lax.optimization_barrier((left, right, back))
    (base,) = call(
        edge_cells,
        [((4, 16, 32, 256), kept_near)],
        8,
        40,
        in_specs=[VMEM] + [ANY] * 4 + [VMEM] * 2 + [ANY],
        scratch_shapes=[pltpu.VMEM((2, 16, 32, 256), F32), pltpu.VMEM((2, 6, 32, 256), F32)]
        + [pltpu.VMEM((16, 32, 256), F32)] * 2
        + [pltpu.VMEM((27, 32, 128), F32), pltpu.VMEM((3, 3, 3, 32), F32), dma((7,))],
        input_output_aliases={0: 0},
    )(
        near(base), inner, outer, far(third), far(last), near(left), near(right), far(taps)
    )
    ball, base = lax.optimization_barrier((ball, base))
    (out,) = call(
        final,
        [((128, 16, 256), plain)],
        3,
        out_specs=[ANY],
        scratch_shapes=[pltpu.VMEM((2, 2, 128, 8, 128), F32), dma((2, 2))],
    )(near(ball), near(base), near(jnp.asarray(tab["iz"])))
    return out.reshape(field.shape)


def solution(mesh):
    placed = (P(None, "gx", "gy", None), P(None, None, "gx", "gy", None, None), P(), P(), P())
    return jax.shard_map(
        on_device, mesh=mesh, in_specs=placed, out_specs=P(None, "gx", "gy", None), check_vma=False
    )
```
